32 devices in a mesh: rows: 8 (over z, y), vecs: 4 (over x, core).
Axes of the slice: x: 2, y: 2, z: 4, core: 2. Of those that a mesh axis runs over, the one named last changes fastest.
Arguments:
- vectors: bfloat16 [32768, 1024], P('rows', 'vecs'), may hold values from -6 to 6, as said below
- blocks: bfloat16 [256, 5, 128, 128], P('rows'), may hold values from -0.25 to 0.25
- columns: int32 [256, 5], P('rows'), may hold values from 0 to 255, as said below
Outputs:
- basis: float32 [32768, 1024], P('rows', 'vecs')
The draws below stay inside these ranges and needn't reach their ends.
Inputs may be any that keep to these rules, and one draw needn't show every extreme that they name: Each block row i names 5 block columns of the form i + d clipped to 0 .. 255, with distinct d in -8 .. 8; near the grid's ends some may repeat. `vectors`: entries of order one.
All inputs are finite; a program needn't handle non-finite values.
Results may differ from the reference program's by a relative error of at most 0.0075.
Values may be sent and summed in bfloat16 or wider, within the bound.
A program may use at most 128 MiB of HBM per device.

```python
import jax
import jax.numpy as jnp
from jax import lax

B = 128
K = 1024
NNZ = 5
DEGREE = 4
BR_DEV = 32
REACH = 8
NB = 256
NROWS = 32768
N_ROWS = 8


def draw_columns(key, part):
    breadth = 2 * REACH + 1
    row_ids = jnp.arange(NB, dtype=jnp.int32)[:, None]
    scores = jax.random.randint(key, (NB, breadth), 0, 1 << 20, dtype=jnp.int32) * breadth + jnp.arange(breadth, dtype=jnp.int32)[None, :]
    values, chosen = lax.top_k(scores, NNZ)
    picked = jnp.clip(row_ids + chosen.astype(jnp.int32) - REACH, 0, NB - 1)
    return picked.astype(jnp.int32)


def draw_vectors(key, part):
    first_key = jax.random.fold_in(key, 11)
    third_key = jax.random.fold_in(key, 13)
    entries = jax.random.normal(first_key, (NROWS, K), jnp.float32)
    common = jax.random.normal(third_key, (NROWS, 1), jnp.float32)
    values = jnp.clip(entries + 0.4 * common, -6.0, 6.0)
    return values.astype(jnp.bfloat16)


def block_scale(rng, shape, shards, smallest, largest):
    loudness = 1.0
    for axis_at, shards_of in shards:
        draws = jax.random.uniform(jax.random.fold_in(jax.random.fold_in(rng, 6), axis_at), (shards_of,), jnp.float32, smallest / len(shards), largest / len(shards))
        loudness = loudness * jnp.repeat(jnp.exp(draws), shape[axis_at] // shards_of).reshape((-1,) + (1,) * (len(shape) - 1 - axis_at))
    return loudness


def bell_draw(key, shape, width, reach, shards=(), held_as=jnp.bfloat16):
    level = block_scale(key, shape, shards, -0.22, 0.18) if shards else 1.0
    values = jax.random.normal(key, shape, jnp.float32) * width * level
    return jnp.minimum(jnp.maximum(values, -reach), reach).astype(held_as)


def setup_inputs(seed: int = 0) -> dict:
    splits = jax.random.split(jax.random.key(seed), 4)
    vectors = draw_vectors(jax.random.fold_in(splits[3], 71), 0)
    blocks = bell_draw(splits[1], (NB, NNZ, B, B), (NNZ * B) ** -0.5, 0.25, ((0, 8),))
    columns = draw_columns(jax.random.fold_in(splits[3], 71), 0)
    return dict(vectors=vectors, blocks=blocks, columns=columns)


filter_center = 0.25
filter_radius = 1.25

def product(vec_bf, blocks, columns):
    stacked = vec_bf.reshape(NB, B, K)
    cols_slab = columns.reshape(N_ROWS, BR_DEV, NNZ)
    blocks_slab = blocks.reshape(N_ROWS, BR_DEV, NNZ, B, B)

    def one_slab(pair):
        slab_cols, slab_blocks = pair
        picked = stacked[slab_cols].astype(jnp.float32)
        return jnp.einsum('rjab,rjbk->rak', slab_blocks.astype(jnp.float32), picked)
    result = lax.map(one_slab, (cols_slab, blocks_slab))
    return result.reshape(NROWS, K)

def reference(vectors, blocks, columns):
    older = vectors.astype(jnp.float32)
    current = (product(vectors, blocks, columns) - filter_center * older) / filter_radius
    for iteration in range(1, DEGREE):
        rounded = current.astype(jnp.bfloat16)
        newer = 2.0 * (product(rounded, blocks, columns) - filter_center * current) / filter_radius - older
        older = current
        current = newer
    final = current.astype(jnp.bfloat16)
    gram_matrix = jnp.dot(final.T.astype(jnp.float32), final.astype(jnp.float32), preferred_element_type=jnp.float32) / NROWS
    lower = jnp.linalg.cholesky(gram_matrix)
    identity = jnp.eye(K, dtype=jnp.float32)
    inverse = lax.linalg.triangular_solve(lower, identity, left_side=True, lower=True)
    inverse_high = inverse.astype(jnp.bfloat16)
    inverse_low = (inverse - inverse_high.astype(jnp.float32)).astype(jnp.bfloat16)
    first = jnp.dot(final.astype(jnp.float32), inverse_high.T.astype(jnp.float32), preferred_element_type=jnp.float32)
    second = jnp.dot(final.astype(jnp.float32), inverse_low.T.astype(jnp.float32), preferred_element_type=jnp.float32)
    return first + second
```

```python
import functools

import jax
import jax.numpy as jnp
from jax import lax
from jax.experimental import pallas as pl
from jax.experimental.pallas import tpu as pltpu
from jax.sharding import PartitionSpec as P

DEGREE = 4

filter_center = 0.25
filter_radius = 1.25

HIGHEST = lax.Precision.HIGHEST
VMEM_LIMIT = 56 * 1024 * 1024
PIVOTS = 8


def filter_kernel(
    place_ref, vectors_ref, blocks_ref, out_ref,
    first_win, even_win, odd_win, top_a, top_b, bottom_a, bottom_b, even, odd, held,
    in_sem, send_sem, recv_sem,
):
    me, count = lax.axis_index("rows"), lax.axis_size("rows")
    block_rows, nnz = blocks_ref.shape[:2]
    reach = block_rows // 4
    span = 2 * reach
    top, bottom = (top_a, top_b), (bottom_a, bottom_b)

    @pl.when(me > 0)
    def _():
        pl.semaphore_signal(pltpu.get_barrier_semaphore(), 1, device_id={"rows": me - 1})

    @pl.when(me < count - 1)
    def _():
        pl.semaphore_signal(pltpu.get_barrier_semaphore(), 1, device_id={"rows": me + 1})

    fetches = [
        pltpu.make_async_copy(vectors_ref, first_win, in_sem.at[0]),
        pltpu.make_async_copy(vectors_ref.at[:span], top_a.at[reach:], in_sem.at[1]),
        pltpu.make_async_copy(vectors_ref.at[block_rows - span :], bottom_a.at[:span], in_sem.at[2]),
        pltpu.make_async_copy(blocks_ref, held, in_sem.at[3]),
    ]
    for fetch in fetches:
        fetch.start()

    inside = jnp.logical_and(me > 0, me < count - 1)

    @pl.when(inside)
    def _():
        pl.semaphore_wait(pltpu.get_barrier_semaphore(), 2)

    @pl.when(jnp.logical_not(inside))
    def _():
        pl.semaphore_wait(pltpu.get_barrier_semaphore(), 1)

    def to_lower(source, slot):
        return pltpu.make_async_remote_copy(
            src_ref=source.at[:reach], dst_ref=bottom[slot].at[span:],
            send_sem=send_sem.at[0, slot], recv_sem=recv_sem.at[0, slot],
            device_id={"rows": me - 1},
        )

    def to_upper(source, slot):
        return pltpu.make_async_remote_copy(
            src_ref=source.at[block_rows - reach :], dst_ref=top[slot].at[:reach],
            send_sem=send_sem.at[1, slot], recv_sem=recv_sem.at[1, slot],
            device_id={"rows": me + 1},
        )

    @pl.when(me > 0)
    def _():
        to_lower(vectors_ref, 0).start()

    @pl.when(me < count - 1)
    def _():
        to_upper(vectors_ref, 0).start()

    for fetch in fetches:
        fetch.wait()

    windows = [first_win, odd_win, even_win, odd_win, even_win]
    states = [None, even, odd, even, None]

    def compute(step, start, stop, window, group=4):
        slot = (step + 1) % 2
        target = windows[step + 1]
        last = step == DEGREE - 1

        @pl.loop(0, (stop - start) // group)
        def _(index):
            for g in range(group):
                row = start + index * group + g
                acc = None
                for j in range(nnz):
                    part = jnp.dot(
                        held[row, j], window[place_ref[row, j]], preferred_element_type=jnp.float32
                    )
                    acc = part if acc is None else acc + part
                cur = first_win[row].astype(jnp.float32) if step == 0 else states[step][row]
                new = (acc - filter_center * cur) * (1.0 / filter_radius)
                if step == 1:
                    new = 2.0 * new - first_win[row].astype(jnp.float32)
                elif step > 1:
                    new = 2.0 * new - states[step - 1][row]
                rounded = new.astype(jnp.bfloat16)
                target[row] = rounded
                if not last:
                    states[step + 1][row] = new
                    if stop <= span:
                        top[slot][row + reach] = rounded
                    if start >= span:
                        bottom[slot][row - span] = rounded

    for step in range(DEGREE):
        now = step % 2
        later = 1 - now
        source = vectors_ref if step == 0 else windows[step]
        compute(step, reach, 2 * reach, windows[step])
        compute(step, 2 * reach, 3 * reach, windows[step])

        @pl.when(me < count - 1)
        def _():
            to_lower(source, now).wait_recv()

        compute(step, 3 * reach, 4 * reach, bottom[now])
        if step < DEGREE - 1:

            @pl.when(me < count - 1)
            def _():
                to_upper(windows[step + 1], later).start()

        @pl.when(me > 0)
        def _():
            to_upper(source, now).wait_recv()

        compute(step, 0, reach, top[now])
        if step < DEGREE - 1:

            @pl.when(me > 0)
            def _():
                to_lower(windows[step + 1], later).start()

        @pl.when(me > 0)
        def _():
            to_lower(source, now).wait_send()

        @pl.when(me < count - 1)
        def _():
            to_upper(source, now).wait_send()

    done = pltpu.make_async_copy(windows[DEGREE], out_ref, in_sem.at[0])
    done.start()
    done.wait()


def filtered_block(vectors, blocks, columns):
    rows, width = vectors.shape
    block_rows, nnz, size_b = blocks.shape[:3]
    reach = block_rows // 4
    row = lax.broadcasted_iota(jnp.int32, columns.shape, 0)
    shift = jnp.where(row < reach, reach, jnp.where(row < block_rows - reach, 0, -2 * reach))
    place = columns - lax.axis_index("rows") * block_rows + shift
    window = pltpu.VMEM((block_rows, size_b, width), jnp.bfloat16)
    side = pltpu.VMEM((3 * reach, size_b, width), jnp.bfloat16)
    state = pltpu.VMEM((block_rows, size_b, width), jnp.float32)
    anywhere = pl.BlockSpec(memory_space=pl.ANY)
    out = pl.pallas_call(
        filter_kernel,
        out_shape=jax.ShapeDtypeStruct((block_rows, size_b, width), jnp.bfloat16),
        in_specs=[pl.BlockSpec(memory_space=pltpu.SMEM), anywhere, anywhere],
        out_specs=anywhere,
        scratch_shapes=[window] * 3 + [side] * 4 + [state] * 2 + [
            pltpu.VMEM(blocks.shape, jnp.bfloat16),
            pltpu.SemaphoreType.DMA((4,)),
            pltpu.SemaphoreType.DMA((2, 2)),
            pltpu.SemaphoreType.DMA((2, 2)),
        ],
        compiler_params=pltpu.CompilerParams(
            vmem_limit_bytes=VMEM_LIMIT, collective_id=0, has_side_effects=True
        ),
    )(place, vectors.reshape(block_rows, size_b, width), blocks)
    return out.reshape(rows, width)


def factor_block(block):
    size = block.shape[0]
    tiles = [block[8 * t : 8 * (t + 1), :] for t in range(size // 8)]
    lane = lax.broadcasted_iota(jnp.int32, (8, size), 1)
    sub = lax.broadcasted_iota(jnp.int32, (8, size), 0)

    def spread(array):
        return jnp.broadcast_to(array, (8, size))

    for j in range(0, size, PIVOTS):
        first, r = divmod(j, 8)
        each = range(PIVOTS)
        at_any = jnp.logical_and(lane >= j, lane < j + PIVOTS)
        head = tiles[first]
        cols = [spread(head[:, j + a : j + a + 1]) for a in each]
        pivots = [[spread(cols[a][r + b : r + b + 1, :]) for a in range(b + 1)] for b in each]
        rows = [jnp.where(at_any, 0.0, spread(head[r + a : r + a + 1, :])) for a in each]
        rows = [jnp.where(lane == j + a, 1.0, rows[a]) for a in each]
        over, ratio = [], {}
        for a in each:
            over.append(1.0 / pivots[a][a])
            for b in range(a + 1, PIVOTS):
                ratio[b, a] = pivots[b][a] * over[a]
                for c in range(a + 1, b + 1):
                    pivots[b][c] = pivots[b][c] - ratio[b, a] * pivots[c][a]
                rows[b] = rows[b] - ratio[b, a] * rows[a]
        use = [None] * PIVOTS
        for a in reversed(each):
            use[a] = rows[a] * over[a]
            for b in range(a + 1, PIVOTS):
                use[a] = use[a] - ratio[b, a] * use[b]
        start = first if r + PIVOTS < 8 else first + 1
        for t in range(start, size // 8):
            tile = tiles[t]
            if t > first:
                cols = [spread(tile[:, j + a : j + a + 1]) for a in each]
            terms = [cols[a] * use[a] for a in each]
            while len(terms) > 1:
                terms = [x + y for x, y in zip(terms[::2], terms[1::2])]
            tiles[t] = jnp.where(at_any, 0.0, tile) - terms[0]
        top = jnp.where(sub < r, head, tiles[first])
        for a in each:
            top = jnp.where(sub == r + a, rows[a] * lax.rsqrt(pivots[a][a]), top)
        tiles[first] = top
    return jnp.concatenate(tiles, axis=0)


def inverse_kernel(size, total_rows, panels, gram_ref, out_ref, work, factor):
    full = gram_ref.shape[0]
    count = full // size
    wide = full // panels
    half = panels // 2
    work[...] = jnp.zeros_like(work)
    for low in range(panels):
        for high in range(low, panels):
            apart = high - low
            own, other = slice(low * wide, (low + 1) * wide), slice(high * wide, (high + 1) * wide)
            if not shared(panels, wide):
                work[own, other] = gram_ref[own, other] / total_rows
            elif apart < half:
                work[own, other] = gram_ref[own, apart * wide : (apart + 1) * wide] / total_rows
            elif apart > half:
                back = panels - apart
                part = gram_ref[other, back * wide : (back + 1) * wide] / total_rows
                work[own, other] = part.T
            else:
                middle = high * wide + wide // 2
                last = slice(half * wide, half * wide + wide // 2)
                work[own, high * wide : middle] = gram_ref[own, last] / total_rows
                work[own, middle : (high + 1) * wide] = gram_ref[other, last] / total_rows

    @pl.loop(0, count)
    def _(k):
        at = pl.multiple_of(k * size, size)
        done = factor_block(work[pl.ds(at, size), pl.ds(at, size)])
        down = lax.broadcasted_iota(jnp.int32, (size, size), 0)
        across = lax.broadcasted_iota(jnp.int32, (size, size), 1)
        factor[...] = jnp.where(across <= down, done, 0.0)
        for c in range(count):
            own = slice(c * size, (c + 1) * size)
            below = slice((c + 1) * size, full)

            @pl.when(k == c)
            def _():
                lower_inv = factor[...]
                left = slice(0, c * size)
                if c > 0:
                    out_ref[own, left] = jnp.dot(
                        lower_inv, work[own, left], precision=HIGHEST,
                        preferred_element_type=jnp.float32,
                    )
                out_ref[own, own] = lower_inv
                if c + 1 < count:
                    out_ref[own, below] = jnp.zeros((size, full - (c + 1) * size), jnp.float32)
                    right = jnp.dot(
                        lower_inv, work[own, below], precision=HIGHEST,
                        preferred_element_type=jnp.float32,
                    )
                    down_left = (((0,), (0,)), ((), ()))
                    work[below, below] -= lax.dot_general(
                        right, right, down_left, precision=HIGHEST,
                        preferred_element_type=jnp.float32,
                    )
                    known = slice(0, (c + 1) * size)
                    change = lax.dot_general(
                        right, out_ref[own, known], down_left, precision=HIGHEST,
                        preferred_element_type=jnp.float32,
                    )
                    if c > 0:
                        work[below, left] -= change[:, : c * size]
                    work[below, own] = -change[:, c * size :]


def shared(panels, wide):
    return panels % 2 == 0 and wide % 256 == 0


def panel_part(panel):
    panels, wide = lax.axis_size("vecs"), panel.shape[0]
    if not shared(panels, wide):
        return panel
    me, half, short = lax.axis_index("vecs"), panels // 2, wide // 2
    twice = jnp.concatenate([panel, panel], axis=1)
    near = lax.dynamic_slice_in_dim(twice, me * wide, half * wide, 1)
    far = lax.dynamic_slice_in_dim(twice, (me + half) * wide, wide, 1)
    middle = jnp.where(me < half, far[:, :short], far[short:, :].T)
    return jnp.concatenate([near, middle], axis=1)


def inverse_factor(gram, total_rows, panels):
    full = gram.shape[0]
    size = 128
    return pl.pallas_call(
        functools.partial(inverse_kernel, size, total_rows, panels),
        out_shape=jax.ShapeDtypeStruct((full, full), jnp.float32),
        in_specs=[pl.BlockSpec(memory_space=pltpu.VMEM)],
        out_specs=pl.BlockSpec(memory_space=pltpu.VMEM),
        scratch_shapes=[
            pltpu.VMEM((full, full), jnp.float32),
            pltpu.VMEM((size, size), jnp.float32),
        ],
        compiler_params=pltpu.CompilerParams(vmem_limit_bytes=VMEM_LIMIT),
        cost_estimate=pl.CostEstimate(
            flops=40 * full * full * full, bytes_accessed=8 * full * full, transcendentals=full
        ),
    )(gram)


def split_apply(left_bf, factor):
    factor_high = factor.astype(jnp.bfloat16)
    factor_low = (factor - factor_high.astype(jnp.float32)).astype(jnp.bfloat16)
    first = jnp.dot(left_bf, factor_high.T, preferred_element_type=jnp.float32)
    second = jnp.dot(left_bf, factor_low.T, preferred_element_type=jnp.float32)
    return first + second


def shards(vectors, blocks, columns):
    total_rows = vectors.shape[0] * lax.axis_size("rows")
    final = filtered_block(vectors, blocks, columns)
    panel_width = final.shape[1]
    whole_block = lax.all_gather(final, "vecs", axis=1, tiled=True)
    panel = lax.dot_general(
        final, whole_block, (((0,), (0,)), ((), ())), preferred_element_type=jnp.float32
    )
    summed = lax.psum(panel_part(panel), "rows")
    gram = lax.all_gather(summed, "vecs", axis=0, tiled=True)
    inverse = inverse_factor(gram, total_rows, lax.axis_size("vecs"))
    own_rows = lax.dynamic_slice_in_dim(
        inverse, lax.axis_index("vecs") * panel_width, panel_width, 0
    )
    return split_apply(whole_block, own_rows)


def solution(mesh):
    in_specs = (P("rows", "vecs"), P("rows", None, None, None), P("rows", None))
    out_specs = P("rows", "vecs")
    return jax.shard_map(shards, mesh=mesh, in_specs=in_specs, out_specs=out_specs, check_vma=False)
```

```python
import functools

import jax
import jax.numpy as jnp
from jax import lax
from jax.experimental import pallas as pl
from jax.experimental.pallas import tpu as pltpu
from jax.sharding import PartitionSpec as P

DEGREE = 4

filter_center = 0.25
filter_radius = 1.25

HIGHEST = lax.Precision.HIGHEST
VMEM_LIMIT = 56 * 1024 * 1024
PIVOTS = 8


def filter_kernel(
    place_ref, vectors_ref, blocks_ref, out_ref,
    first_win, even_win, odd_win, top_a, top_b, bottom_a, bottom_b, even, odd, held,
    in_sem, send_sem, recv_sem,
):
    me, count = lax.axis_index("rows"), lax.axis_size("rows")
    block_rows, nnz = blocks_ref.shape[:2]
    reach = block_rows // 4
    span = 2 * reach
    top, bottom = (top_a, top_b), (bottom_a, bottom_b)

    @pl.when(me > 0)
    def _():
        pl.semaphore_signal(pltpu.get_barrier_semaphore(), 1, device_id={"rows": me - 1})

    @pl.when(me < count - 1)
    def _():
        pl.semaphore_signal(pltpu.get_barrier_semaphore(), 1, device_id={"rows": me + 1})

    fetches = [
        pltpu.make_async_copy(vectors_ref, first_win, in_sem.at[0]),
        pltpu.make_async_copy(vectors_ref.at[:span], top_a.at[reach:], in_sem.at[1]),
        pltpu.make_async_copy(vectors_ref.at[block_rows - span :], bottom_a.at[:span], in_sem.at[2]),
        pltpu.make_async_copy(blocks_ref, held, in_sem.at[3]),
    ]
    for fetch in fetches:
        fetch.start()

    inside = jnp.logical_and(me > 0, me < count - 1)

    @pl.when(inside)
    def _():
        pl.semaphore_wait(pltpu.get_barrier_semaphore(), 2)

    @pl.when(jnp.logical_not(inside))
    def _():
        pl.semaphore_wait(pltpu.get_barrier_semaphore(), 1)

    def to_lower(source, slot):
        return pltpu.make_async_remote_copy(
            src_ref=source.at[:reach], dst_ref=bottom[slot].at[span:],
            send_sem=send_sem.at[0, slot], recv_sem=recv_sem.at[0, slot],
            device_id={"rows": me - 1},
        )

    def to_upper(source, slot):
        return pltpu.make_async_remote_copy(
            src_ref=source.at[block_rows - reach :], dst_ref=top[slot].at[:reach],
            send_sem=send_sem.at[1, slot], recv_sem=recv_sem.at[1, slot],
            device_id={"rows": me + 1},
        )

    @pl.when(me > 0)
    def _():
        to_lower(vectors_ref, 0).start()

    @pl.when(me < count - 1)
    def _():
        to_upper(vectors_ref, 0).start()

    for fetch in fetches:
        fetch.wait()

    windows = [first_win, odd_win, even_win, odd_win, even_win]
    states = [None, even, odd, even, None]

    def compute(step, start, stop, window, group=4):
        slot = (step + 1) % 2
        target = windows[step + 1]
        last = step == DEGREE - 1

        @pl.loop(0, (stop - start) // group)
        def _(index):
            for g in range(group):
                row = start + index * group + g
                acc = None
                for j in range(nnz):
                    part = jnp.dot(
                        held[row, j], window[place_ref[row, j]], preferred_element_type=jnp.float32
                    )
                    acc = part if acc is None else acc + part
                cur = first_win[row].astype(jnp.float32) if step == 0 else states[step][row]
                new = (acc - filter_center * cur) * (1.0 / filter_radius)
                if step == 1:
                    new = 2.0 * new - first_win[row].astype(jnp.float32)
                elif step > 1:
                    new = 2.0 * new - states[step - 1][row]
                rounded = new.astype(jnp.bfloat16)
                target[row] = rounded
                if not last:
                    states[step + 1][row] = new
                    if stop <= span:
                        top[slot][row + reach] = rounded
                    if start >= span:
                        bottom[slot][row - span] = rounded

    for step in range(DEGREE):
        now = step % 2
        later = 1 - now
        source = vectors_ref if step == 0 else windows[step]
        compute(step, reach, 2 * reach, windows[step])
        compute(step, 2 * reach, 3 * reach, windows[step])

        @pl.when(me < count - 1)
        def _():
            to_lower(source, now).wait_recv()

        compute(step, 3 * reach, 4 * reach, bottom[now])
        if step < DEGREE - 1:

            @pl.when(me < count - 1)
            def _():
                to_upper(windows[step + 1], later).start()

        @pl.when(me > 0)
        def _():
            to_upper(source, now).wait_recv()

        compute(step, 0, reach, top[now])
        if step < DEGREE - 1:

            @pl.when(me > 0)
            def _():
                to_lower(windows[step + 1], later).start()

        @pl.when(me > 0)
        def _():
            to_lower(source, now).wait_send()

        @pl.when(me < count - 1)
        def _():
            to_upper(source, now).wait_send()

    done = pltpu.make_async_copy(windows[DEGREE], out_ref, in_sem.at[0])
    done.start()
    done.wait()


def filtered_block(vectors, blocks, columns):
    rows, width = vectors.shape
    block_rows, nnz, size_b = blocks.shape[:3]
    reach = block_rows // 4
    row = lax.broadcasted_iota(jnp.int32, columns.shape, 0)
    shift = jnp.where(row < reach, reach, jnp.where(row < block_rows - reach, 0, -2 * reach))
    place = columns - lax.axis_index("rows") * block_rows + shift
    window = pltpu.VMEM((block_rows, size_b, width), jnp.bfloat16)
    side = pltpu.VMEM((3 * reach, size_b, width), jnp.bfloat16)
    state = pltpu.VMEM((block_rows, size_b, width), jnp.float32)
    anywhere = pl.BlockSpec(memory_space=pl.ANY)
    out = pl.pallas_call(
        filter_kernel,
        out_shape=jax.ShapeDtypeStruct((block_rows, size_b, width), jnp.bfloat16),
        in_specs=[pl.BlockSpec(memory_space=pltpu.SMEM), anywhere, anywhere],
        out_specs=anywhere,
        scratch_shapes=[window] * 3 + [side] * 4 + [state] * 2 + [
            pltpu.VMEM(blocks.shape, jnp.bfloat16),
            pltpu.SemaphoreType.DMA((4,)),
            pltpu.SemaphoreType.DMA((2, 2)),
            pltpu.SemaphoreType.DMA((2, 2)),
        ],
        compiler_params=pltpu.CompilerParams(
            vmem_limit_bytes=VMEM_LIMIT, collective_id=0, has_side_effects=True
        ),
    )(place, vectors.reshape(block_rows, size_b, width), blocks)
    return out.reshape(rows, width)


def factor_block(block):
    size = block.shape[0]
    tiles = [block[8 * t : 8 * (t + 1), :] for t in range(size // 8)]
    lane = lax.broadcasted_iota(jnp.int32, (8, size), 1)
    sub = lax.broadcasted_iota(jnp.int32, (8, size), 0)

    def spread(array):
        return jnp.broadcast_to(array, (8, size))

    for j in range(0, size, PIVOTS):
        first, r = divmod(j, 8)
        each = range(PIVOTS)
        at_any = jnp.logical_and(lane >= j, lane < j + PIVOTS)
        head = tiles[first]
        cols = [spread(head[:, j + a : j + a + 1]) for a in each]
        pivots = [[spread(cols[a][r + b : r + b + 1, :]) for a in range(b + 1)] for b in each]
        rows = [jnp.where(at_any, 0.0, spread(head[r + a : r + a + 1, :])) for a in each]
        rows = [jnp.where(lane == j + a, 1.0, rows[a]) for a in each]
        over, ratio = [], {}
        for a in each:
            over.append(1.0 / pivots[a][a])
            for b in range(a + 1, PIVOTS):
                ratio[b, a] = pivots[b][a] * over[a]
                for c in range(a + 1, b + 1):
                    pivots[b][c] = pivots[b][c] - ratio[b, a] * pivots[c][a]
                rows[b] = rows[b] - ratio[b, a] * rows[a]
        use = [None] * PIVOTS
        for a in reversed(each):
            use[a] = rows[a] * over[a]
            for b in range(a + 1, PIVOTS):
                use[a] = use[a] - ratio[b, a] * use[b]
        start = first if r + PIVOTS < 8 else first + 1
        for t in range(start, size // 8):
            tile = tiles[t]
            if t > first:
                cols = [spread(tile[:, j + a : j + a + 1]) for a in each]
            terms = [cols[a] * use[a] for a in each]
            while len(terms) > 1:
                terms = [x + y for x, y in zip(terms[::2], terms[1::2])]
            tiles[t] = jnp.where(at_any, 0.0, tile) - terms[0]
        top = jnp.where(sub < r, head, tiles[first])
        for a in each:
            top = jnp.where(sub == r + a, rows[a] * lax.rsqrt(pivots[a][a]), top)
        tiles[first] = top
    return jnp.concatenate(tiles, axis=0)


def gram_stages(rows, devices):
    stages, bit, held = [], 1, rows
    while bit < devices:
        halve = held % 16 == 0
        stages.append((bit, halve))
        held, bit = held // 2 if halve else held, bit * 2
    return stages


def flipped(index, bit):
    return index + bit - 2 * bit * lax.rem(index // bit, 2)


def gram_kernel(
    stages, final_ref, out_ref, own, beside, across, far, cross, total, full, landing, cross_in,
    local_sem, side_send, side_recv, x_send, x_recv, pass_send, pass_recv, stage_sem, all_send, all_recv,
):
    me, panel = lax.axis_index("rows"), lax.axis_index("vecs")
    core, side = lax.rem(panel, 2), panel // 2
    rows, wide = own.shape
    half, short = rows // 2, wide // 2
    parts = across.shape[0]
    chunk = half // parts
    near, over = flipped(panel, 1), flipped(panel, 2)
    contract = (((0,), (0,)), ((), ()))

    peers = [{"vecs": near}, {"vecs": over}] + [{"rows": flipped(me, bit)} for bit, _ in stages]
    barrier = pltpu.get_barrier_semaphore()
    for peer in peers:
        pl.semaphore_signal(barrier, 1, device_id=peer)
    fetch = pltpu.make_async_copy(final_ref, own, local_sem.at[0])
    fetch.start()
    pl.semaphore_wait(barrier, len(peers))
    fetch.wait()

    to_over, to_near, passed = [], [], []
    for part in range(parts):
        start = pl.multiple_of((1 - side) * half + part * chunk, chunk)
        to_over.append(
            pltpu.make_async_remote_copy(
                src_ref=own.at[pl.ds(start, chunk)], dst_ref=across.at[part],
                send_sem=x_send.at[part], recv_sem=x_recv.at[part], device_id={"vecs": over},
            )
        )
        passed.append(
            pltpu.make_async_remote_copy(
                src_ref=across.at[part], dst_ref=far.at[part],
                send_sem=pass_send.at[part], recv_sem=pass_recv.at[part], device_id={"vecs": near},
            )
        )
    for copy in to_over:
        copy.start()
    for part in range(2):
        to_near.append(
            pltpu.make_async_remote_copy(
                src_ref=own.at[part * half : (part + 1) * half], dst_ref=beside.at[part],
                send_sem=side_send.at[part], recv_sem=side_recv.at[part], device_id={"vecs": near},
            )
        )
        to_near[-1].start()

    def product(left, right):
        return lax.dot_general(left, right, contract, preferred_element_type=jnp.float32)

    total[: wide + short, :] = jnp.zeros((wide + short, wide), jnp.float32)
    cross[...] = jnp.zeros_like(cross)

    @pl.loop(0, rows // chunk)
    def _(index):
        at = pl.ds(pl.multiple_of(index * chunk, chunk), chunk)
        total[:wide, :] += product(own[at, :], own[at, :])

    for copy in to_near:
        copy.wait()
    for part in range(2):

        @pl.loop(0, parts)
        def _(index):
            at = pl.ds(pl.multiple_of(index * chunk, chunk), chunk)
            mine = pl.ds(pl.multiple_of(part * half + index * chunk, chunk), chunk)

            @pl.when(core == 0)
            def _():
                total[wide : wide + short, :] += product(own[mine, :short], beside[part, at, :])

            @pl.when(core == 1)
            def _():
                total[wide : wide + short, :] += product(beside[part, at, short:], own[mine, :])

    for part in range(parts):
        to_over[part].wait()
        at = slice(part * chunk, (part + 1) * chunk)

        @pl.when(side == 0)
        def _():
            passed[part].start()
            mine = own[at, :]

            @pl.when(core == 0)
            def _():
                cross[0] += product(mine, across[part])

            @pl.when(core == 1)
            def _():
                cross[1] += product(mine, across[part])

        @pl.when(side == 1)
        def _():
            there = across[part]
            later = slice(half + part * chunk, half + (part + 1) * chunk)

            @pl.when(core == 0)
            def _():
                cross[0] += product(there, own[later, :])
                cross[1] += product(there, beside[1, at, :])

            @pl.when(core == 1)
            def _():
                cross[0] += product(there, beside[1, at, :])
                cross[1] += product(there, own[later, :])

    @pl.when(side == 0)
    def _():
        for part in range(parts):
            passed[part].wait()
            mine = own[part * chunk : (part + 1) * chunk, :]

            @pl.when(core == 0)
            def _():
                cross[1] += product(mine, far[part])

            @pl.when(core == 1)
            def _():
                cross[0] += product(mine, far[part])

    swap = pltpu.make_async_remote_copy(
        src_ref=cross.at[1 - side], dst_ref=cross_in,
        send_sem=local_sem.at[1], recv_sem=local_sem.at[2], device_id={"vecs": over},
    )
    swap.start()
    swap.wait()
    total[wide + short :, :] = cross[side] + cross_in[...]

    start, held, taken = 0, total.shape[0], 0
    ranges = []
    for number, (bit, halve) in enumerate(stages):
        size = held // 2 if halve else held
        upper = lax.rem(me // bit, 2)
        ranges.append((start, size))
        keep = pl.multiple_of(start + upper * size, 8) if halve else start
        give = pl.multiple_of(start + (1 - upper) * size, 8) if halve else start
        slot = landing.at[taken : taken + size]
        copy = pltpu.make_async_remote_copy(
            src_ref=total.at[pl.ds(give, size)], dst_ref=slot,
            send_sem=stage_sem.at[0, number], recv_sem=stage_sem.at[1, number],
            device_id={"rows": flipped(me, bit)},
        )
        copy.start()
        copy.wait()
        total[pl.ds(keep, size), :] += landing[taken : taken + size, :]
        start, held, taken = keep, size, taken + size

    full[panel, pl.ds(start, held), :] = total[pl.ds(start, held), :]
    pending = []

    def share(number, first, size):
        piece = full.at[panel, pl.ds(first, size)]
        copies = []
        for kind, peer in enumerate((over, near)):
            copies.append(
                pltpu.make_async_remote_copy(
                    src_ref=piece, dst_ref=piece, send_sem=all_send.at[kind, number],
                    recv_sem=all_recv.at[kind, number], device_id={"vecs": peer},
                )
            )
            copies[-1].start()
        theirs = full.at[over, pl.ds(first, size)]
        onward = pltpu.make_async_remote_copy(
            src_ref=theirs, dst_ref=theirs, send_sem=all_send.at[2, number],
            recv_sem=all_recv.at[2, number], device_id={"vecs": near},
        )
        pending.append((copies, onward))

    share(0, start, held)
    count = 1
    for number in reversed(range(len(stages))):
        bit, halve = stages[number]
        if not halve:
            continue
        upper = lax.rem(me // bit, 2)
        below, size = ranges[number]
        mine = pl.multiple_of(below + upper * size, 8)
        other = pl.multiple_of(below + (1 - upper) * size, 8)
        piece = full.at[panel, pl.ds(mine, size)]
        copy = pltpu.make_async_remote_copy(
            src_ref=piece, dst_ref=piece, send_sem=stage_sem.at[2, number],
            recv_sem=stage_sem.at[3, number], device_id={"rows": flipped(me, bit)},
        )
        copy.start()
        copy.wait()
        share(count, other, size)
        count += 1
    for copies, onward in pending:
        copies[0].wait()
        onward.start()
        copies[1].wait()
    for _, onward in pending:
        onward.wait()
    done = pltpu.make_async_copy(full, out_ref, local_sem.at[3])
    done.start()
    done.wait()


def gram_sum(final):
    rows, wide = final.shape
    panels, devices = lax.axis_size("vecs"), lax.axis_size("rows")
    tall = 2 * wide + wide // 2
    stages = gram_stages(tall, devices)
    parts = 4
    chunk = rows // 2 // parts
    dma = pltpu.SemaphoreType.DMA
    steps = len(stages)
    return pl.pallas_call(
        functools.partial(gram_kernel, stages),
        out_shape=jax.ShapeDtypeStruct((panels, tall, wide), jnp.float32),
        in_specs=[pl.BlockSpec(memory_space=pl.ANY)],
        out_specs=pl.BlockSpec(memory_space=pl.ANY),
        scratch_shapes=[
            pltpu.VMEM((rows, wide), jnp.bfloat16),
            pltpu.VMEM((2, rows // 2, wide), jnp.bfloat16),
            pltpu.VMEM((parts, chunk, wide), jnp.bfloat16),
            pltpu.VMEM((parts, chunk, wide), jnp.bfloat16),
            pltpu.VMEM((2, wide, wide), jnp.float32),
            pltpu.VMEM((tall, wide), jnp.float32),
            pltpu.VMEM((panels, tall, wide), jnp.float32),
            pltpu.VMEM((2 * tall, wide), jnp.float32),
            pltpu.VMEM((wide, wide), jnp.float32),
            dma((4,)), dma((2,)), dma((2,)), dma((parts,)), dma((parts,)), dma((parts,)), dma((parts,)),
            dma((4, steps)), dma((3, steps + 1)), dma((3, steps + 1)),
        ],
        compiler_params=pltpu.CompilerParams(
            vmem_limit_bytes=VMEM_LIMIT, collective_id=1, has_side_effects=True
        ),
    )(final)


def inverse_kernel(size, total_rows, gram_ref, out_ref, work, factor):
    full = out_ref.shape[0]
    panels, _, wide = gram_ref.shape
    count, short = full // size, wide // 2
    work[...] = jnp.zeros_like(work)
    for panel in range(panels):
        core, side = panel % 2, panel // 2
        own = slice(panel * wide, (panel + 1) * wide)
        work[own, own] = gram_ref[panel, :wide, :] / total_rows
        first = 2 * side * wide
        high = slice(first + core * short, first + (core + 1) * short)
        work[high, first + wide : first + 2 * wide] = gram_ref[panel, wide : wide + short, :] / total_rows
        low = slice(core * wide, (core + 1) * wide)
        other = slice((2 + side) * wide, (3 + side) * wide)
        work[low, other] = gram_ref[panel, wide + short :, :] / total_rows

    @pl.loop(0, count)
    def _(k):
        at = pl.multiple_of(k * size, size)
        done = factor_block(work[pl.ds(at, size), pl.ds(at, size)])
        down = lax.broadcasted_iota(jnp.int32, (size, size), 0)
        across = lax.broadcasted_iota(jnp.int32, (size, size), 1)
        factor[...] = jnp.where(across <= down, done, 0.0)
        for c in range(count):
            own = slice(c * size, (c + 1) * size)
            below = slice((c + 1) * size, full)

            @pl.when(k == c)
            def _():
                lower_inv = factor[...]
                left = slice(0, c * size)
                if c > 0:
                    out_ref[own, left] = jnp.dot(
                        lower_inv, work[own, left], precision=HIGHEST,
                        preferred_element_type=jnp.float32,
                    )
                out_ref[own, own] = lower_inv
                if c + 1 < count:
                    out_ref[own, below] = jnp.zeros((size, full - (c + 1) * size), jnp.float32)
                    right = jnp.dot(
                        lower_inv, work[own, below], precision=HIGHEST,
                        preferred_element_type=jnp.float32,
                    )
                    down_left = (((0,), (0,)), ((), ()))
                    work[below, below] -= lax.dot_general(
                        right, right, down_left, precision=HIGHEST,
                        preferred_element_type=jnp.float32,
                    )
                    known = slice(0, (c + 1) * size)
                    change = lax.dot_general(
                        right, out_ref[own, known], down_left, precision=HIGHEST,
                        preferred_element_type=jnp.float32,
                    )
                    if c > 0:
                        work[below, left] -= change[:, : c * size]
                    work[below, own] = -change[:, c * size :]


def inverse_factor(gram, total_rows):
    full = gram.shape[0] * gram.shape[2]
    size = 128
    return pl.pallas_call(
        functools.partial(inverse_kernel, size, total_rows),
        out_shape=jax.ShapeDtypeStruct((full, full), jnp.float32),
        in_specs=[pl.BlockSpec(memory_space=pltpu.VMEM)],
        out_specs=pl.BlockSpec(memory_space=pltpu.VMEM),
        scratch_shapes=[
            pltpu.VMEM((full, full), jnp.float32),
            pltpu.VMEM((size, size), jnp.float32),
        ],
        compiler_params=pltpu.CompilerParams(vmem_limit_bytes=VMEM_LIMIT),
        cost_estimate=pl.CostEstimate(
            flops=40 * full * full * full, bytes_accessed=8 * full * full, transcendentals=full
        ),
    )(gram)


def split_apply(left_bf, factor):
    factor_high = factor.astype(jnp.bfloat16)
    factor_low = (factor - factor_high.astype(jnp.float32)).astype(jnp.bfloat16)
    first = jnp.dot(left_bf, factor_high.T, preferred_element_type=jnp.float32)
    second = jnp.dot(left_bf, factor_low.T, preferred_element_type=jnp.float32)
    return first + second


def shards(vectors, blocks, columns):
    total_rows = vectors.shape[0] * lax.axis_size("rows")
    final = filtered_block(vectors, blocks, columns)
    panel_width = final.shape[1]
    gram = gram_sum(final)
    final, gram = lax.optimization_barrier((final, gram))
    whole_block = lax.all_gather(final, "vecs", axis=1, tiled=True)
    inverse = inverse_factor(gram, total_rows)
    own_rows = lax.dynamic_slice_in_dim(
        inverse, lax.axis_index("vecs") * panel_width, panel_width, 0
    )
    return split_apply(whole_block, own_rows)


def solution(mesh):
    in_specs = (P("rows", "vecs"), P("rows", None, None, None), P("rows", None))
    out_specs = P("rows", "vecs")
    return jax.shard_map(shards, mesh=mesh, in_specs=in_specs, out_specs=out_specs, check_vma=False)
```

```python
import functools

import jax
import jax.numpy as jnp
from jax import lax
from jax.experimental import pallas as pl
from jax.experimental.pallas import tpu as pltpu
from jax.sharding import PartitionSpec as P

DEGREE = 4

filter_center = 0.25
filter_radius = 1.25

VMEM_LIMIT = 56 * 1024 * 1024


def filter_kernel(
    place_ref, vectors_ref, blocks_ref, out_ref,
    first_win, even_win, odd_win, top_a, top_b, bottom_a, bottom_b, even, odd, held,
    in_sem, send_sem, recv_sem,
):
    me, count = lax.axis_index("rows"), lax.axis_size("rows")
    block_rows, nnz = blocks_ref.shape[:2]
    reach = block_rows // 4
    span = 2 * reach
    top, bottom = (top_a, top_b), (bottom_a, bottom_b)

    @pl.when(me > 0)
    def _():
        pl.semaphore_signal(pltpu.get_barrier_semaphore(), 1, device_id={"rows": me - 1})

    @pl.when(me < count - 1)
    def _():
        pl.semaphore_signal(pltpu.get_barrier_semaphore(), 1, device_id={"rows": me + 1})

    fetches = [
        pltpu.make_async_copy(vectors_ref, first_win, in_sem.at[0]),
        pltpu.make_async_copy(vectors_ref.at[:span], top_a.at[reach:], in_sem.at[1]),
        pltpu.make_async_copy(vectors_ref.at[block_rows - span :], bottom_a.at[:span], in_sem.at[2]),
        pltpu.make_async_copy(blocks_ref, held, in_sem.at[3]),
    ]
    for fetch in fetches:
        fetch.start()

    inside = jnp.logical_and(me > 0, me < count - 1)

    @pl.when(inside)
    def _():
        pl.semaphore_wait(pltpu.get_barrier_semaphore(), 2)

    @pl.when(jnp.logical_not(inside))
    def _():
        pl.semaphore_wait(pltpu.get_barrier_semaphore(), 1)

    def to_lower(source, slot):
        return pltpu.make_async_remote_copy(
            src_ref=source.at[:reach], dst_ref=bottom[slot].at[span:],
            send_sem=send_sem.at[0, slot], recv_sem=recv_sem.at[0, slot],
            device_id={"rows": me - 1},
        )

    def to_upper(source, slot):
        return pltpu.make_async_remote_copy(
            src_ref=source.at[block_rows - reach :], dst_ref=top[slot].at[:reach],
            send_sem=send_sem.at[1, slot], recv_sem=recv_sem.at[1, slot],
            device_id={"rows": me + 1},
        )

    @pl.when(me > 0)
    def _():
        to_lower(vectors_ref, 0).start()

    @pl.when(me < count - 1)
    def _():
        to_upper(vectors_ref, 0).start()

    for fetch in fetches:
        fetch.wait()

    windows = [first_win, odd_win, even_win, odd_win, even_win]
    states = [None, even, odd, even, None]

    def compute(step, start, stop, window, group=4):
        slot = (step + 1) % 2
        target = windows[step + 1]
        last = step == DEGREE - 1

        @pl.loop(0, (stop - start) // group)
        def _(index):
            for g in range(group):
                row = start + index * group + g
                acc = None
                for j in range(nnz):
                    part = jnp.dot(
                        held[row, j], window[place_ref[row, j]], preferred_element_type=jnp.float32
                    )
                    acc = part if acc is None else acc + part
                cur = first_win[row].astype(jnp.float32) if step == 0 else states[step][row]
                new = (acc - filter_center * cur) * (1.0 / filter_radius)
                if step == 1:
                    new = 2.0 * new - first_win[row].astype(jnp.float32)
                elif step > 1:
                    new = 2.0 * new - states[step - 1][row]
                rounded = new.astype(jnp.bfloat16)
                target[row] = rounded
                if not last:
                    states[step + 1][row] = new
                    if stop <= span:
                        top[slot][row + reach] = rounded
                    if start >= span:
                        bottom[slot][row - span] = rounded

    for step in range(DEGREE):
        now = step % 2
        later = 1 - now
        source = vectors_ref if step == 0 else windows[step]
        compute(step, reach, 2 * reach, windows[step])
        compute(step, 2 * reach, 3 * reach, windows[step])

        @pl.when(me < count - 1)
        def _():
            to_lower(source, now).wait_recv()

        compute(step, 3 * reach, 4 * reach, bottom[now])
        if step < DEGREE - 1:

            @pl.when(me < count - 1)
            def _():
                to_upper(windows[step + 1], later).start()

        @pl.when(me > 0)
        def _():
            to_upper(source, now).wait_recv()

        compute(step, 0, reach, top[now])
        if step < DEGREE - 1:

            @pl.when(me > 0)
            def _():
                to_lower(windows[step + 1], later).start()

        @pl.when(me > 0)
        def _():
            to_lower(source, now).wait_send()

        @pl.when(me < count - 1)
        def _():
            to_upper(source, now).wait_send()

    done = pltpu.make_async_copy(windows[DEGREE], out_ref, in_sem.at[0])
    done.start()
    done.wait()


def filtered_block(vectors, blocks, columns):
    rows, width = vectors.shape
    block_rows, nnz, size_b = blocks.shape[:3]
    reach = block_rows // 4
    row = lax.broadcasted_iota(jnp.int32, columns.shape, 0)
    shift = jnp.where(row < reach, reach, jnp.where(row < block_rows - reach, 0, -2 * reach))
    place = columns - lax.axis_index("rows") * block_rows + shift
    window = pltpu.VMEM((block_rows, size_b, width), jnp.bfloat16)
    side = pltpu.VMEM((3 * reach, size_b, width), jnp.bfloat16)
    state = pltpu.VMEM((block_rows, size_b, width), jnp.float32)
    anywhere = pl.BlockSpec(memory_space=pl.ANY)
    out = pl.pallas_call(
        filter_kernel,
        out_shape=jax.ShapeDtypeStruct((block_rows, size_b, width), jnp.bfloat16),
        in_specs=[pl.BlockSpec(memory_space=pltpu.SMEM), anywhere, anywhere],
        out_specs=anywhere,
        scratch_shapes=[window] * 3 + [side] * 4 + [state] * 2 + [
            pltpu.VMEM(blocks.shape, jnp.bfloat16),
            pltpu.SemaphoreType.DMA((4,)),
            pltpu.SemaphoreType.DMA((2, 2)),
            pltpu.SemaphoreType.DMA((2, 2)),
        ],
        compiler_params=pltpu.CompilerParams(
            vmem_limit_bytes=VMEM_LIMIT, collective_id=0, has_side_effects=True
        ),
    )(place, vectors.reshape(block_rows, size_b, width), blocks)
    return out.reshape(rows, width)


def factor_block(block):
    size = block.shape[0]
    tiles = [block[8 * t : 8 * (t + 1), :] for t in range(size // 8)]
    lane = lax.broadcasted_iota(jnp.int32, (8, size), 1)
    sub = lax.broadcasted_iota(jnp.int32, (8, size), 0)

    def spread(array):
        return jnp.broadcast_to(array, (8, size))

    for first in range(size // 8):
        j = 8 * first
        each = range(8)
        at_any = jnp.logical_and(lane >= j, lane < j + 8)
        head = tiles[first]
        cols = [spread(head[:, j + a : j + a + 1]) for a in each]
        p = [[spread(cols[a][b : b + 1, :]) for a in range(b + 1)] for b in each]
        rows = [jnp.where(at_any, 0.0, spread(head[a : a + 1, :])) for a in each]
        rows = [jnp.where(lane == j + a, 1.0, rows[a]) for a in each]
        pairs, ready = [], []
        for a in range(0, 8, 2):
            b = a + 1
            det = p[a][a] * p[b][b] - p[b][a] * p[b][a]
            inv = 1.0 / det
            e_aa, e_ab, e_bb = p[b][b] * inv, p[b][a] * inv, p[a][a] * inv
            over = 1.0 / p[a][a]
            ready.append(rows[a] * lax.rsqrt(p[a][a]))
            ready.append((rows[b] - (p[b][a] * over) * rows[a]) * lax.rsqrt(det * over))
            mult = {}
            for c in range(b + 1, 8):
                mult[c, 0] = p[c][a] * e_aa - p[c][b] * e_ab
                mult[c, 1] = p[c][b] * e_bb - p[c][a] * e_ab
            for c in range(b + 1, 8):
                for d in range(b + 1, c + 1):
                    p[c][d] = p[c][d] - (mult[c, 0] * p[d][a] + mult[c, 1] * p[d][b])
            pairs.append((e_aa, e_ab, e_bb, mult, rows[a], rows[b]))
            for c in range(b + 1, 8):
                rows[c] = rows[c] - (mult[c, 0] * rows[a] + mult[c, 1] * rows[b])
        use = [None] * 8
        for number in reversed(range(4)):
            a, b = 2 * number, 2 * number + 1
            e_aa, e_ab, e_bb, mult, row_a, row_b = pairs[number]
            use[a] = e_aa * row_a - e_ab * row_b
            use[b] = e_bb * row_b - e_ab * row_a
            for c in range(b + 1, 8):
                use[a] = use[a] - mult[c, 0] * use[c]
                use[b] = use[b] - mult[c, 1] * use[c]
        for t in range(first + 1, size // 8):
            tile = tiles[t]
            cols = [spread(tile[:, j + a : j + a + 1]) for a in each]
            terms = [cols[a] * use[a] for a in each]
            while len(terms) > 1:
                terms = [x + y for x, y in zip(terms[::2], terms[1::2])]
            tiles[t] = jnp.where(at_any, 0.0, tile) - terms[0]
        top = ready[0]
        for a in range(1, 8):
            top = jnp.where(sub == a, ready[a], top)
        tiles[first] = top
    done = jnp.concatenate(tiles, axis=0)
    down = lax.broadcasted_iota(jnp.int32, (size, size), 0)
    across = lax.broadcasted_iota(jnp.int32, (size, size), 1)
    return jnp.where(across <= down, done, 0.0)


def halves(array):
    high = array.astype(jnp.bfloat16)
    return high, (array - high.astype(jnp.float32)).astype(jnp.bfloat16)


PLAIN = (((1,), (0,)), ((), ()))
TURNED = (((1,), (1,)), ((), ()))


def triple(left, right, dims):
    def one(a, b):
        return lax.dot_general(a, b, dims, preferred_element_type=jnp.float32)

    return one(left[0], right[0]) + (one(left[0], right[1]) + one(left[1], right[0]))


def gram_stages(rows, devices):
    stages, bit, held = [], 1, rows
    while bit < devices:
        halve = held % 16 == 0
        stages.append((bit, halve))
        held, bit = held // 2 if halve else held, bit * 2
    return stages


def flipped(index, bit):
    return index + bit - 2 * bit * lax.rem(index // bit, 2)


def gram_kernel(
    stages, parts, final_ref, out_ref, block_ref, block, cross, total, full, landing, cross_in,
    local_sem, side_sem, x_sem, pass_sem, rest_sem, on_sem, stage_sem, all_sem,
):
    me, panel = lax.axis_index("rows"), lax.axis_index("vecs")
    core, side = lax.rem(panel, 2), panel // 2
    _, rows, wide = block.shape
    half, short = rows // 2, wide // 2
    chunk = half // parts
    near, over = flipped(panel, 1), flipped(panel, 2)
    beyond = flipped(over, 1)
    contract = (((0,), (0,)), ((), ()))

    peers = [{"vecs": near}, {"vecs": over}] + [{"rows": flipped(me, bit)} for bit, _ in stages]
    barrier = pltpu.get_barrier_semaphore()
    for peer in peers:
        pl.semaphore_signal(barrier, 1, device_id=peer)
    fetch = pltpu.make_async_copy(final_ref, block.at[panel], local_sem.at[0])
    fetch.start()
    pl.semaphore_wait(barrier, len(peers))
    fetch.wait()

    def send(which, start, size, sems, number, peer):
        piece = block.at[which, pl.ds(pl.multiple_of(start, chunk), size)]
        return pltpu.make_async_remote_copy(
            src_ref=piece, dst_ref=piece, send_sem=sems.at[0, number],
            recv_sem=sems.at[1, number], device_id={"vecs": peer},
        )

    def at(start):
        return pl.ds(pl.multiple_of(start, chunk), chunk)

    to_over = [send(panel, (1 - side) * half + n * chunk, chunk, x_sem, n, over) for n in range(parts)]
    passed = [send(over, side * half + n * chunk, chunk, pass_sem, n, near) for n in range(parts)]
    to_near = [send(panel, n * half, half, side_sem, n, near) for n in range(2)]
    for copy in to_over + to_near:
        copy.start()
    keep_own = pltpu.make_async_copy(block.at[panel], block_ref.at[panel], local_sem.at[0])
    keep_own.start()

    def product(left, right):
        return lax.dot_general(left, right, contract, preferred_element_type=jnp.float32)

    total[: wide + short, :] = jnp.zeros((wide + short, wide), jnp.float32)
    cross[...] = jnp.zeros_like(cross)

    @pl.loop(0, rows // chunk)
    def _(index):
        own = block[panel, at(index * chunk), :]
        total[:wide, :] += product(own, own)

    for copy in to_near:
        copy.wait()
    keep_near = pltpu.make_async_copy(block.at[near], block_ref.at[near], local_sem.at[1])
    keep_near.start()

    @pl.loop(0, rows // chunk)
    def _(index):
        own = block[panel, at(index * chunk), :]
        beside = block[near, at(index * chunk), :]

        @pl.when(core == 0)
        def _():
            total[wide : wide + short, :] += product(beside[:, :short], own)

        @pl.when(core == 1)
        def _():
            total[wide : wide + short, :] += product(own[:, short:], beside)

    for part in range(parts):
        to_over[part].wait()
        passed[part].start()
        here = at(side * half + part * chunk)
        own = block[panel, here, :]
        there = block[over, here, :]

        @pl.when(side == 0)
        def _():
            cross[core] += product(there, own)

        @pl.when(side == 1)
        def _():
            cross[core] += product(own, there)
            cross[1 - core] += product(block[near, here, :], there)

    for part in range(parts):
        passed[part].wait()

        @pl.when(side == 0)
        def _():
            here = at(part * chunk)
            cross[1 - core] += product(block[beyond, here, :], block[panel, here, :])

    swap = pltpu.make_async_remote_copy(
        src_ref=cross.at[1 - side], dst_ref=cross_in,
        send_sem=local_sem.at[2], recv_sem=local_sem.at[3], device_id={"vecs": over},
    )
    swap.start()
    swap.wait()
    total[wide + short :, :] = cross[side] + cross_in[...]

    rest = [send(panel, n * half // 2, half // 2, rest_sem, n, over) for n in range(2)]
    onward = [send(over, n * half // 2, half // 2, on_sem, n, near) for n in range(2)]

    @pl.when(side == 0)
    def _():
        for copy in rest:
            copy.start()

    start, held, taken = 0, total.shape[0], 0
    ranges = []
    for number, (bit, halve) in enumerate(stages):
        size = held // 2 if halve else held
        upper = lax.rem(me // bit, 2)
        ranges.append((start, size))
        keep = pl.multiple_of(start + upper * size, 8) if halve else start
        give = pl.multiple_of(start + (1 - upper) * size, 8) if halve else start
        copy = pltpu.make_async_remote_copy(
            src_ref=total.at[pl.ds(give, size)], dst_ref=landing.at[taken : taken + size],
            send_sem=stage_sem.at[0, number], recv_sem=stage_sem.at[1, number],
            device_id={"rows": flipped(me, bit)},
        )
        copy.start()
        copy.wait()
        total[pl.ds(keep, size), :] += landing[taken : taken + size, :]
        start, held, taken = keep, size, taken + size

    full[panel, pl.ds(start, held), :] = total[pl.ds(start, held), :]
    pending = []

    def share(number, first, size):
        def hand(which, kind, peer):
            piece = full.at[which, pl.ds(first, size)]
            return pltpu.make_async_remote_copy(
                src_ref=piece, dst_ref=piece, send_sem=all_sem.at[0, kind, number],
                recv_sem=all_sem.at[1, kind, number], device_id={"vecs": peer},
            )

        copies = [hand(panel, 0, over), hand(panel, 1, near)]
        for copy in copies:
            copy.start()
        pending.append(copies + [hand(over, 2, near)])

    share(0, start, held)
    count = 1
    for number in reversed(range(len(stages))):
        bit, halve = stages[number]
        if not halve:
            continue
        upper = lax.rem(me // bit, 2)
        below, size = ranges[number]
        mine = pl.multiple_of(below + upper * size, 8)
        other = pl.multiple_of(below + (1 - upper) * size, 8)
        piece = full.at[panel, pl.ds(mine, size)]
        copy = pltpu.make_async_remote_copy(
            src_ref=piece, dst_ref=piece, send_sem=stage_sem.at[2, number],
            recv_sem=stage_sem.at[3, number], device_id={"rows": flipped(me, bit)},
        )
        copy.start()
        copy.wait()
        share(count, other, size)
        count += 1

    for first, second, third in pending:
        first.wait()
        third.start()
        second.wait()
    keep_own.wait()
    keep_near.wait()
    keep_over = pltpu.make_async_copy(block.at[over], block_ref.at[over], local_sem.at[0])
    keep_beyond = pltpu.make_async_copy(block.at[beyond], block_ref.at[beyond], local_sem.at[1])

    @pl.when(side == 0)
    def _():
        for copy in rest:
            copy.wait_send()

    @pl.when(side == 1)
    def _():
        for number in range(2):
            rest[number].wait_recv()
            onward[number].start()
        keep_over.start()
        for copy in onward:
            copy.wait()
        keep_beyond.start()

    for _, _, third in pending:
        third.wait()
    done = pltpu.make_async_copy(full, out_ref, local_sem.at[2])
    done.start()

    @pl.when(side == 1)
    def _():
        keep_over.wait()
        keep_beyond.wait()

    done.wait()


def gram_sum(final):
    rows, wide = final.shape
    panels, devices = lax.axis_size("vecs"), lax.axis_size("rows")
    tall = 2 * wide + wide // 2
    stages = gram_stages(tall, devices)
    parts = 4
    dma = pltpu.SemaphoreType.DMA
    steps = len(stages)
    return pl.pallas_call(
        functools.partial(gram_kernel, stages, parts),
        out_shape=[
            jax.ShapeDtypeStruct((panels, tall, wide), jnp.float32),
            jax.ShapeDtypeStruct((panels, rows, wide), jnp.bfloat16),
        ],
        in_specs=[pl.BlockSpec(memory_space=pl.ANY)],
        out_specs=[pl.BlockSpec(memory_space=pl.ANY)] * 2,
        scratch_shapes=[
            pltpu.VMEM((panels, rows, wide), jnp.bfloat16),
            pltpu.VMEM((2, wide, wide), jnp.float32),
            pltpu.VMEM((tall, wide), jnp.float32),
            pltpu.VMEM((panels, tall, wide), jnp.float32),
            pltpu.VMEM((2 * tall, wide), jnp.float32),
            pltpu.VMEM((wide, wide), jnp.float32),
            dma((4,)), dma((2, 2)), dma((2, parts)), dma((2, parts)), dma((2, 2)), dma((2, 2)),
            dma((4, steps)), dma((2, 3, steps + 1)),
        ],
        compiler_params=pltpu.CompilerParams(
            vmem_limit_bytes=VMEM_LIMIT, collective_id=1, has_side_effects=True
        ),
    )(final)


def inverse_kernel(size, total_rows, gram_ref, out_ref, work, inverse, scale):
    full = inverse.shape[0]
    panels, _, wide = gram_ref.shape
    count, short = full // size, wide // 2
    same = lax.broadcasted_iota(jnp.int32, (wide, wide), 0) == lax.broadcasted_iota(
        jnp.int32, (wide, wide), 1
    )
    down, along = [], []
    for panel in range(panels):
        diagonal = jnp.where(same, gram_ref[panel, :wide, :], 0.0)
        sums = jnp.sum(diagonal, axis=0, keepdims=True)
        along.append(lax.rsqrt(sums))
        down.append(lax.rsqrt(jnp.sum(diagonal, axis=1, keepdims=True)))
        scale[:, panel * wide : (panel + 1) * wide] = lax.rsqrt(sums * (1.0 / total_rows))
    for panel in range(panels):
        core, side = panel % 2, panel // 2
        own = slice(panel * wide, (panel + 1) * wide)
        work[own, own] = gram_ref[panel, :wide, :] * down[panel] * along[panel]
        first = 2 * side
        part = slice(core * short, (core + 1) * short)
        low = (first + 1) * wide + core * short
        work[low : low + short, first * wide : (first + 1) * wide] = (
            gram_ref[panel, wide : wide + short, :] * down[first + 1][part, :] * along[first]
        )
        other = 2 + side
        work[other * wide : (other + 1) * wide, core * wide : (core + 1) * wide] = (
            gram_ref[panel, wide + short :, :] * down[other] * along[core]
        )

    def span(c):
        return slice(c * size, (c + 1) * size)

    done = factor_block(work[span(0), span(0)])
    for c in range(count):
        own = span(c)
        stop = ((c * size) // wide + 1) * wide
        if stop > (c + 1) * size:
            inverse[own, (c + 1) * size : stop] = jnp.zeros((size, stop - (c + 1) * size), jnp.float32)
        lower = halves(done)
        inverse[own, own] = done
        if c + 1 < count:
            below = slice((c + 1) * size, full)
            column = triple(halves(work[below, own]), lower, TURNED)
            pieces = halves(column)
            top = (pieces[0][:size], pieces[1][:size])
            following = work[span(c + 1), span(c + 1)] - triple(top, top, TURNED)
        if c > 0:
            known = triple(lower, halves(work[own, : c * size]), PLAIN)
            inverse[own, : c * size] = known
        if c + 1 < count:
            done = factor_block(following)
            work[below, own] = -triple(pieces, lower, PLAIN)
            if c > 0:
                work[below, : c * size] -= triple(pieces, halves(known), PLAIN)
            for j in range(c + 1, count):
                first = max(j, c + 2)
                if first == count:
                    continue
                rows = slice((first - c - 1) * size, (count - c - 1) * size)
                cols = slice((j - c - 1) * size, (j - c) * size)
                work[first * size :, span(j)] -= triple(
                    (pieces[0][rows], pieces[1][rows]), (pieces[0][cols], pieces[1][cols]), TURNED
                )
    mine = pl.ds(pl.multiple_of(lax.axis_index("vecs") * wide, wide), wide)
    high, low = halves(inverse[mine, :] * scale[...])
    out_ref[0] = high
    out_ref[1] = low


def inverse_rows(gram, total_rows):
    panels, _, wide = gram.shape
    full = panels * wide
    size = 128
    return pl.pallas_call(
        functools.partial(inverse_kernel, size, total_rows),
        out_shape=jax.ShapeDtypeStruct((2, wide, full), jnp.bfloat16),
        in_specs=[pl.BlockSpec(memory_space=pltpu.VMEM)],
        out_specs=pl.BlockSpec(memory_space=pltpu.VMEM),
        scratch_shapes=[
            pltpu.VMEM((full, full), jnp.float32),
            pltpu.VMEM((full, full), jnp.float32),
            pltpu.VMEM((1, full), jnp.float32),
        ],
        compiler_params=pltpu.CompilerParams(vmem_limit_bytes=VMEM_LIMIT),
        cost_estimate=pl.CostEstimate(
            flops=4 * full * full * full, bytes_accessed=8 * full * full, transcendentals=full
        ),
    )(gram)


def apply_kernel(block_ref, inverse_ref, out_ref):
    panels, _, wide = block_ref.shape
    mine = lax.axis_index("vecs")
    for panel in range(panels):

        def term():
            cols = slice(panel * wide, (panel + 1) * wide)
            left = block_ref[panel]
            return sum(
                lax.dot_general(
                    left, inverse_ref[half, :, cols], TURNED, preferred_element_type=jnp.float32
                )
                for half in range(2)
            )

        if panel == 0:
            out_ref[...] = term()
        else:

            @pl.when(panel <= mine)
            def _():
                out_ref[...] += term()


def apply_factor(block, inverse):
    panels, rows, wide = block.shape
    tile = rows // 8
    return pl.pallas_call(
        apply_kernel,
        grid=(rows // tile,),
        out_shape=jax.ShapeDtypeStruct((rows, wide), jnp.float32),
        in_specs=[
            pl.BlockSpec((panels, tile, wide), lambda i: (0, i, 0)),
            pl.BlockSpec(inverse.shape, lambda i: (0, 0, 0)),
        ],
        out_specs=pl.BlockSpec((tile, wide), lambda i: (i, 0)),
        compiler_params=pltpu.CompilerParams(vmem_limit_bytes=VMEM_LIMIT),
        cost_estimate=pl.CostEstimate(
            flops=4 * rows * panels * wide * wide,
            bytes_accessed=2 * panels * rows * wide + 4 * rows * wide,
            transcendentals=0,
        ),
    )(block, inverse)


def shards(vectors, blocks, columns):
    total_rows = vectors.shape[0] * lax.axis_size("rows")
    final = filtered_block(vectors, blocks, columns)
    gram, whole_block = gram_sum(final)
    return apply_factor(whole_block, inverse_rows(gram, total_rows))


def solution(mesh):
    in_specs = (P("rows", "vecs"), P("rows", None, None, None), P("rows", None))
    out_specs = P("rows", "vecs")
    return jax.shard_map(shards, mesh=mesh, in_specs=in_specs, out_specs=out_specs, check_vma=False)
```

```python
import functools

import jax
import jax.numpy as jnp
from jax import lax
from jax.experimental import pallas as pl
from jax.experimental.pallas import tpu as pltpu
from jax.sharding import PartitionSpec as P

DEGREE = 4

filter_center = 0.25
filter_radius = 1.25

VMEM_LIMIT = 56 * 1024 * 1024


def filter_kernel(
    place_ref, vectors_ref, blocks_ref, out_ref,
    first_win, even_win, odd_win, tops, bottoms, even, odd, held,
    in_sem, send_sem, recv_sem, copy_sem,
):
    me, count = lax.axis_index("rows"), lax.axis_size("rows")
    block_rows, nnz = blocks_ref.shape[:2]
    reach = block_rows // 4
    span, part = 2 * reach, reach // 2
    windows = [first_win, odd_win, even_win, odd_win, even_win]
    states = [None, even, odd, even, None]
    above, below = me < count - 1, me > 0

    @pl.when(below)
    def _():
        pl.semaphore_signal(pltpu.get_barrier_semaphore(), 1, device_id={"rows": me - 1})

    @pl.when(above)
    def _():
        pl.semaphore_signal(pltpu.get_barrier_semaphore(), 1, device_id={"rows": me + 1})

    pieces = [
        (vectors_ref, first_win),
        (vectors_ref.at[:span], tops[0][0].at[part:]),
        (vectors_ref.at[: reach + part], tops[0][1].at[reach:]),
        (vectors_ref.at[span:], bottoms[0][0].at[:span]),
        (vectors_ref.at[span + part :], bottoms[0][1].at[: reach + part]),
        (blocks_ref, held),
    ]
    fetches = [pltpu.make_async_copy(*pair, in_sem.at[n]) for n, pair in enumerate(pieces)]
    for fetch in fetches:
        fetch.start()
    inside = jnp.logical_and(above, below)

    @pl.when(inside)
    def _():
        pl.semaphore_wait(pltpu.get_barrier_semaphore(), 2)

    @pl.when(jnp.logical_not(inside))
    def _():
        pl.semaphore_wait(pltpu.get_barrier_semaphore(), 1)

    def to_lower(step, far):
        source = vectors_ref if step == 0 else windows[step]
        return pltpu.make_async_remote_copy(
            src_ref=source.at[far * part : (far + 1) * part],
            dst_ref=bottoms[step % 2][far].at[span:],
            send_sem=send_sem.at[0, far, step % 2], recv_sem=recv_sem.at[0, far, step % 2],
            device_id={"rows": me - 1},
        )

    def to_upper(step, far):
        source = vectors_ref if step == 0 else windows[step]
        first = block_rows - (far + 1) * part
        return pltpu.make_async_remote_copy(
            src_ref=source.at[first : first + part], dst_ref=tops[step % 2][far].at[:part],
            send_sem=send_sem.at[1, far, step % 2], recv_sem=recv_sem.at[1, far, step % 2],
            device_id={"rows": me + 1},
        )

    def join_bottom(step):
        near, far = bottoms[step % 2]
        return pltpu.make_async_copy(near.at[span:], far.at[reach + part : span], copy_sem.at[0])

    def join_top(step):
        near, far = tops[step % 2]
        return pltpu.make_async_copy(near.at[:part], far.at[part:reach], copy_sem.at[1])

    def compute(step, start, rows, window):
        slot = (step + 1) % 2
        for row in range(start, start + rows):
            left = jnp.concatenate([held[row, j] for j in range(nnz)], axis=1)
            right = jnp.concatenate([window[place_ref[row, j]] for j in range(nnz)], axis=0)
            acc = jnp.dot(left, right, preferred_element_type=jnp.float32)
            cur = first_win[row].astype(jnp.float32) if step == 0 else states[step][row]
            new = (acc - filter_center * cur) * (1.0 / filter_radius)
            if step == 1:
                new = 2.0 * new - first_win[row].astype(jnp.float32)
            elif step > 1:
                new = 2.0 * new - states[step - 1][row]
            rounded = new.astype(jnp.bfloat16)
            windows[step + 1][row] = rounded
            if step == DEGREE - 1:
                continue
            states[step + 1][row] = new
            if row < span:
                tops[slot][0][row + part] = rounded
            if row < reach + part:
                tops[slot][1][row + reach] = rounded
            if row >= span:
                bottoms[slot][0][row - span] = rounded
            if row >= span + part:
                bottoms[slot][1][row - span - part] = rounded

    @pl.when(below)
    def _():
        to_lower(0, 0).start()

    @pl.when(above)
    def _():
        to_upper(0, 0).start()

    for fetch in fetches:
        fetch.wait()

    for step in range(DEGREE):
        last = step == DEGREE - 1
        compute(step, reach, reach, windows[step])
        compute(step, span, reach, windows[step])

        @pl.when(below)
        def _():
            to_lower(step, 0).wait_send()
            to_lower(step, 1).start()

        @pl.when(above)
        def _():
            to_upper(step, 0).wait_send()
            to_upper(step, 1).start()
            to_lower(step, 0).wait_recv()
            join_bottom(step).start()

        compute(step, 3 * reach, part, bottoms[step % 2][0])

        @pl.when(below)
        def _():
            to_upper(step, 0).wait_recv()
            join_top(step).start()

        compute(step, part, part, tops[step % 2][0])

        @pl.when(above)
        def _():
            join_bottom(step).wait()
            to_lower(step, 1).wait_recv()

        compute(step, 3 * reach + part, part, bottoms[step % 2][1])

        @pl.when(above)
        def _():
            if not last:
                to_upper(step + 1, 0).start()

        @pl.when(below)
        def _():
            join_top(step).wait()
            to_upper(step, 1).wait_recv()

        compute(step, 0, part, tops[step % 2][1])

        @pl.when(below)
        def _():
            if not last:
                to_lower(step + 1, 0).start()
            to_lower(step, 1).wait_send()

        @pl.when(above)
        def _():
            to_upper(step, 1).wait_send()

    done = pltpu.make_async_copy(windows[DEGREE], out_ref, in_sem.at[0])
    done.start()
    done.wait()


def filtered_block(vectors, blocks, columns):
    rows, width = vectors.shape
    block_rows, nnz, size_b = blocks.shape[:3]
    reach = block_rows // 4
    part = reach // 2
    row = lax.broadcasted_iota(jnp.int32, columns.shape, 0)
    shift = jnp.zeros_like(columns)
    for start, amount in (
        (0, reach), (part, part), (reach, 0), (3 * reach, -2 * reach), (3 * reach + part, -2 * reach - part),
    ):
        shift = jnp.where(row >= start, amount, shift)
    place = columns - lax.axis_index("rows") * block_rows + shift
    window = pltpu.VMEM((block_rows, size_b, width), jnp.bfloat16)
    side = pltpu.VMEM((2 * reach + part, size_b, width), jnp.bfloat16)
    state = pltpu.VMEM((block_rows, size_b, width), jnp.float32)
    anywhere = pl.BlockSpec(memory_space=pl.ANY)
    dma = pltpu.SemaphoreType.DMA

    def kernel(place_ref, vectors_ref, blocks_ref, out_ref, *refs):
        first, even_win, odd_win, *refs = refs
        tops = ((refs[0], refs[1]), (refs[2], refs[3]))
        bottoms = ((refs[4], refs[5]), (refs[6], refs[7]))
        filter_kernel(
            place_ref, vectors_ref, blocks_ref, out_ref, first, even_win, odd_win, tops, bottoms, *refs[8:]
        )

    out = pl.pallas_call(
        kernel,
        out_shape=jax.ShapeDtypeStruct((block_rows, size_b, width), jnp.bfloat16),
        in_specs=[pl.BlockSpec(memory_space=pltpu.SMEM), anywhere, anywhere],
        out_specs=anywhere,
        scratch_shapes=[window] * 3 + [side] * 8 + [state] * 2 + [
            pltpu.VMEM(blocks.shape, jnp.bfloat16),
            dma((6,)), dma((2, 2, 2)), dma((2, 2, 2)), dma((2,)),
        ],
        compiler_params=pltpu.CompilerParams(
            vmem_limit_bytes=VMEM_LIMIT, collective_id=0, has_side_effects=True
        ),
    )(place, vectors.reshape(block_rows, size_b, width), blocks)
    return out.reshape(rows, width)


def factor_block(block):
    size = block.shape[0]
    tiles = [block[8 * t : 8 * (t + 1), :] for t in range(size // 8)]
    lane = lax.broadcasted_iota(jnp.int32, (8, size), 1)
    sub = lax.broadcasted_iota(jnp.int32, (8, size), 0)

    def spread(array):
        return jnp.broadcast_to(array, (8, size))

    for first in range(size // 8):
        j = 8 * first
        each = range(8)
        at_any = jnp.logical_and(lane >= j, lane < j + 8)
        head = tiles[first]
        cols = [spread(head[:, j + a : j + a + 1]) for a in each]
        p = [[spread(cols[a][b : b + 1, :]) for a in range(b + 1)] for b in each]
        rows = [jnp.where(at_any, 0.0, spread(head[a : a + 1, :])) for a in each]
        rows = [jnp.where(lane == j + a, 1.0, rows[a]) for a in each]
        pairs, ready = [], []
        for a in range(0, 8, 2):
            b = a + 1
            det = p[a][a] * p[b][b] - p[b][a] * p[b][a]
            inv = 1.0 / det
            e_aa, e_ab, e_bb = p[b][b] * inv, p[b][a] * inv, p[a][a] * inv
            over = 1.0 / p[a][a]
            ready.append(rows[a] * lax.rsqrt(p[a][a]))
            ready.append((rows[b] - (p[b][a] * over) * rows[a]) * lax.rsqrt(det * over))
            mult = {}
            for c in range(b + 1, 8):
                mult[c, 0] = p[c][a] * e_aa - p[c][b] * e_ab
                mult[c, 1] = p[c][b] * e_bb - p[c][a] * e_ab
            for c in range(b + 1, 8):
                for d in range(b + 1, c + 1):
                    p[c][d] = p[c][d] - (mult[c, 0] * p[d][a] + mult[c, 1] * p[d][b])
            pairs.append((e_aa, e_ab, e_bb, mult, rows[a], rows[b]))
            for c in range(b + 1, 8):
                rows[c] = rows[c] - (mult[c, 0] * rows[a] + mult[c, 1] * rows[b])
        use = [None] * 8
        for number in reversed(range(4)):
            a, b = 2 * number, 2 * number + 1
            e_aa, e_ab, e_bb, mult, row_a, row_b = pairs[number]
            use[a] = e_aa * row_a - e_ab * row_b
            use[b] = e_bb * row_b - e_ab * row_a
            for c in range(b + 1, 8):
                use[a] = use[a] - mult[c, 0] * use[c]
                use[b] = use[b] - mult[c, 1] * use[c]
        for t in range(first + 1, size // 8):
            tile = tiles[t]
            cols = [spread(tile[:, j + a : j + a + 1]) for a in each]
            terms = [cols[a] * use[a] for a in each]
            while len(terms) > 1:
                terms = [x + y for x, y in zip(terms[::2], terms[1::2])]
            tiles[t] = jnp.where(at_any, 0.0, tile) - terms[0]
        top = ready[0]
        for a in range(1, 8):
            top = jnp.where(sub == a, ready[a], top)
        tiles[first] = top
    done = jnp.concatenate(tiles, axis=0)
    down = lax.broadcasted_iota(jnp.int32, (size, size), 0)
    across = lax.broadcasted_iota(jnp.int32, (size, size), 1)
    return jnp.where(across <= down, done, 0.0)


def halves(array):
    high = array.astype(jnp.bfloat16)
    return high, (array - high.astype(jnp.float32)).astype(jnp.bfloat16)


PLAIN = (((1,), (0,)), ((), ()))
TURNED = (((1,), (1,)), ((), ()))


def triple(left, right, dims):
    def one(a, b):
        return lax.dot_general(a, b, dims, preferred_element_type=jnp.float32)

    return one(left[0], right[0]) + (one(left[0], right[1]) + one(left[1], right[0]))


def gram_stages(rows, devices):
    stages, bit, held = [], 1, rows
    while bit < devices:
        halve = held % 16 == 0
        stages.append((bit, halve))
        held, bit = held // 2 if halve else held, bit * 2
    return stages


def flipped(index, bit):
    return index + bit - 2 * bit * lax.rem(index // bit, 2)


def gram_kernel(
    stages, parts, final_ref, out_ref, block_ref, block, cross, total, full, landing, cross_in,
    local_sem, side_sem, x_sem, pass_sem, rest_sem, on_sem, stage_sem, all_sem,
):
    me, panel = lax.axis_index("rows"), lax.axis_index("vecs")
    core, side = lax.rem(panel, 2), panel // 2
    _, rows, wide = block.shape
    half, short = rows // 2, wide // 2
    chunk = half // parts
    near, over = flipped(panel, 1), flipped(panel, 2)
    beyond = flipped(over, 1)
    contract = (((0,), (0,)), ((), ()))

    peers = [{"vecs": near}, {"vecs": over}] + [{"rows": flipped(me, bit)} for bit, _ in stages]
    barrier = pltpu.get_barrier_semaphore()
    for peer in peers:
        pl.semaphore_signal(barrier, 1, device_id=peer)
    fetch = pltpu.make_async_copy(final_ref, block.at[panel], local_sem.at[0])
    fetch.start()
    pl.semaphore_wait(barrier, len(peers))
    fetch.wait()

    def send(which, start, size, sems, number, peer):
        piece = block.at[which, pl.ds(pl.multiple_of(start, chunk), size)]
        return pltpu.make_async_remote_copy(
            src_ref=piece, dst_ref=piece, send_sem=sems.at[0, number],
            recv_sem=sems.at[1, number], device_id={"vecs": peer},
        )

    def at(start):
        return pl.ds(pl.multiple_of(start, chunk), chunk)

    to_over = [send(panel, (1 - side) * half + n * chunk, chunk, x_sem, n, over) for n in range(parts)]
    passed = [send(over, side * half + n * chunk, chunk, pass_sem, n, near) for n in range(parts)]
    to_near = [send(panel, n * half, half, side_sem, n, near) for n in range(2)]
    for copy in to_over + to_near:
        copy.start()
    keep_own = pltpu.make_async_copy(block.at[panel], block_ref.at[panel], local_sem.at[0])
    keep_own.start()

    def product(left, right):
        return lax.dot_general(left, right, contract, preferred_element_type=jnp.float32)

    total[: wide + short, :] = jnp.zeros((wide + short, wide), jnp.float32)
    cross[...] = jnp.zeros_like(cross)

    @pl.loop(0, rows // chunk)
    def _(index):
        own = block[panel, at(index * chunk), :]
        total[:wide, :] += product(own, own)

    for copy in to_near:
        copy.wait()
    keep_near = pltpu.make_async_copy(block.at[near], block_ref.at[near], local_sem.at[1])
    keep_near.start()

    @pl.loop(0, rows // chunk)
    def _(index):
        own = block[panel, at(index * chunk), :]
        beside = block[near, at(index * chunk), :]

        @pl.when(core == 0)
        def _():
            total[wide : wide + short, :] += product(beside[:, :short], own)

        @pl.when(core == 1)
        def _():
            total[wide : wide + short, :] += product(own[:, short:], beside)

    for part in range(parts):
        to_over[part].wait()
        passed[part].start()
        here = at(side * half + part * chunk)
        own = block[panel, here, :]
        there = block[over, here, :]

        @pl.when(side == 0)
        def _():
            cross[core] += product(there, own)

        @pl.when(side == 1)
        def _():
            cross[core] += product(own, there)
            cross[1 - core] += product(block[near, here, :], there)

    for part in range(parts):
        passed[part].wait()

        @pl.when(side == 0)
        def _():
            here = at(part * chunk)
            cross[1 - core] += product(block[beyond, here, :], block[panel, here, :])

    swap = pltpu.make_async_remote_copy(
        src_ref=cross.at[1 - side], dst_ref=cross_in,
        send_sem=local_sem.at[2], recv_sem=local_sem.at[3], device_id={"vecs": over},
    )
    swap.start()
    swap.wait()
    total[wide + short :, :] = cross[side] + cross_in[...]

    rest = [send(panel, n * half // 2, half // 2, rest_sem, n, over) for n in range(2)]
    onward = [send(over, n * half // 2, half // 2, on_sem, n, near) for n in range(2)]

    @pl.when(side == 0)
    def _():
        for copy in rest:
            copy.start()

    start, held, taken = 0, total.shape[0], 0
    ranges = []
    for number, (bit, halve) in enumerate(stages):
        size = held // 2 if halve else held
        upper = lax.rem(me // bit, 2)
        ranges.append((start, size))
        keep = pl.multiple_of(start + upper * size, 8) if halve else start
        give = pl.multiple_of(start + (1 - upper) * size, 8) if halve else start
        copy = pltpu.make_async_remote_copy(
            src_ref=total.at[pl.ds(give, size)], dst_ref=landing.at[taken : taken + size],
            send_sem=stage_sem.at[0, number], recv_sem=stage_sem.at[1, number],
            device_id={"rows": flipped(me, bit)},
        )
        copy.start()
        copy.wait()
        total[pl.ds(keep, size), :] += landing[taken : taken + size, :]
        start, held, taken = keep, size, taken + size

    full[panel, pl.ds(start, held), :] = total[pl.ds(start, held), :]
    pending = []

    def share(number, first, size):
        def hand(which, kind, peer):
            piece = full.at[which, pl.ds(first, size)]
            return pltpu.make_async_remote_copy(
                src_ref=piece, dst_ref=piece, send_sem=all_sem.at[0, kind, number],
                recv_sem=all_sem.at[1, kind, number], device_id={"vecs": peer},
            )

        copies = [hand(panel, 0, over), hand(panel, 1, near)]
        for copy in copies:
            copy.start()
        pending.append(copies + [hand(over, 2, near)])

    share(0, start, held)
    count = 1
    for number in reversed(range(len(stages))):
        bit, halve = stages[number]
        if not halve:
            continue
        upper = lax.rem(me // bit, 2)
        below, size = ranges[number]
        mine = pl.multiple_of(below + upper * size, 8)
        other = pl.multiple_of(below + (1 - upper) * size, 8)
        piece = full.at[panel, pl.ds(mine, size)]
        copy = pltpu.make_async_remote_copy(
            src_ref=piece, dst_ref=piece, send_sem=stage_sem.at[2, number],
            recv_sem=stage_sem.at[3, number], device_id={"rows": flipped(me, bit)},
        )
        copy.start()
        copy.wait()
        share(count, other, size)
        count += 1

    for first, second, third in pending:
        first.wait()
        third.start()
        second.wait()
    keep_own.wait()
    keep_near.wait()
    keep_over = pltpu.make_async_copy(block.at[over], block_ref.at[over], local_sem.at[0])
    keep_beyond = pltpu.make_async_copy(block.at[beyond], block_ref.at[beyond], local_sem.at[1])

    @pl.when(side == 0)
    def _():
        for copy in rest:
            copy.wait_send()

    @pl.when(side == 1)
    def _():
        for number in range(2):
            rest[number].wait_recv()
            onward[number].start()
        keep_over.start()
        for copy in onward:
            copy.wait()
        keep_beyond.start()

    for _, _, third in pending:
        third.wait()
    done = pltpu.make_async_copy(full, out_ref, local_sem.at[2])
    done.start()

    @pl.when(side == 1)
    def _():
        keep_over.wait()
        keep_beyond.wait()

    done.wait()


def gram_sum(final):
    rows, wide = final.shape
    panels, devices = lax.axis_size("vecs"), lax.axis_size("rows")
    tall = 2 * wide + wide // 2
    stages = gram_stages(tall, devices)
    parts = 4
    dma = pltpu.SemaphoreType.DMA
    steps = len(stages)
    return pl.pallas_call(
        functools.partial(gram_kernel, stages, parts),
        out_shape=[
            jax.ShapeDtypeStruct((panels, tall, wide), jnp.float32),
            jax.ShapeDtypeStruct((panels, rows, wide), jnp.bfloat16),
        ],
        in_specs=[pl.BlockSpec(memory_space=pl.ANY)],
        out_specs=[pl.BlockSpec(memory_space=pl.ANY)] * 2,
        scratch_shapes=[
            pltpu.VMEM((panels, rows, wide), jnp.bfloat16),
            pltpu.VMEM((2, wide, wide), jnp.float32),
            pltpu.VMEM((tall, wide), jnp.float32),
            pltpu.VMEM((panels, tall, wide), jnp.float32),
            pltpu.VMEM((2 * tall, wide), jnp.float32),
            pltpu.VMEM((wide, wide), jnp.float32),
            dma((4,)), dma((2, 2)), dma((2, parts)), dma((2, parts)), dma((2, 2)), dma((2, 2)),
            dma((4, steps)), dma((2, 3, steps + 1)),
        ],
        compiler_params=pltpu.CompilerParams(
            vmem_limit_bytes=VMEM_LIMIT, collective_id=1, has_side_effects=True
        ),
    )(final)


def finish_kernel(
    size, total_rows, gram_ref, block_ref, out_ref, work, inverse, scale, block, result, in_sem, out_sem
):
    full = inverse.shape[0]
    mine = lax.axis_index("vecs")

    def fetch(panel):
        return pltpu.make_async_copy(block_ref.at[panel], block.at[panel], in_sem.at[panel])

    for panel in range(gram_ref.shape[0]):

        @pl.when(panel <= mine)
        def _():
            fetch(panel).start()

    panels, _, wide = gram_ref.shape
    count, short = full // size, wide // 2
    same = lax.broadcasted_iota(jnp.int32, (wide, wide), 0) == lax.broadcasted_iota(
        jnp.int32, (wide, wide), 1
    )
    down, along = [], []
    for panel in range(panels):
        diagonal = jnp.where(same, gram_ref[panel, :wide, :], 0.0)
        sums = jnp.sum(diagonal, axis=0, keepdims=True)
        along.append(lax.rsqrt(sums))
        down.append(lax.rsqrt(jnp.sum(diagonal, axis=1, keepdims=True)))
        scale[:, panel * wide : (panel + 1) * wide] = lax.rsqrt(sums * (1.0 / total_rows))
    for panel in range(panels):
        core, side = panel % 2, panel // 2
        own = slice(panel * wide, (panel + 1) * wide)
        work[own, own] = gram_ref[panel, :wide, :] * down[panel] * along[panel]
        first = 2 * side
        part = slice(core * short, (core + 1) * short)
        low = (first + 1) * wide + core * short
        work[low : low + short, first * wide : (first + 1) * wide] = (
            gram_ref[panel, wide : wide + short, :] * down[first + 1][part, :] * along[first]
        )
        other = 2 + side
        work[other * wide : (other + 1) * wide, core * wide : (core + 1) * wide] = (
            gram_ref[panel, wide + short :, :] * down[other] * along[core]
        )

    def span(c):
        return slice(c * size, (c + 1) * size)

    done = factor_block(work[span(0), span(0)])
    for c in range(count):
        own = span(c)
        stop = ((c * size) // wide + 1) * wide
        if stop > (c + 1) * size:
            inverse[own, (c + 1) * size : stop] = jnp.zeros((size, stop - (c + 1) * size), jnp.float32)
        lower = halves(done)
        inverse[own, own] = done
        if c + 1 < count:
            below = slice((c + 1) * size, full)
            column = triple(halves(work[below, own]), lower, TURNED)
            pieces = halves(column)
            top = (pieces[0][:size], pieces[1][:size])
            following = work[span(c + 1), span(c + 1)] - triple(top, top, TURNED)
        if c > 0:
            known = triple(lower, halves(work[own, : c * size]), PLAIN)
            inverse[own, : c * size] = known
        if c + 1 < count:
            done = factor_block(following)
            work[below, own] = -triple(pieces, lower, PLAIN)
            if c > 0:
                work[below, : c * size] -= triple(pieces, halves(known), PLAIN)
            for j in range(c + 1, count):
                first = max(j, c + 2)
                if first == count:
                    continue
                rows = slice((first - c - 1) * size, (count - c - 1) * size)
                cols = slice((j - c - 1) * size, (j - c) * size)
                work[first * size :, span(j)] -= triple(
                    (pieces[0][rows], pieces[1][rows]), (pieces[0][cols], pieces[1][cols]), TURNED
                )
    high, low = halves(inverse[pl.ds(pl.multiple_of(mine * wide, wide), wide), :] * scale[...])
    tiles = out_sem.shape[0]
    tile = block.shape[1] // tiles

    def store(index):
        rows = pl.ds(pl.multiple_of(index * tile, tile), tile)
        return pltpu.make_async_copy(result.at[rows], out_ref.at[rows], out_sem.at[index])

    for number in range(1, panels + 1):

        @pl.when(mine == number - 1)
        def _():
            for panel in range(number):
                fetch(panel).wait()
            deep = number * wide
            right = jnp.concatenate([high[:, :deep], low[:, :deep]], axis=1)

            @pl.loop(0, tiles)
            def _(index):
                rows = pl.ds(pl.multiple_of(index * tile, tile), tile)
                left = jnp.concatenate([block[panel, rows, :] for panel in range(number)] * 2, axis=1)
                result[rows, :] = lax.dot_general(
                    left, right, TURNED, preferred_element_type=jnp.float32
                )
                store(index).start()

    for index in range(tiles):
        store(index).wait()


def finish(gram, block, total_rows):
    panels, rows, wide = block.shape
    full = panels * wide
    size = 128
    tiles = 4
    anywhere = pl.BlockSpec(memory_space=pl.ANY)
    return pl.pallas_call(
        functools.partial(finish_kernel, size, total_rows),
        out_shape=jax.ShapeDtypeStruct((rows, wide), jnp.float32),
        in_specs=[pl.BlockSpec(memory_space=pltpu.VMEM), anywhere],
        out_specs=anywhere,
        scratch_shapes=[
            pltpu.VMEM((full, full), jnp.float32),
            pltpu.VMEM((full, full), jnp.float32),
            pltpu.VMEM((1, full), jnp.float32),
            pltpu.VMEM((panels, rows, wide), jnp.bfloat16),
            pltpu.VMEM((rows, wide), jnp.float32),
            pltpu.SemaphoreType.DMA((panels,)),
            pltpu.SemaphoreType.DMA((tiles,)),
        ],
        compiler_params=pltpu.CompilerParams(vmem_limit_bytes=VMEM_LIMIT),
    )(gram, block)


def shards(vectors, blocks, columns):
    total_rows = vectors.shape[0] * lax.axis_size("rows")
    final = filtered_block(vectors, blocks, columns)
    gram, whole_block = gram_sum(final)
    return finish(gram, whole_block, total_rows)


def solution(mesh):
    in_specs = (P("rows", "vecs"), P("rows", None, None, None), P("rows", None))
    out_specs = P("rows", "vecs")
    return jax.shard_map(shards, mesh=mesh, in_specs=in_specs, out_specs=out_specs, check_vma=False)
```

```python
import functools

import jax
import jax.numpy as jnp
from jax import lax
from jax.experimental import pallas as pl
from jax.experimental.pallas import tpu as pltpu
from jax.sharding import PartitionSpec as P

DEGREE = 4

filter_center = 0.25
filter_radius = 1.25

VMEM_LIMIT = 56 * 1024 * 1024


def factor_block(block):
    size = block.shape[0]
    tiles = [block[8 * t : 8 * (t + 1), :] for t in range(size // 8)]
    lane = lax.broadcasted_iota(jnp.int32, (8, size), 1)
    sub = lax.broadcasted_iota(jnp.int32, (8, size), 0)

    def spread(array):
        return jnp.broadcast_to(array, (8, size))

    for first in range(size // 8):
        j = 8 * first
        each = range(8)
        at_any = jnp.logical_and(lane >= j, lane < j + 8)
        head = tiles[first]
        cols = [spread(head[:, j + a : j + a + 1]) for a in each]
        p = [[spread(cols[a][b : b + 1, :]) for a in range(b + 1)] for b in each]
        rows = [jnp.where(at_any, 0.0, spread(head[a : a + 1, :])) for a in each]
        rows = [jnp.where(lane == j + a, 1.0, rows[a]) for a in each]
        pairs, ready = [], []
        for a in range(0, 8, 2):
            b = a + 1
            det = p[a][a] * p[b][b] - p[b][a] * p[b][a]
            inv = 1.0 / det
            e_aa, e_ab, e_bb = p[b][b] * inv, p[b][a] * inv, p[a][a] * inv
            over = 1.0 / p[a][a]
            ready.append(rows[a] * lax.rsqrt(p[a][a]))
            ready.append((rows[b] - (p[b][a] * over) * rows[a]) * lax.rsqrt(det * over))
            mult = {}
            for c in range(b + 1, 8):
                mult[c, 0] = p[c][a] * e_aa - p[c][b] * e_ab
                mult[c, 1] = p[c][b] * e_bb - p[c][a] * e_ab
            for c in range(b + 1, 8):
                for d in range(b + 1, c + 1):
                    p[c][d] = p[c][d] - (mult[c, 0] * p[d][a] + mult[c, 1] * p[d][b])
            pairs.append((e_aa, e_ab, e_bb, mult, rows[a], rows[b]))
            for c in range(b + 1, 8):
                rows[c] = rows[c] - (mult[c, 0] * rows[a] + mult[c, 1] * rows[b])
        use = [None] * 8
        for number in reversed(range(4)):
            a, b = 2 * number, 2 * number + 1
            e_aa, e_ab, e_bb, mult, row_a, row_b = pairs[number]
            use[a] = e_aa * row_a - e_ab * row_b
            use[b] = e_bb * row_b - e_ab * row_a
            for c in range(b + 1, 8):
                use[a] = use[a] - mult[c, 0] * use[c]
                use[b] = use[b] - mult[c, 1] * use[c]
        for t in range(first + 1, size // 8):
            tile = tiles[t]
            cols = [spread(tile[:, j + a : j + a + 1]) for a in each]
            terms = [cols[a] * use[a] for a in each]
            while len(terms) > 1:
                terms = [x + y for x, y in zip(terms[::2], terms[1::2])]
            tiles[t] = jnp.where(at_any, 0.0, tile) - terms[0]
        top = ready[0]
        for a in range(1, 8):
            top = jnp.where(sub == a, ready[a], top)
        tiles[first] = top
    done = jnp.concatenate(tiles, axis=0)
    down = lax.broadcasted_iota(jnp.int32, (size, size), 0)
    across = lax.broadcasted_iota(jnp.int32, (size, size), 1)
    return jnp.where(across <= down, done, 0.0)


def halves(array):
    high = array.astype(jnp.bfloat16)
    return high, (array - high.astype(jnp.float32)).astype(jnp.bfloat16)


PLAIN = (((1,), (0,)), ((), ()))
TURNED = (((1,), (1,)), ((), ()))


def triple(left, right, dims):
    def one(a, b):
        return lax.dot_general(a, b, dims, preferred_element_type=jnp.float32)

    return one(left[0], right[0]) + (one(left[0], right[1]) + one(left[1], right[0]))


def gram_stages(rows, devices):
    stages, bit, held = [], 1, rows
    while bit < devices:
        halve = held % 16 == 0
        stages.append((bit, halve))
        held, bit = held // 2 if halve else held, bit * 2
    return stages


def flipped(index, bit):
    return index + bit - 2 * bit * lax.rem(index // bit, 2)


class Reduction:
    def __init__(self, stages, me, panel, total, landing, full, base, stage_sem, all_sem):
        self.me, self.panel, self.total, self.landing, self.full = me, panel, total, landing, full
        self.base, self.stage_sem, self.all_sem = base, stage_sem, all_sem
        self.near, self.over, self.side = flipped(panel, 1), flipped(panel, 2), panel // 2
        self.steps, self.shared = [], []
        start, held, taken = 0, total.shape[0], 0
        for bit, halve in stages:
            size = held // 2 if halve else held
            upper = lax.rem(me // bit, 2)
            keep = pl.multiple_of(start + upper * size, 8) if halve else start
            give = pl.multiple_of(start + (1 - upper) * size, 8) if halve else start
            self.steps.append((bit, size, keep, give, taken))
            start, held, taken = keep, size, taken + size
        self.start, self.held = start, held
        self.gathers = [n for n in reversed(range(len(stages))) if stages[n][1]]

    def reduce_copy(self, number):
        bit, size, _, give, taken = self.steps[number]
        return pltpu.make_async_remote_copy(
            src_ref=self.total.at[pl.ds(give, size)], dst_ref=self.landing.at[taken : taken + size],
            send_sem=self.stage_sem.at[0, number], recv_sem=self.stage_sem.at[1, number],
            device_id={"rows": flipped(self.me, bit)},
        )

    def reduce_start(self, number):
        if number < len(self.steps):
            self.reduce_copy(number).start()

    def reduce_finish(self, number):
        if number < len(self.steps):
            _, size, keep, _, taken = self.steps[number]
            self.reduce_copy(number).wait()
            self.total[pl.ds(keep, size), :] += self.landing[taken : taken + size, :]

    def piece(self, which, first, size):
        return self.full.at[which, pl.ds(pl.multiple_of(self.base + first, 8), size)]

    def hand(self, which, kind, number, first, size, peer):
        piece = self.piece(which, first, size)
        return pltpu.make_async_remote_copy(
            src_ref=piece, dst_ref=piece, send_sem=self.all_sem.at[0, kind, number],
            recv_sem=self.all_sem.at[1, kind, number], device_id={"vecs": peer},
        )

    def share(self, first, size):
        number = len(self.shared)
        across = self.hand(self.panel, 0, number, first, size, self.over)
        beside = self.hand(self.panel, 1, number, first, size, self.near)

        @pl.when(self.side == 0)
        def _():
            across.start()

        beside.start()
        self.shared.append((across, beside, self.hand(self.over, 2, number, first, size, self.near)))

    def publish(self):
        rows = pl.ds(pl.multiple_of(self.base + self.start, 8), self.held)
        self.full[self.panel, rows, :] = self.total[pl.ds(self.start, self.held), :]
        self.share(self.start, self.held)

    def gather_copy(self, index):
        number = self.gathers[index]
        bit, size, keep, _, _ = self.steps[number]
        piece = self.piece(self.panel, keep, size)
        return pltpu.make_async_remote_copy(
            src_ref=piece, dst_ref=piece, send_sem=self.stage_sem.at[2, number],
            recv_sem=self.stage_sem.at[3, number], device_id={"rows": flipped(self.me, bit)},
        )

    def gather_start(self, index):
        if index < len(self.gathers):
            self.gather_copy(index).start()

    def gather_finish(self, index):
        if index < len(self.gathers):
            self.gather_copy(index).wait()
            _, size, _, give, _ = self.steps[self.gathers[index]]
            self.share(give, size)

    def settle(self):
        for across, beside, third in self.shared:

            @pl.when(self.side == 1)
            def _():
                across.wait_recv()
                third.start()

            @pl.when(self.side == 0)
            def _():
                across.wait_send()

            beside.wait()

    def close(self):
        @pl.when(self.side == 1)
        def _():
            for _, _, third in self.shared:
                third.wait()


def filter_kernel(
    near_stages, cross_stages, place_ref, vectors_ref, blocks_ref, sums_ref, block_ref,
    first_win, even_win, odd_win, tops, bottoms, even, odd, held,
    block, cross, near_total, cross_total, full, near_landing, cross_landing, cross_in,
    in_sem, send_sem, recv_sem, copy_sem, keep_sem, swap_sem, side_sem, x_sem, pass_sem, rest_sem, on_sem,
    near_stage_sem, near_all_sem, cross_stage_sem, cross_all_sem,
):
    me, count = lax.axis_index("rows"), lax.axis_size("rows")
    panel = lax.axis_index("vecs")
    core, side = lax.rem(panel, 2), panel // 2
    near, over = flipped(panel, 1), flipped(panel, 2)
    beyond = flipped(over, 1)
    block_rows, nnz = blocks_ref.shape[:2]
    wide = block.shape[3]
    short = wide // 2
    reach = block_rows // 4
    span, part = 2 * reach, reach // 2
    windows = [first_win, odd_win, even_win, odd_win]
    states = [None, even, odd, even]
    above, below = me < count - 1, me > 0

    peers = [{"vecs": near}, {"vecs": over}] + [{"rows": flipped(me, bit)} for bit, _ in near_stages]
    inside = jnp.logical_and(above, below)
    for peer in peers:
        pl.semaphore_signal(pltpu.get_barrier_semaphore(), 1, device_id=peer)

    @pl.when(inside)
    def _():
        other = me - 1 + 2 * lax.rem(me, 2)
        pl.semaphore_signal(pltpu.get_barrier_semaphore(), 1, device_id={"rows": other})

    pieces = [
        (vectors_ref, first_win),
        (vectors_ref.at[:span], tops[0][0].at[part:]),
        (vectors_ref.at[: reach + part], tops[0][1].at[reach:]),
        (vectors_ref.at[span:], bottoms[0][0].at[:span]),
        (vectors_ref.at[span + part :], bottoms[0][1].at[: reach + part]),
        (blocks_ref, held),
    ]
    fetches = [pltpu.make_async_copy(*pair, in_sem.at[n]) for n, pair in enumerate(pieces)]
    for fetch in fetches:
        fetch.start()

    @pl.when(inside)
    def _():
        pl.semaphore_wait(pltpu.get_barrier_semaphore(), len(peers) + 1)

    @pl.when(jnp.logical_not(inside))
    def _():
        pl.semaphore_wait(pltpu.get_barrier_semaphore(), len(peers))

    def to_lower(step, far):
        source = vectors_ref if step == 0 else windows[step]
        return pltpu.make_async_remote_copy(
            src_ref=source.at[far * part : (far + 1) * part],
            dst_ref=bottoms[step % 2][far].at[span:],
            send_sem=send_sem.at[0, far, step % 2], recv_sem=recv_sem.at[0, far, step % 2],
            device_id={"rows": me - 1},
        )

    def to_upper(step, far):
        source = vectors_ref if step == 0 else windows[step]
        first = block_rows - (far + 1) * part
        return pltpu.make_async_remote_copy(
            src_ref=source.at[first : first + part], dst_ref=tops[step % 2][far].at[:part],
            send_sem=send_sem.at[1, far, step % 2], recv_sem=recv_sem.at[1, far, step % 2],
            device_id={"rows": me + 1},
        )

    def join_bottom(step):
        close, far = bottoms[step % 2]
        return pltpu.make_async_copy(close.at[span:], far.at[reach + part : span], copy_sem.at[0])

    def join_top(step):
        close, far = tops[step % 2]
        return pltpu.make_async_copy(close.at[:part], far.at[part:reach], copy_sem.at[1])

    def compute(step, start, rows, window):
        slot = (step + 1) % 2
        for row in range(start, start + rows):
            left = jnp.concatenate([held[row, j] for j in range(nnz)], axis=1)
            right = jnp.concatenate([window[place_ref[row, j]] for j in range(nnz)], axis=0)
            acc = jnp.dot(left, right, preferred_element_type=jnp.float32)
            cur = first_win[row].astype(jnp.float32) if step == 0 else states[step][row]
            new = (acc - filter_center * cur) * (1.0 / filter_radius)
            if step == 1:
                new = 2.0 * new - first_win[row].astype(jnp.float32)
            elif step > 1:
                new = 2.0 * new - states[step - 1][row]
            rounded = new.astype(jnp.bfloat16)
            if step == DEGREE - 1:
                block[panel, row] = rounded
                continue
            windows[step + 1][row] = rounded
            states[step + 1][row] = new
            if row < span:
                tops[slot][0][row + part] = rounded
            if row < reach + part:
                tops[slot][1][row + reach] = rounded
            if row >= span:
                bottoms[slot][0][row - span] = rounded
            if row >= span + part:
                bottoms[slot][1][row - span - part] = rounded

    def send(which, start, size, sems, number, peer):
        piece = block.at[which, pl.ds(start, size)]
        return pltpu.make_async_remote_copy(
            src_ref=piece, dst_ref=piece, send_sem=sems.at[0, number],
            recv_sem=sems.at[1, number], device_id={"vecs": peer},
        )

    def part_start(half, number):
        return half * 3 * reach if number else reach + half * reach

    to_over = [send(panel, part_start(1 - side, n), reach, x_sem, n, over) for n in range(2)]
    passed = [send(over, part_start(side, n), reach, pass_sem, n, near) for n in range(2)]
    rest = [send(panel, part_start(0, n), reach, rest_sem, n, over) for n in range(2)]
    onward = [send(over, part_start(0, n), reach, on_sem, n, near) for n in range(2)]
    to_near = [
        send(panel, first, size, side_sem, n, near)
        for n, (first, size) in enumerate(((reach, span), (3 * reach, reach), (0, reach)))
    ]
    contract = (((0,), (0,)), ((), ()))

    def product(left, right):
        return lax.dot_general(left, right, contract, preferred_element_type=jnp.float32)

    def rows_of(which, start, size):
        return block[which, pl.ds(start, size)].reshape(size * block.shape[2], wide)

    def add_own(start, size):
        @pl.loop(0, size // part)
        def _(index):
            own = rows_of(panel, start + index * part, part)
            near_total[:wide, :] += product(own, own)

    def add_near(start, size):
        @pl.loop(0, size // part)
        def _(index):
            own = rows_of(panel, start + index * part, part)
            beside = rows_of(near, start + index * part, part)

            @pl.when(core == 0)
            def _():
                near_total[wide:, :] += product(beside[:, :short], own)

            @pl.when(core == 1)
            def _():
                near_total[wide:, :] += product(own[:, short:], beside)

    def add_across(number):
        @pl.loop(0, 2)
        def _(index):
            start = part_start(side, number) + index * part
            own, there = rows_of(panel, start, part), rows_of(over, start, part)

            @pl.when(side == 0)
            def _():
                cross[core] += product(there, own)

            @pl.when(side == 1)
            def _():
                cross[core] += product(own, there)
                cross[1 - core] += product(rows_of(near, start, part), there)

    def add_beyond(number):
        @pl.when(side == 0)
        def _():
            @pl.loop(0, 2)
            def _(index):
                start = part_start(0, number) + index * part
                cross[1 - core] += product(rows_of(beyond, start, part), rows_of(panel, start, part))

    @pl.when(below)
    def _():
        to_lower(0, 0).start()

    @pl.when(above)
    def _():
        to_upper(0, 0).start()

    near_total[...] = jnp.zeros_like(near_total)
    cross[...] = jnp.zeros_like(cross)
    for fetch in fetches:
        fetch.wait()

    for step in range(DEGREE):
        last = step == DEGREE - 1
        compute(step, reach, reach, windows[step])
        compute(step, span, reach, windows[step])
        if last:
            to_over[0].start()
            to_near[0].start()

        @pl.when(below)
        def _():
            to_lower(step, 0).wait_send()
            to_lower(step, 1).start()

        @pl.when(above)
        def _():
            to_upper(step, 0).wait_send()
            to_upper(step, 1).start()

        if last:
            add_own(reach, span)

        @pl.when(above)
        def _():
            to_lower(step, 0).wait_recv()
            join_bottom(step).start()

        compute(step, 3 * reach, part, bottoms[step % 2][0])

        @pl.when(below)
        def _():
            to_upper(step, 0).wait_recv()
            join_top(step).start()

        compute(step, part, part, tops[step % 2][0])
        if last:
            to_over[0].wait_send()

            @pl.when(side == 0)
            def _():
                rest[0].start()

        @pl.when(above)
        def _():
            join_bottom(step).wait()
            to_lower(step, 1).wait_recv()

        compute(step, 3 * reach + part, part, bottoms[step % 2][1])
        if last:
            to_near[1].start()

            @pl.when(side == 0)
            def _():
                to_over[1].start()
        else:

            @pl.when(above)
            def _():
                to_upper(step + 1, 0).start()

        @pl.when(below)
        def _():
            join_top(step).wait()
            to_upper(step, 1).wait_recv()

        compute(step, 0, part, tops[step % 2][1])
        if last:
            to_near[2].start()

            @pl.when(side == 1)
            def _():
                to_over[1].start()
        else:

            @pl.when(below)
            def _():
                to_lower(step + 1, 0).start()

        @pl.when(below)
        def _():
            to_lower(step, 1).wait_send()

        @pl.when(above)
        def _():
            to_upper(step, 1).wait_send()

    keep_own = pltpu.make_async_copy(block.at[panel], block_ref.at[panel], keep_sem.at[0])
    keep_own.start()
    add_own(3 * reach, reach)
    add_own(0, reach)
    to_near[0].wait()
    add_near(reach, span)
    to_near[1].wait()
    add_near(3 * reach, reach)
    to_near[2].wait()
    add_near(0, reach)
    keep_near = pltpu.make_async_copy(block.at[near], block_ref.at[near], keep_sem.at[1])
    keep_near.start()

    shape = (me, panel)
    near_sum = Reduction(near_stages, *shape, near_total, near_landing, full, 0, near_stage_sem, near_all_sem)
    cross_sum = Reduction(
        cross_stages, *shape, cross_total, cross_landing, full, wide + short, cross_stage_sem, cross_all_sem
    )
    stages = len(near_stages)
    ahead = min(stages, 3)
    near_sum.reduce_start(0)
    to_over[0].wait_recv()
    passed[0].start()
    add_across(0)
    for number in range(ahead):
        near_sum.reduce_finish(number)
        near_sum.reduce_start(number + 1)
        if number == 0:
            passed[0].wait()
            add_beyond(0)
    to_over[1].wait()
    passed[1].start()
    add_across(1)
    passed[1].wait()
    add_beyond(1)
    swap = pltpu.make_async_remote_copy(
        src_ref=cross.at[1 - side], dst_ref=cross_in,
        send_sem=swap_sem.at[0], recv_sem=swap_sem.at[1], device_id={"vecs": over},
    )
    swap.start()
    for number in range(ahead, stages):
        near_sum.reduce_finish(number)
        near_sum.reduce_start(number + 1)
    near_sum.publish()
    near_sum.gather_start(0)
    swap.wait()
    cross_total[...] = cross[side] + cross_in[...]
    cross_sum.reduce_start(0)

    @pl.when(side == 0)
    def _():
        rest[0].wait_send()
        rest[1].start()

    @pl.when(side == 1)
    def _():
        rest[0].wait_recv()
        onward[0].start()

    for number in range(stages):
        cross_sum.reduce_finish(number)
        cross_sum.reduce_start(number + 1)
        near_sum.gather_finish(number)
        near_sum.gather_start(number + 1)
    cross_sum.publish()
    cross_sum.gather_start(0)
    for number in range(stages):
        cross_sum.gather_finish(number)
        cross_sum.gather_start(number + 1)

    near_sum.settle()
    keep_own.wait()
    keep_near.wait()
    keep_over = pltpu.make_async_copy(block.at[over], block_ref.at[over], keep_sem.at[0])
    keep_beyond = pltpu.make_async_copy(block.at[beyond], block_ref.at[beyond], keep_sem.at[1])

    @pl.when(side == 0)
    def _():
        rest[1].wait_send()

    @pl.when(side == 1)
    def _():
        rest[1].wait_recv()
        onward[1].start()
        onward[0].wait()
        keep_over.start()

    cross_sum.settle()
    near_sum.close()
    cross_sum.close()
    low_sums = pltpu.make_async_copy(full.at[:2], sums_ref.at[:2], keep_sem.at[2])
    high_sums = pltpu.make_async_copy(full.at[2:], sums_ref.at[2:], keep_sem.at[3])
    low_sums.start()

    @pl.when(side == 1)
    def _():
        high_sums.start()
        onward[1].wait()
        keep_beyond.start()
        keep_over.wait()
        keep_beyond.wait()
        high_sums.wait()

    low_sums.wait()


def filtered_sums(vectors, blocks, columns):
    rows, width = vectors.shape
    block_rows, nnz, size_b = blocks.shape[:3]
    panels, devices = lax.axis_size("vecs"), lax.axis_size("rows")
    reach = block_rows // 4
    part = reach // 2
    near_rows, cross_rows = width + width // 2, width
    near_stages, cross_stages = gram_stages(near_rows, devices), gram_stages(cross_rows, devices)
    steps = len(near_stages)
    row = lax.broadcasted_iota(jnp.int32, columns.shape, 0)
    shift = jnp.zeros_like(columns)
    for start, amount in (
        (0, reach), (part, part), (reach, 0), (3 * reach, -2 * reach), (3 * reach + part, -2 * reach - part),
    ):
        shift = jnp.where(row >= start, amount, shift)
    place = columns - lax.axis_index("rows") * block_rows + shift
    window = pltpu.VMEM((block_rows, size_b, width), jnp.bfloat16)
    side = pltpu.VMEM((2 * reach + part, size_b, width), jnp.bfloat16)
    state = pltpu.VMEM((block_rows, size_b, width), jnp.float32)
    anywhere = pl.BlockSpec(memory_space=pl.ANY)
    dma = pltpu.SemaphoreType.DMA

    def single(tall):
        return pltpu.VMEM((tall, width), jnp.float32)

    def kernel(*refs):
        inputs, wins, refs = refs[:5], refs[5:8], refs[8:]
        tops = ((refs[0], refs[1]), (refs[2], refs[3]))
        bottoms = ((refs[4], refs[5]), (refs[6], refs[7]))
        filter_kernel(near_stages, cross_stages, *inputs, *wins, tops, bottoms, *refs[8:])

    sums, block = pl.pallas_call(
        kernel,
        out_shape=[
            jax.ShapeDtypeStruct((panels, near_rows + cross_rows, width), jnp.float32),
            jax.ShapeDtypeStruct((panels, block_rows, size_b, width), jnp.bfloat16),
        ],
        in_specs=[pl.BlockSpec(memory_space=pltpu.SMEM), anywhere, anywhere],
        out_specs=[anywhere, anywhere],
        scratch_shapes=[window] * 3 + [side] * 8 + [state] * 2 + [
            pltpu.VMEM(blocks.shape, jnp.bfloat16),
            pltpu.VMEM((panels, block_rows, size_b, width), jnp.bfloat16),
            pltpu.VMEM((2, width, width), jnp.float32),
            single(near_rows), single(cross_rows),
            pltpu.VMEM((panels, near_rows + cross_rows, width), jnp.float32),
            single(2 * near_rows), single(2 * cross_rows), single(width),
            dma((6,)), dma((2, 2, 2)), dma((2, 2, 2)), dma((2,)), dma((4,)), dma((2,)),
            dma((2, 3)), dma((2, 2)), dma((2, 2)), dma((2, 2)), dma((2, 2)),
            dma((4, steps)), dma((2, 3, steps + 1)), dma((4, steps)), dma((2, 3, steps + 1)),
        ],
        compiler_params=pltpu.CompilerParams(
            vmem_limit_bytes=VMEM_LIMIT, collective_id=0, has_side_effects=True
        ),
    )(place, vectors.reshape(block_rows, size_b, width), blocks)
    return sums, block.reshape(panels, rows, width)


def finish_kernel(
    size, total_rows, gram_ref, block_ref, out_ref, work, inverse, scale, block, result, in_sem, out_sem
):
    full = inverse.shape[0]
    mine = lax.axis_index("vecs")

    def fetch(panel):
        return pltpu.make_async_copy(block_ref.at[panel], block.at[panel], in_sem.at[panel])

    for panel in range(gram_ref.shape[0]):

        @pl.when(panel <= mine)
        def _():
            fetch(panel).start()

    panels, _, wide = gram_ref.shape
    count, short = full // size, wide // 2
    same = lax.broadcasted_iota(jnp.int32, (wide, wide), 0) == lax.broadcasted_iota(
        jnp.int32, (wide, wide), 1
    )
    down, along = [], []
    for panel in range(panels):
        diagonal = jnp.where(same, gram_ref[panel, :wide, :], 0.0)
        sums = jnp.sum(diagonal, axis=0, keepdims=True)
        along.append(lax.rsqrt(sums))
        down.append(lax.rsqrt(jnp.sum(diagonal, axis=1, keepdims=True)))
        scale[:, panel * wide : (panel + 1) * wide] = lax.rsqrt(sums * (1.0 / total_rows))
    for panel in range(panels):
        core, side = panel % 2, panel // 2
        own = slice(panel * wide, (panel + 1) * wide)
        work[own, own] = gram_ref[panel, :wide, :] * down[panel] * along[panel]
        first = 2 * side
        part = slice(core * short, (core + 1) * short)
        low = (first + 1) * wide + core * short
        work[low : low + short, first * wide : (first + 1) * wide] = (
            gram_ref[panel, wide : wide + short, :] * down[first + 1][part, :] * along[first]
        )
        other = 2 + side
        work[other * wide : (other + 1) * wide, core * wide : (core + 1) * wide] = (
            gram_ref[panel, wide + short :, :] * down[other] * along[core]
        )

    def span(c):
        return slice(c * size, (c + 1) * size)

    done = factor_block(work[span(0), span(0)])
    for c in range(count):
        own = span(c)
        stop = ((c * size) // wide + 1) * wide
        if stop > (c + 1) * size:
            inverse[own, (c + 1) * size : stop] = jnp.zeros((size, stop - (c + 1) * size), jnp.float32)
        lower = halves(done)
        inverse[own, own] = done
        if c + 1 < count:
            below = slice((c + 1) * size, full)
            column = triple(halves(work[below, own]), lower, TURNED)
            pieces = halves(column)
            top = (pieces[0][:size], pieces[1][:size])
            following = work[span(c + 1), span(c + 1)] - triple(top, top, TURNED)
        if c > 0:
            known = triple(lower, halves(work[own, : c * size]), PLAIN)
            inverse[own, : c * size] = known
        if c + 1 < count:
            done = factor_block(following)
            work[below, own] = -triple(pieces, lower, PLAIN)
            if c > 0:
                work[below, : c * size] -= triple(pieces, halves(known), PLAIN)
            for j in range(c + 1, count):
                first = max(j, c + 2)
                if first == count:
                    continue
                rows = slice((first - c - 1) * size, (count - c - 1) * size)
                cols = slice((j - c - 1) * size, (j - c) * size)
                work[first * size :, span(j)] -= triple(
                    (pieces[0][rows], pieces[1][rows]), (pieces[0][cols], pieces[1][cols]), TURNED
                )
    high, low = halves(inverse[pl.ds(pl.multiple_of(mine * wide, wide), wide), :] * scale[...])
    tiles = out_sem.shape[0]
    tile = block.shape[1] // tiles

    def store(index):
        rows = pl.ds(pl.multiple_of(index * tile, tile), tile)
        return pltpu.make_async_copy(result.at[rows], out_ref.at[rows], out_sem.at[index])

    for number in range(1, panels + 1):

        @pl.when(mine == number - 1)
        def _():
            for panel in range(number):
                fetch(panel).wait()
            deep = number * wide
            right = jnp.concatenate([high[:, :deep], low[:, :deep]], axis=1)

            @pl.loop(0, tiles)
            def _(index):
                rows = pl.ds(pl.multiple_of(index * tile, tile), tile)
                left = jnp.concatenate([block[panel, rows, :] for panel in range(number)] * 2, axis=1)
                result[rows, :] = lax.dot_general(
                    left, right, TURNED, preferred_element_type=jnp.float32
                )
                store(index).start()

    for index in range(tiles):
        store(index).wait()


def finish(gram, block, total_rows):
    panels, rows, wide = block.shape
    full = panels * wide
    size = 128
    tiles = 4
    anywhere = pl.BlockSpec(memory_space=pl.ANY)
    return pl.pallas_call(
        functools.partial(finish_kernel, size, total_rows),
        out_shape=jax.ShapeDtypeStruct((rows, wide), jnp.float32),
        in_specs=[pl.BlockSpec(memory_space=pltpu.VMEM), anywhere],
        out_specs=anywhere,
        scratch_shapes=[
            pltpu.VMEM((full, full), jnp.float32),
            pltpu.VMEM((full, full), jnp.float32),
            pltpu.VMEM((1, full), jnp.float32),
            pltpu.VMEM((panels, rows, wide), jnp.bfloat16),
            pltpu.VMEM((rows, wide), jnp.float32),
            pltpu.SemaphoreType.DMA((panels,)),
            pltpu.SemaphoreType.DMA((tiles,)),
        ],
        compiler_params=pltpu.CompilerParams(vmem_limit_bytes=VMEM_LIMIT),
    )(gram, block)


def shards(vectors, blocks, columns):
    total_rows = vectors.shape[0] * lax.axis_size("rows")
    sums, block = filtered_sums(vectors, blocks, columns)
    return finish(sums, block, total_rows)


def solution(mesh):
    in_specs = (P("rows", "vecs"), P("rows", None, None, None), P("rows", None))
    out_specs = P("rows", "vecs")
    return jax.shard_map(shards, mesh=mesh, in_specs=in_specs, out_specs=out_specs, check_vma=False)
```

```python
import functools

import jax
import jax.numpy as jnp
from jax import lax
from jax.experimental import pallas as pl
from jax.experimental.pallas import tpu as pltpu
from jax.sharding import PartitionSpec as P

DEGREE = 4

filter_center = 0.25
filter_radius = 1.25

VMEM_LIMIT = 56 * 1024 * 1024


def factor_block(block, middle=None):
    size = block.shape[0]
    tiles = [block[8 * t : 8 * (t + 1), :] for t in range(size // 8)]
    lane = lax.broadcasted_iota(jnp.int32, (8, size), 1)
    sub = lax.broadcasted_iota(jnp.int32, (8, size), 0)

    def spread(array):
        return jnp.broadcast_to(array, (8, size))

    for first in range(size // 8):
        if middle and first == size // 16:
            middle()
        j = 8 * first
        each = range(8)
        at_any = jnp.logical_and(lane >= j, lane < j + 8)
        head = tiles[first]
        cols = [spread(head[:, j + a : j + a + 1]) for a in each]
        p = [[spread(cols[a][b : b + 1, :]) for a in range(b + 1)] for b in each]
        rows = [jnp.where(at_any, 0.0, spread(head[a : a + 1, :])) for a in each]
        rows = [jnp.where(lane == j + a, 1.0, rows[a]) for a in each]
        pairs, ready = [], []
        for a in range(0, 8, 2):
            b = a + 1
            det = p[a][a] * p[b][b] - p[b][a] * p[b][a]
            inv = 1.0 / det
            e_aa, e_ab, e_bb = p[b][b] * inv, p[b][a] * inv, p[a][a] * inv
            over = 1.0 / p[a][a]
            ready.append(rows[a] * lax.rsqrt(p[a][a]))
            ready.append((rows[b] - (p[b][a] * over) * rows[a]) * lax.rsqrt(det * over))
            mult = {}
            for c in range(b + 1, 8):
                mult[c, 0] = p[c][a] * e_aa - p[c][b] * e_ab
                mult[c, 1] = p[c][b] * e_bb - p[c][a] * e_ab
            for c in range(b + 1, 8):
                for d in range(b + 1, c + 1):
                    p[c][d] = p[c][d] - (mult[c, 0] * p[d][a] + mult[c, 1] * p[d][b])
            pairs.append((e_aa, e_ab, e_bb, mult, rows[a], rows[b]))
            for c in range(b + 1, 8):
                rows[c] = rows[c] - (mult[c, 0] * rows[a] + mult[c, 1] * rows[b])
        use = [None] * 8
        for number in reversed(range(4)):
            a, b = 2 * number, 2 * number + 1
            e_aa, e_ab, e_bb, mult, row_a, row_b = pairs[number]
            use[a] = e_aa * row_a - e_ab * row_b
            use[b] = e_bb * row_b - e_ab * row_a
            for c in range(b + 1, 8):
                use[a] = use[a] - mult[c, 0] * use[c]
                use[b] = use[b] - mult[c, 1] * use[c]
        for t in range(first + 1, size // 8):
            tile = tiles[t]
            cols = [spread(tile[:, j + a : j + a + 1]) for a in each]
            terms = [cols[a] * use[a] for a in each]
            while len(terms) > 1:
                terms = [x + y for x, y in zip(terms[::2], terms[1::2])]
            tiles[t] = jnp.where(at_any, 0.0, tile) - terms[0]
        top = ready[0]
        for a in range(1, 8):
            top = jnp.where(sub == a, ready[a], top)
        tiles[first] = top
    done = jnp.concatenate(tiles, axis=0)
    down = lax.broadcasted_iota(jnp.int32, (size, size), 0)
    across = lax.broadcasted_iota(jnp.int32, (size, size), 1)
    return jnp.where(across <= down, done, 0.0)


def halves(array):
    high = array.astype(jnp.bfloat16)
    return high, (array - high.astype(jnp.float32)).astype(jnp.bfloat16)


PLAIN = (((1,), (0,)), ((), ()))
TURNED = (((1,), (1,)), ((), ()))


def triple(left, right, dims):
    def one(a, b):
        return lax.dot_general(a, b, dims, preferred_element_type=jnp.float32)

    return one(left[0], right[0]) + (one(left[0], right[1]) + one(left[1], right[0]))


def gram_stages(rows, devices):
    stages, bit, held = [], 1, rows
    while bit < devices:
        halve = held % 16 == 0
        stages.append((bit, halve))
        held, bit = held // 2 if halve else held, bit * 2
    return stages


def flipped(index, bit):
    return index + bit - 2 * bit * lax.rem(index // bit, 2)


class Reduction:
    def __init__(self, stages, me, panel, total, landing, full, base, stage_sem, all_sem):
        self.me, self.panel, self.total, self.landing, self.full = me, panel, total, landing, full
        self.base, self.stage_sem, self.all_sem = base, stage_sem, all_sem
        self.near, self.over, self.side = flipped(panel, 1), flipped(panel, 2), panel // 2
        self.steps, self.shared = [], []
        start, held, taken = 0, total.shape[0], 0
        for bit, halve in stages:
            size = held // 2 if halve else held
            upper = lax.rem(me // bit, 2)
            keep = pl.multiple_of(start + upper * size, 8) if halve else start
            give = pl.multiple_of(start + (1 - upper) * size, 8) if halve else start
            self.steps.append((bit, size, keep, give, taken))
            start, held, taken = keep, size, taken + size
        self.start, self.held = start, held
        self.gathers = [n for n in reversed(range(len(stages))) if stages[n][1]]

    def reduce_copy(self, number):
        bit, size, _, give, taken = self.steps[number]
        return pltpu.make_async_remote_copy(
            src_ref=self.total.at[pl.ds(give, size)], dst_ref=self.landing.at[taken : taken + size],
            send_sem=self.stage_sem.at[0, number], recv_sem=self.stage_sem.at[1, number],
            device_id={"rows": flipped(self.me, bit)},
        )

    def reduce_start(self, number):
        if number < len(self.steps):
            self.reduce_copy(number).start()

    def reduce_finish(self, number):
        if number < len(self.steps):
            _, size, keep, _, taken = self.steps[number]
            self.reduce_copy(number).wait()
            self.total[pl.ds(keep, size), :] += self.landing[taken : taken + size, :]

    def piece(self, which, first, size):
        return self.full.at[which, pl.ds(pl.multiple_of(self.base + first, 8), size)]

    def hand(self, which, kind, number, first, size, peer):
        piece = self.piece(which, first, size)
        return pltpu.make_async_remote_copy(
            src_ref=piece, dst_ref=piece, send_sem=self.all_sem.at[0, kind, number],
            recv_sem=self.all_sem.at[1, kind, number], device_id={"vecs": peer},
        )

    def hands(self, number, kind):
        first, size = self.shared[number]
        which = self.over if kind == 2 else self.panel
        peer = self.near if kind else self.over
        return self.hand(which, kind, number, first, size, peer)

    def share(self, first, size):
        self.shared.append((first, size))
        number = len(self.shared) - 1

        @pl.when(self.side == 0)
        def _():
            self.hands(number, 0).start()

        self.hands(number, 1).start()

    def publish(self):
        rows = pl.ds(pl.multiple_of(self.base + self.start, 8), self.held)
        self.full[self.panel, rows, :] = self.total[pl.ds(self.start, self.held), :]
        self.share(self.start, self.held)

    def gather_copy(self, index):
        number = self.gathers[index]
        bit, size, keep, _, _ = self.steps[number]
        piece = self.piece(self.panel, keep, size)
        return pltpu.make_async_remote_copy(
            src_ref=piece, dst_ref=piece, send_sem=self.stage_sem.at[2, number],
            recv_sem=self.stage_sem.at[3, number], device_id={"rows": flipped(self.me, bit)},
        )

    def gather_start(self, index):
        if index < len(self.gathers):
            self.gather_copy(index).start()

    def gather_finish(self, index):
        if index < len(self.gathers):
            self.gather_copy(index).wait()
            _, size, _, give, _ = self.steps[self.gathers[index]]
            self.share(give, size)

    def settle(self):
        for number in range(len(self.shared)):

            @pl.when(self.side == 1)
            def _():
                self.hands(number, 0).wait_recv()
                self.hands(number, 2).start()

            @pl.when(self.side == 0)
            def _():
                self.hands(number, 0).wait_send()

            self.hands(number, 1).wait()

    def close(self):
        @pl.when(self.side == 1)
        def _():
            for number in range(len(self.shared)):
                self.hands(number, 2).wait()


def filter_kernel(
    near_stages, cross_stages, place_ref, vectors_ref, blocks_ref, sums_ref, block_ref, lead_ref,
    first_win, even_win, odd_win, tops, bottoms, even, odd, held,
    block, cross, near_total, cross_total, full, near_landing, cross_landing, cross_in, work, lead,
    in_sem, send_sem, recv_sem, copy_sem, keep_sem, swap_sem, side_sem, x_sem, pass_sem, rest_sem, on_sem,
    near_stage_sem, near_all_sem, cross_stage_sem, cross_all_sem,
):
    me, count = lax.axis_index("rows"), lax.axis_size("rows")
    panel = lax.axis_index("vecs")
    core, side = lax.rem(panel, 2), panel // 2
    near, over = flipped(panel, 1), flipped(panel, 2)
    beyond = flipped(over, 1)
    block_rows, nnz = blocks_ref.shape[:2]
    wide = block.shape[3]
    short = wide // 2
    reach = block_rows // 4
    span, part = 2 * reach, reach // 2
    windows = [first_win, odd_win, even_win, odd_win]
    states = [None, even, odd, even]
    above, below = me < count - 1, me > 0

    peers = [{"vecs": near}, {"vecs": over}] + [{"rows": flipped(me, bit)} for bit, _ in near_stages]
    inside = jnp.logical_and(above, below)
    for peer in peers:
        pl.semaphore_signal(pltpu.get_barrier_semaphore(), 1, device_id=peer)

    @pl.when(inside)
    def _():
        other = me - 1 + 2 * lax.rem(me, 2)
        pl.semaphore_signal(pltpu.get_barrier_semaphore(), 1, device_id={"rows": other})

    pieces = [
        (vectors_ref, first_win),
        (vectors_ref.at[:span], tops[0][0].at[part:]),
        (vectors_ref.at[: reach + part], tops[0][1].at[reach:]),
        (vectors_ref.at[span:], bottoms[0][0].at[:span]),
        (vectors_ref.at[span + part :], bottoms[0][1].at[: reach + part]),
        (blocks_ref, held),
    ]
    fetches = [pltpu.make_async_copy(*pair, in_sem.at[n]) for n, pair in enumerate(pieces)]
    for fetch in fetches:
        fetch.start()

    @pl.when(inside)
    def _():
        pl.semaphore_wait(pltpu.get_barrier_semaphore(), len(peers) + 1)

    @pl.when(jnp.logical_not(inside))
    def _():
        pl.semaphore_wait(pltpu.get_barrier_semaphore(), len(peers))

    def to_lower(step, far):
        source = vectors_ref if step == 0 else windows[step]
        return pltpu.make_async_remote_copy(
            src_ref=source.at[far * part : (far + 1) * part],
            dst_ref=bottoms[step % 2][far].at[span:],
            send_sem=send_sem.at[0, far, step % 2], recv_sem=recv_sem.at[0, far, step % 2],
            device_id={"rows": me - 1},
        )

    def to_upper(step, far):
        source = vectors_ref if step == 0 else windows[step]
        first = block_rows - (far + 1) * part
        return pltpu.make_async_remote_copy(
            src_ref=source.at[first : first + part], dst_ref=tops[step % 2][far].at[:part],
            send_sem=send_sem.at[1, far, step % 2], recv_sem=recv_sem.at[1, far, step % 2],
            device_id={"rows": me + 1},
        )

    def join_bottom(step):
        close, far = bottoms[step % 2]
        return pltpu.make_async_copy(close.at[span:], far.at[reach + part : span], copy_sem.at[0])

    def join_top(step):
        close, far = tops[step % 2]
        return pltpu.make_async_copy(close.at[:part], far.at[part:reach], copy_sem.at[1])

    def compute(step, start, rows, window):
        slot = (step + 1) % 2
        for row in range(start, start + rows):
            left = jnp.concatenate([held[row, j] for j in range(nnz)], axis=1)
            right = jnp.concatenate([window[place_ref[row, j]] for j in range(nnz)], axis=0)
            acc = jnp.dot(left, right, preferred_element_type=jnp.float32)
            cur = first_win[row].astype(jnp.float32) if step == 0 else states[step][row]
            new = (acc - filter_center * cur) * (1.0 / filter_radius)
            if step == 1:
                new = 2.0 * new - first_win[row].astype(jnp.float32)
            elif step > 1:
                new = 2.0 * new - states[step - 1][row]
            rounded = new.astype(jnp.bfloat16)
            if step == DEGREE - 1:
                block[panel, row] = rounded
                continue
            windows[step + 1][row] = rounded
            states[step + 1][row] = new
            if row < span:
                tops[slot][0][row + part] = rounded
            if row < reach + part:
                tops[slot][1][row + reach] = rounded
            if row >= span:
                bottoms[slot][0][row - span] = rounded
            if row >= span + part:
                bottoms[slot][1][row - span - part] = rounded

    def send(which, start, size, sems, number, peer):
        piece = block.at[which, pl.ds(start, size)]
        return pltpu.make_async_remote_copy(
            src_ref=piece, dst_ref=piece, send_sem=sems.at[0, number],
            recv_sem=sems.at[1, number], device_id={"vecs": peer},
        )

    def part_start(half, number):
        return half * 3 * reach if number else reach + half * reach

    to_over = [send(panel, part_start(1 - side, n), reach, x_sem, n, over) for n in range(2)]
    passed = [send(over, part_start(side, n), reach, pass_sem, n, near) for n in range(2)]
    rest = [send(panel, part_start(0, n), reach, rest_sem, n, over) for n in range(2)]
    onward = [send(over, part_start(0, n), reach, on_sem, n, near) for n in range(2)]
    to_near = [
        send(panel, first, size, side_sem, n, near)
        for n, (first, size) in enumerate(((reach, span), (3 * reach, reach), (0, reach)))
    ]
    contract = (((0,), (0,)), ((), ()))

    def product(left, right):
        return lax.dot_general(left, right, contract, preferred_element_type=jnp.float32)

    def rows_of(which, start, size):
        return block[which, pl.ds(start, size)].reshape(size * block.shape[2], wide)

    def add_own(start, size):
        @pl.loop(0, size // part)
        def _(index):
            own = rows_of(panel, start + index * part, part)
            near_total[:wide, :] += product(own, own)

    def add_near(start, size):
        @pl.loop(0, size // part)
        def _(index):
            own = rows_of(panel, start + index * part, part)
            beside = rows_of(near, start + index * part, part)

            @pl.when(core == 0)
            def _():
                near_total[wide:, :] += product(beside[:, :short], own)

            @pl.when(core == 1)
            def _():
                near_total[wide:, :] += product(own[:, short:], beside)

    def add_across(number):
        @pl.loop(0, 2)
        def _(index):
            start = part_start(side, number) + index * part
            own, there = rows_of(panel, start, part), rows_of(over, start, part)

            @pl.when(side == 0)
            def _():
                cross[core] += product(there, own)

            @pl.when(side == 1)
            def _():
                cross[core] += product(own, there)
                cross[1 - core] += product(rows_of(near, start, part), there)

    def add_beyond(number):
        @pl.when(side == 0)
        def _():
            @pl.loop(0, 2)
            def _(index):
                start = part_start(0, number) + index * part
                cross[1 - core] += product(rows_of(beyond, start, part), rows_of(panel, start, part))

    @pl.when(below)
    def _():
        to_lower(0, 0).start()

    @pl.when(above)
    def _():
        to_upper(0, 0).start()

    near_total[...] = jnp.zeros_like(near_total)
    cross[...] = jnp.zeros_like(cross)
    for fetch in fetches:
        fetch.wait()

    for step in range(DEGREE):
        last = step == DEGREE - 1
        compute(step, reach, reach, windows[step])
        compute(step, span, reach, windows[step])
        if last:
            to_over[0].start()
            to_near[0].start()

        @pl.when(below)
        def _():
            to_lower(step, 0).wait_send()
            to_lower(step, 1).start()

        @pl.when(above)
        def _():
            to_upper(step, 0).wait_send()
            to_upper(step, 1).start()

        if last:
            add_own(reach, span)

        @pl.when(above)
        def _():
            to_lower(step, 0).wait_recv()
            join_bottom(step).start()

        compute(step, 3 * reach, part, bottoms[step % 2][0])

        @pl.when(below)
        def _():
            to_upper(step, 0).wait_recv()
            join_top(step).start()

        compute(step, part, part, tops[step % 2][0])
        if last:
            to_over[0].wait_send()

            @pl.when(side == 0)
            def _():
                rest[0].start()

        @pl.when(above)
        def _():
            join_bottom(step).wait()
            to_lower(step, 1).wait_recv()

        compute(step, 3 * reach + part, part, bottoms[step % 2][1])
        if last:
            to_near[1].start()

            @pl.when(side == 0)
            def _():
                to_over[1].start()
        else:

            @pl.when(above)
            def _():
                to_upper(step + 1, 0).start()

        @pl.when(below)
        def _():
            join_top(step).wait()
            to_upper(step, 1).wait_recv()

        compute(step, 0, part, tops[step % 2][1])
        if last:
            to_near[2].start()

            @pl.when(side == 1)
            def _():
                to_over[1].start()
        else:

            @pl.when(below)
            def _():
                to_lower(step + 1, 0).start()

        @pl.when(below)
        def _():
            to_lower(step, 1).wait_send()

        @pl.when(above)
        def _():
            to_upper(step, 1).wait_send()

    keep_own = pltpu.make_async_copy(block.at[panel], block_ref.at[panel], keep_sem.at[0])
    keep_own.start()
    add_own(3 * reach, reach)
    add_own(0, reach)
    to_near[0].wait()
    add_near(reach, span)
    to_near[1].wait()
    add_near(3 * reach, reach)
    to_near[2].wait()
    add_near(0, reach)
    keep_near = pltpu.make_async_copy(block.at[near], block_ref.at[near], keep_sem.at[1])
    keep_near.start()

    shape = (me, panel)
    near_sum = Reduction(near_stages, *shape, near_total, near_landing, full, 0, near_stage_sem, near_all_sem)
    cross_sum = Reduction(
        cross_stages, *shape, cross_total, cross_landing, full, wide + short, cross_stage_sem, cross_all_sem
    )
    stages = len(near_stages)
    ahead = min(stages, 3)
    near_sum.reduce_start(0)
    to_over[0].wait_recv()
    passed[0].start()
    add_across(0)
    for number in range(stages):
        near_sum.reduce_finish(number)
        near_sum.reduce_start(number + 1)
        if number == 0:
            passed[0].wait()
            add_beyond(0)
    near_sum.publish()
    near_sum.gather_start(0)
    to_over[1].wait()
    passed[1].start()
    add_across(1)
    passed[1].wait()
    add_beyond(1)
    swap = pltpu.make_async_remote_copy(
        src_ref=cross.at[1 - side], dst_ref=cross_in,
        send_sem=swap_sem.at[0], recv_sem=swap_sem.at[1], device_id={"vecs": over},
    )
    swap.start()
    near_sum.gather_finish(0)
    near_sum.gather_start(1)
    swap.wait()
    cross_total[...] = cross[side] + cross_in[...]
    cross_sum.reduce_start(0)
    for number in range(1, stages):
        near_sum.gather_finish(number)
        near_sum.gather_start(number + 1)
        if number == 1:
            cross_sum.reduce_finish(0)
            cross_sum.reduce_start(1)
    near_sum.settle()
    near_sum.close()

    @pl.when(side == 0)
    def _():
        rest[0].wait_send()
        rest[1].start()

    def gather_next(number):
        cross_sum.gather_finish(number)
        cross_sum.gather_start(number + 1)

    def reduced():
        cross_sum.reduce_finish(2)
        for number in range(3, stages):
            cross_sum.reduce_start(number)
            cross_sum.reduce_finish(number)
        cross_sum.publish()
        cross_sum.gather_start(0)

    def reduce_second():
        cross_sum.reduce_finish(1)
        cross_sum.reduce_start(2)

    def pass_rest():
        @pl.when(side == 1)
        def _():
            for copy, pass_on in zip(rest, onward):
                copy.wait_recv()
                pass_on.start()

    later = [functools.partial(gather_next, n) for n in range(1, len(cross_sum.gathers))]
    actions = [
        [reduce_second], [reduced], [functools.partial(gather_next, 0)], later[:1], later[1:], [],
        [pass_rest], [cross_sum.settle],
    ]
    lead_factor(full, work, lead, actions)
    lead_copy = pltpu.make_async_copy(lead, lead_ref, copy_sem.at[0])
    lead_copy.start()
    keep_own.wait()
    keep_near.wait()
    keep_over = pltpu.make_async_copy(block.at[over], block_ref.at[over], keep_sem.at[0])
    keep_beyond = pltpu.make_async_copy(block.at[beyond], block_ref.at[beyond], keep_sem.at[1])

    @pl.when(side == 0)
    def _():
        rest[1].wait_send()

    @pl.when(side == 1)
    def _():
        keep_over.start()

    cross_sum.close()
    low_sums = pltpu.make_async_copy(full.at[:2], sums_ref.at[:2], keep_sem.at[2])
    high_sums = pltpu.make_async_copy(full.at[2:], sums_ref.at[2:], keep_sem.at[3])
    low_sums.start()

    @pl.when(side == 1)
    def _():
        high_sums.start()
        onward[0].wait()
        onward[1].wait()
        keep_beyond.start()
        keep_over.wait()
        keep_beyond.wait()
        high_sums.wait()

    low_sums.wait()
    lead_copy.wait()


def filtered_sums(vectors, blocks, columns):
    rows, width = vectors.shape
    block_rows, nnz, size_b = blocks.shape[:3]
    panels, devices = lax.axis_size("vecs"), lax.axis_size("rows")
    reach = block_rows // 4
    part = reach // 2
    near_rows, cross_rows = width + width // 2, width
    near_stages, cross_stages = gram_stages(near_rows, devices), gram_stages(cross_rows, devices)
    steps = len(near_stages)
    row = lax.broadcasted_iota(jnp.int32, columns.shape, 0)
    shift = jnp.zeros_like(columns)
    for start, amount in (
        (0, reach), (part, part), (reach, 0), (3 * reach, -2 * reach), (3 * reach + part, -2 * reach - part),
    ):
        shift = jnp.where(row >= start, amount, shift)
    place = columns - lax.axis_index("rows") * block_rows + shift
    window = pltpu.VMEM((block_rows, size_b, width), jnp.bfloat16)
    side = pltpu.VMEM((2 * reach + part, size_b, width), jnp.bfloat16)
    state = pltpu.VMEM((block_rows, size_b, width), jnp.float32)
    anywhere = pl.BlockSpec(memory_space=pl.ANY)
    dma = pltpu.SemaphoreType.DMA

    def single(tall):
        return pltpu.VMEM((tall, width), jnp.float32)

    def kernel(*refs):
        inputs, wins, refs = refs[:6], refs[6:9], refs[9:]
        tops = ((refs[0], refs[1]), (refs[2], refs[3]))
        bottoms = ((refs[4], refs[5]), (refs[6], refs[7]))
        filter_kernel(near_stages, cross_stages, *inputs, *wins, tops, bottoms, *refs[8:])

    sums, block, lead = pl.pallas_call(
        kernel,
        out_shape=[
            jax.ShapeDtypeStruct((panels, near_rows + cross_rows, width), jnp.float32),
            jax.ShapeDtypeStruct((panels, block_rows, size_b, width), jnp.bfloat16),
            jax.ShapeDtypeStruct((2 * width, 2 * width), jnp.float32),
        ],
        in_specs=[pl.BlockSpec(memory_space=pltpu.SMEM), anywhere, anywhere],
        out_specs=[anywhere] * 3,
        scratch_shapes=[window] * 3 + [side] * 8 + [state] * 2 + [
            pltpu.VMEM(blocks.shape, jnp.bfloat16),
            pltpu.VMEM((panels, block_rows, size_b, width), jnp.bfloat16),
            pltpu.VMEM((2, width, width), jnp.float32),
            single(near_rows), single(cross_rows),
            pltpu.VMEM((panels, near_rows + cross_rows, width), jnp.float32),
            single(2 * near_rows), single(2 * cross_rows), single(width),
            pltpu.VMEM((2 * width, 2 * width), jnp.float32),
            pltpu.VMEM((2 * width, 2 * width), jnp.float32),
            dma((6,)), dma((2, 2, 2)), dma((2, 2, 2)), dma((2,)), dma((4,)), dma((2,)),
            dma((2, 3)), dma((2, 2)), dma((2, 2)), dma((2, 2)), dma((2, 2)),
            dma((4, steps)), dma((2, 3, steps + 1)), dma((4, steps)), dma((2, 3, steps + 1)),
        ],
        compiler_params=pltpu.CompilerParams(
            vmem_limit_bytes=VMEM_LIMIT, collective_id=0, has_side_effects=True
        ),
    )(place, vectors.reshape(block_rows, size_b, width), blocks)
    return sums, block.reshape(panels, rows, width), lead


def scales(diagonal):
    wide = diagonal.shape[0]
    down = lax.broadcasted_iota(jnp.int32, (wide, wide), 0)
    across = lax.broadcasted_iota(jnp.int32, (wide, wide), 1)
    kept = jnp.where(down == across, diagonal, 0.0)
    sums = jnp.sum(kept, axis=0, keepdims=True)
    return lax.rsqrt(jnp.sum(kept, axis=1, keepdims=True)), lax.rsqrt(sums), sums


def fill_lower(full, first, work):
    wide = full.shape[2]
    short = wide // 2
    parts = [scales(full[first + n, :wide, :]) for n in range(2)]
    for n in range(2):
        own = slice(n * wide, (n + 1) * wide)
        work[own, own] = full[first + n, :wide, :] * parts[n][0] * parts[n][1]
        rows = slice(n * short, (n + 1) * short)
        below = wide + n * short
        work[below : below + short, :wide] = (
            full[first + n, wide : wide + short, :] * parts[1][0][rows, :] * parts[0][1]
        )
    return parts


def lead_factor(full, work, lead, actions):
    whole = work.shape[0]
    wide, size = whole // 2, whole // 4
    work[:wide, wide:] = jnp.zeros((wide, wide), jnp.float32)
    fill_lower(full, 0, work)

    @pl.loop(0, 4)
    def _(k):
        start = pl.multiple_of(k * size, size)
        at = pl.ds(start, size)

        def act(second):
            for n in range(4):

                @pl.when(k == n)
                def _():
                    for action in actions[2 * n + second]:
                        action()

        done = factor_block(work[at, at], functools.partial(act, 0))
        act(1)
        lower = halves(done)
        rows = lax.broadcasted_iota(jnp.int32, (whole, size), 0)
        cols = lax.broadcasted_iota(jnp.int32, (size, whole), 1)
        below = rows >= start + size
        own = work[:, at]
        column = jnp.where(below, triple(halves(own), lower, TURNED), 0.0)
        known = jnp.where(cols < start, work[at, :], 0.0)
        lead[at, :] = triple(lower, halves(known), PLAIN)
        lead[at, at] = done
        work[:, at] = jnp.where(below, 0.0, own)
        pieces = halves(column)
        work[...] -= triple(pieces, halves(lead[at, :]), PLAIN) + triple(pieces, pieces, TURNED)


def trail_factor(work, inverse, size):
    full = work.shape[0]
    count = full // size

    def span(c):
        return slice(c * size, (c + 1) * size)

    done = factor_block(work[span(0), span(0)])
    for c in range(count):
        own = span(c)
        lower = halves(done)
        inverse[own, own] = done
        if c + 1 < count:
            inverse[own, (c + 1) * size :] = jnp.zeros((size, full - (c + 1) * size), jnp.float32)
            below = slice((c + 1) * size, full)
            column = triple(halves(work[below, own]), lower, TURNED)
            pieces = halves(column)
            top = (pieces[0][:size], pieces[1][:size])
            following = work[span(c + 1), span(c + 1)] - triple(top, top, TURNED)
        if c > 0:
            known = triple(lower, halves(work[own, : c * size]), PLAIN)
            inverse[own, : c * size] = known
        if c + 1 < count:
            done = factor_block(following)
            work[below, own] = -triple(pieces, lower, PLAIN)
            if c > 0:
                work[below, : c * size] -= triple(pieces, halves(known), PLAIN)
            for j in range(c + 1, count):
                first = max(j, c + 2)
                if first == count:
                    continue
                rows = slice((first - c - 1) * size, (count - c - 1) * size)
                cols = slice((j - c - 1) * size, (j - c) * size)
                work[first * size :, span(j)] -= triple(
                    (pieces[0][rows], pieces[1][rows]), (pieces[0][cols], pieces[1][cols]), TURNED
                )


def finish_kernel(
    size, total_rows, sums_ref, lead_ref, block_ref, out_ref,
    work, inverse, cross, mixed, factor, block, result, in_sem, out_sem,
):
    panels, _, wide = sums_ref.shape
    short = wide // 2
    mine = lax.axis_index("vecs")
    side = mine // 2

    def fetch(panel):
        return pltpu.make_async_copy(block_ref.at[panel], block.at[panel], in_sem.at[panel])

    for panel in range(panels):

        @pl.when(panel <= mine)
        def _():
            fetch(panel).start()

    def scaled(sums):
        return lax.rsqrt(sums * (1.0 / total_rows))

    parts = [scales(sums_ref[panel, :wide, :]) for panel in range(2)]
    left_scale = jnp.concatenate([scaled(part[2]) for part in parts], axis=1)

    def keep(rows, first):
        high, low = halves(rows)
        factor[0, :, first : first + 2 * wide] = high
        factor[1, :, first : first + 2 * wide] = low

    @pl.when(side == 0)
    def _():
        keep(lead_ref[pl.ds(pl.multiple_of(mine * wide, wide), wide), :] * left_scale, 0)

    @pl.when(side == 1)
    def _():
        later = fill_lower(sums_ref, 2, work)
        for panel in range(panels):
            core, row = panel % 2, panel // 2
            cross[row * wide : (row + 1) * wide, core * wide : (core + 1) * wide] = (
                sums_ref[panel, wide + short :, :] * later[row][0] * parts[core][1]
            )
        lead = halves(lead_ref[...])
        ratio = halves(triple(halves(cross[...]), lead, TURNED))
        upper = (ratio[0][:wide], ratio[1][:wide])
        lower = (ratio[0][wide:], ratio[1][wide:])
        work[:wide, :wide] -= triple(upper, upper, TURNED)
        work[wide:, :] -= triple(lower, ratio, TURNED)
        mixed[...] = triple(ratio, lead, PLAIN)
        trail_factor(work, inverse, size)
        own = inverse[pl.ds(pl.multiple_of((mine - 2) * wide, wide), wide), :]
        keep(-triple(halves(own), halves(mixed[...]), PLAIN) * left_scale, 0)
        keep(own * jnp.concatenate([scaled(part[2]) for part in later], axis=1), 2 * wide)

    tiles = out_sem.shape[0]
    tile = block.shape[1] // tiles

    def store(index):
        rows = pl.ds(pl.multiple_of(index * tile, tile), tile)
        return pltpu.make_async_copy(result.at[rows], out_ref.at[rows], out_sem.at[index])

    for number in range(1, panels + 1):

        @pl.when(mine == number - 1)
        def _():
            for panel in range(number):
                fetch(panel).wait()
            deep = number * wide
            right = jnp.concatenate([factor[0, :, :deep], factor[1, :, :deep]], axis=1)

            @pl.loop(0, tiles)
            def _(index):
                rows = pl.ds(pl.multiple_of(index * tile, tile), tile)
                left = jnp.concatenate([block[panel, rows, :] for panel in range(number)] * 2, axis=1)
                result[rows, :] = lax.dot_general(
                    left, right, TURNED, preferred_element_type=jnp.float32
                )
                store(index).start()

    for index in range(tiles):
        store(index).wait()


def finish(sums, block, lead, total_rows):
    panels, rows, wide = block.shape
    size = 128
    tiles = 4
    anywhere = pl.BlockSpec(memory_space=pl.ANY)
    near = pl.BlockSpec(memory_space=pltpu.VMEM)
    square = pltpu.VMEM((2 * wide, 2 * wide), jnp.float32)
    return pl.pallas_call(
        functools.partial(finish_kernel, size, total_rows),
        out_shape=jax.ShapeDtypeStruct((rows, wide), jnp.float32),
        in_specs=[near, near, anywhere],
        out_specs=anywhere,
        scratch_shapes=[square] * 4 + [
            pltpu.VMEM((2, wide, panels * wide), jnp.bfloat16),
            pltpu.VMEM((panels, rows, wide), jnp.bfloat16),
            pltpu.VMEM((rows, wide), jnp.float32),
            pltpu.SemaphoreType.DMA((panels,)),
            pltpu.SemaphoreType.DMA((tiles,)),
        ],
        compiler_params=pltpu.CompilerParams(vmem_limit_bytes=VMEM_LIMIT),
    )(sums, lead, block)


def shards(vectors, blocks, columns):
    total_rows = vectors.shape[0] * lax.axis_size("rows")
    sums, block, lead = filtered_sums(vectors, blocks, columns)
    return finish(sums, block, lead, total_rows)


def solution(mesh):
    in_specs = (P("rows", "vecs"), P("rows", None, None, None), P("rows", None))
    out_specs = P("rows", "vecs")
    return jax.shard_map(shards, mesh=mesh, in_specs=in_specs, out_specs=out_specs, check_vma=False)
```

```python
import functools

import jax
import jax.numpy as jnp
from jax import lax
from jax.experimental import pallas as pl
from jax.experimental.pallas import tpu as pltpu
from jax.sharding import PartitionSpec as P

DEGREE = 4

filter_center = 0.25
filter_radius = 1.25

VMEM_LIMIT = 56 * 1024 * 1024


def factor_block(block, middle=None):
    size = block.shape[0]
    tiles = [block[8 * t : 8 * (t + 1), :] for t in range(size // 8)]
    lane = lax.broadcasted_iota(jnp.int32, (8, size), 1)
    sub = lax.broadcasted_iota(jnp.int32, (8, size), 0)

    def spread(array):
        return jnp.broadcast_to(array, (8, size))

    for first in range(size // 8):
        if middle and first == size // 16:
            middle()
        j = 8 * first
        each = range(8)
        at_any = jnp.logical_and(lane >= j, lane < j + 8)
        head = tiles[first]
        cols = [spread(head[:, j + a : j + a + 1]) for a in each]
        p = [[spread(cols[a][b : b + 1, :]) for a in range(b + 1)] for b in each]
        rows = [jnp.where(at_any, 0.0, spread(head[a : a + 1, :])) for a in each]
        rows = [jnp.where(lane == j + a, 1.0, rows[a]) for a in each]
        pairs, ready = [], []
        for a in range(0, 8, 2):
            b = a + 1
            det = p[a][a] * p[b][b] - p[b][a] * p[b][a]
            inv = 1.0 / det
            e_aa, e_ab, e_bb = p[b][b] * inv, p[b][a] * inv, p[a][a] * inv
            over = 1.0 / p[a][a]
            ready.append(rows[a] * lax.rsqrt(p[a][a]))
            ready.append((rows[b] - (p[b][a] * over) * rows[a]) * lax.rsqrt(det * over))
            mult = {}
            for c in range(b + 1, 8):
                mult[c, 0] = p[c][a] * e_aa - p[c][b] * e_ab
                mult[c, 1] = p[c][b] * e_bb - p[c][a] * e_ab
            for c in range(b + 1, 8):
                for d in range(b + 1, c + 1):
                    p[c][d] = p[c][d] - (mult[c, 0] * p[d][a] + mult[c, 1] * p[d][b])
            pairs.append((e_aa, e_ab, e_bb, mult, rows[a], rows[b]))
            for c in range(b + 1, 8):
                rows[c] = rows[c] - (mult[c, 0] * rows[a] + mult[c, 1] * rows[b])
        use = [None] * 8
        for number in reversed(range(4)):
            a, b = 2 * number, 2 * number + 1
            e_aa, e_ab, e_bb, mult, row_a, row_b = pairs[number]
            use[a] = e_aa * row_a - e_ab * row_b
            use[b] = e_bb * row_b - e_ab * row_a
            for c in range(b + 1, 8):
                use[a] = use[a] - mult[c, 0] * use[c]
                use[b] = use[b] - mult[c, 1] * use[c]
        for t in range(first + 1, size // 8):
            tile = tiles[t]
            cols = [spread(tile[:, j + a : j + a + 1]) for a in each]
            terms = [cols[a] * use[a] for a in each]
            while len(terms) > 1:
                terms = [x + y for x, y in zip(terms[::2], terms[1::2])]
            tiles[t] = jnp.where(at_any, 0.0, tile) - terms[0]
        top = ready[0]
        for a in range(1, 8):
            top = jnp.where(sub == a, ready[a], top)
        tiles[first] = top
    done = jnp.concatenate(tiles, axis=0)
    down = lax.broadcasted_iota(jnp.int32, (size, size), 0)
    across = lax.broadcasted_iota(jnp.int32, (size, size), 1)
    return jnp.where(across <= down, done, 0.0)


def halves(array):
    high = array.astype(jnp.bfloat16)
    return high, (array - high.astype(jnp.float32)).astype(jnp.bfloat16)


PLAIN = (((1,), (0,)), ((), ()))
TURNED = (((1,), (1,)), ((), ()))


def triple(left, right, dims):
    def one(a, b):
        return lax.dot_general(a, b, dims, preferred_element_type=jnp.float32)

    return one(left[0], right[0]) + (one(left[0], right[1]) + one(left[1], right[0]))


def gram_stages(rows, devices):
    stages, bit, held = [], 1, rows
    while bit < devices:
        halve = held % 16 == 0
        stages.append((bit, halve))
        held, bit = held // 2 if halve else held, bit * 2
    return stages


def flipped(index, bit):
    return index + bit - 2 * bit * lax.rem(index // bit, 2)


class Reduction:
    def __init__(self, stages, me, panel, total, landing, full, base, stage_sem, all_sem):
        self.me, self.panel, self.total, self.landing, self.full = me, panel, total, landing, full
        self.base, self.stage_sem, self.all_sem = base, stage_sem, all_sem
        self.near, self.over, self.side = flipped(panel, 1), flipped(panel, 2), panel // 2
        self.steps, self.shared = [], []
        start, held, taken = 0, total.shape[0], 0
        for bit, halve in stages:
            size = held // 2 if halve else held
            upper = lax.rem(me // bit, 2)
            keep = pl.multiple_of(start + upper * size, 8) if halve else start
            give = pl.multiple_of(start + (1 - upper) * size, 8) if halve else start
            self.steps.append((bit, size, keep, give, taken))
            start, held, taken = keep, size, taken + size
        self.start, self.held = start, held
        self.gathers = [n for n in reversed(range(len(stages))) if stages[n][1]]

    def reduce_copy(self, number):
        bit, size, _, give, taken = self.steps[number]
        return pltpu.make_async_remote_copy(
            src_ref=self.total.at[pl.ds(give, size)], dst_ref=self.landing.at[taken : taken + size],
            send_sem=self.stage_sem.at[0, number], recv_sem=self.stage_sem.at[1, number],
            device_id={"rows": flipped(self.me, bit)},
        )

    def reduce_start(self, number):
        if number < len(self.steps):
            self.reduce_copy(number).start()

    def reduce_finish(self, number):
        if number < len(self.steps):
            _, size, keep, _, taken = self.steps[number]
            self.reduce_copy(number).wait()
            self.total[pl.ds(keep, size), :] += self.landing[taken : taken + size, :]

    def piece(self, which, first, size):
        return self.full.at[which, pl.ds(pl.multiple_of(self.base + first, 8), size)]

    def hand(self, which, kind, number, first, size, peer):
        piece = self.piece(which, first, size)
        return pltpu.make_async_remote_copy(
            src_ref=piece, dst_ref=piece, send_sem=self.all_sem.at[0, kind, number],
            recv_sem=self.all_sem.at[1, kind, number], device_id={"vecs": peer},
        )

    def hands(self, number, kind):
        first, size = self.shared[number]
        which = self.over if kind == 2 else self.panel
        peer = self.near if kind else self.over
        return self.hand(which, kind, number, first, size, peer)

    def share(self, first, size):
        self.shared.append((first, size))
        number = len(self.shared) - 1

        @pl.when(self.side == 0)
        def _():
            self.hands(number, 0).start()

        self.hands(number, 1).start()

    def publish(self):
        rows = pl.ds(pl.multiple_of(self.base + self.start, 8), self.held)
        self.full[self.panel, rows, :] = self.total[pl.ds(self.start, self.held), :]
        self.share(self.start, self.held)

    def gather_copy(self, index):
        number = self.gathers[index]
        bit, size, keep, _, _ = self.steps[number]
        piece = self.piece(self.panel, keep, size)
        return pltpu.make_async_remote_copy(
            src_ref=piece, dst_ref=piece, send_sem=self.stage_sem.at[2, number],
            recv_sem=self.stage_sem.at[3, number], device_id={"rows": flipped(self.me, bit)},
        )

    def gather_start(self, index):
        if index < len(self.gathers):
            self.gather_copy(index).start()

    def gather_finish(self, index):
        if index < len(self.gathers):
            self.gather_copy(index).wait()
            _, size, _, give, _ = self.steps[self.gathers[index]]
            self.share(give, size)

    def settle(self):
        for number in range(len(self.shared)):

            @pl.when(self.side == 1)
            def _():
                self.hands(number, 0).wait_recv()
                self.hands(number, 2).start()

            @pl.when(self.side == 0)
            def _():
                self.hands(number, 0).wait_send()

            self.hands(number, 1).wait()

    def close(self):
        @pl.when(self.side == 1)
        def _():
            for number in range(len(self.shared)):
                self.hands(number, 2).wait()


def filter_kernel(
    near_stages, cross_stages, place_ref, vectors_ref, blocks_ref, sums_ref, block_ref, lead_ref,
    first_win, even_win, odd_win, tops, bottoms, even, odd, held,
    block, cross, near_acc, near_total, cross_total, full, near_landing, cross_landing, cross_in, work, lead,
    in_sem, send_sem, recv_sem, copy_sem, keep_sem, swap_sem, side_sem, x_sem, pass_sem, rest_sem, on_sem,
    near_stage_sem, near_all_sem, cross_stage_sem, cross_all_sem,
):
    me, count = lax.axis_index("rows"), lax.axis_size("rows")
    panel = lax.axis_index("vecs")
    core, side = lax.rem(panel, 2), panel // 2
    near, over = flipped(panel, 1), flipped(panel, 2)
    beyond = flipped(over, 1)
    block_rows, nnz = blocks_ref.shape[:2]
    wide = block.shape[3]
    short = wide // 2
    reach = block_rows // 4
    span, part = 2 * reach, reach // 2
    windows = [first_win, odd_win, even_win, odd_win]
    states = [None, even, odd, even]
    above, below = me < count - 1, me > 0

    peers = [{"vecs": near}, {"vecs": over}] + [{"rows": flipped(me, bit)} for bit, _ in near_stages]
    inside = jnp.logical_and(above, below)
    for peer in peers:
        pl.semaphore_signal(pltpu.get_barrier_semaphore(), 1, device_id=peer)

    @pl.when(inside)
    def _():
        other = me - 1 + 2 * lax.rem(me, 2)
        pl.semaphore_signal(pltpu.get_barrier_semaphore(), 1, device_id={"rows": other})

    pieces = [
        (vectors_ref, first_win),
        (vectors_ref.at[:span], tops[0][0].at[part:]),
        (vectors_ref.at[: reach + part], tops[0][1].at[reach:]),
        (vectors_ref.at[span:], bottoms[0][0].at[:span]),
        (vectors_ref.at[span + part :], bottoms[0][1].at[: reach + part]),
        (blocks_ref, held),
    ]
    fetches = [pltpu.make_async_copy(*pair, in_sem.at[n]) for n, pair in enumerate(pieces)]
    for fetch in fetches:
        fetch.start()

    @pl.when(inside)
    def _():
        pl.semaphore_wait(pltpu.get_barrier_semaphore(), len(peers) + 1)

    @pl.when(jnp.logical_not(inside))
    def _():
        pl.semaphore_wait(pltpu.get_barrier_semaphore(), len(peers))

    def to_lower(step, far):
        source = vectors_ref if step == 0 else windows[step]
        return pltpu.make_async_remote_copy(
            src_ref=source.at[far * part : (far + 1) * part],
            dst_ref=bottoms[step % 2][far].at[span:],
            send_sem=send_sem.at[0, far, step % 2], recv_sem=recv_sem.at[0, far, step % 2],
            device_id={"rows": me - 1},
        )

    def to_upper(step, far):
        source = vectors_ref if step == 0 else windows[step]
        first = block_rows - (far + 1) * part
        return pltpu.make_async_remote_copy(
            src_ref=source.at[first : first + part], dst_ref=tops[step % 2][far].at[:part],
            send_sem=send_sem.at[1, far, step % 2], recv_sem=recv_sem.at[1, far, step % 2],
            device_id={"rows": me + 1},
        )

    def join_bottom(step):
        close, far = bottoms[step % 2]
        return pltpu.make_async_copy(close.at[span:], far.at[reach + part : span], copy_sem.at[0])

    def join_top(step):
        close, far = tops[step % 2]
        return pltpu.make_async_copy(close.at[:part], far.at[part:reach], copy_sem.at[1])

    def compute(step, start, rows, window):
        slot = (step + 1) % 2
        for row in range(start, start + rows):
            left = jnp.concatenate([held[row, j] for j in range(nnz)], axis=1)
            right = jnp.concatenate([window[place_ref[row, j]] for j in range(nnz)], axis=0)
            acc = jnp.dot(left, right, preferred_element_type=jnp.float32)
            cur = first_win[row].astype(jnp.float32) if step == 0 else states[step][row]
            new = (acc - filter_center * cur) * (1.0 / filter_radius)
            if step == 1:
                new = 2.0 * new - first_win[row].astype(jnp.float32)
            elif step > 1:
                new = 2.0 * new - states[step - 1][row]
            rounded = new.astype(jnp.bfloat16)
            if step == DEGREE - 1:
                block[panel, row] = rounded
                continue
            windows[step + 1][row] = rounded
            states[step + 1][row] = new
            if row < span:
                tops[slot][0][row + part] = rounded
            if row < reach + part:
                tops[slot][1][row + reach] = rounded
            if row >= span:
                bottoms[slot][0][row - span] = rounded
            if row >= span + part:
                bottoms[slot][1][row - span - part] = rounded

    def send(which, start, size, sems, number, peer):
        piece = block.at[which, pl.ds(start, size)]
        return pltpu.make_async_remote_copy(
            src_ref=piece, dst_ref=piece, send_sem=sems.at[0, number],
            recv_sem=sems.at[1, number], device_id={"vecs": peer},
        )

    def part_start(half, number):
        return half * 3 * reach if number else reach + half * reach

    to_over = [send(panel, part_start(1 - side, n), reach, x_sem, n, over) for n in range(2)]
    passed = [send(over, part_start(side, n), reach, pass_sem, n, near) for n in range(2)]
    rest = [send(panel, part_start(0, n), reach, rest_sem, n, over) for n in range(2)]
    onward = [send(over, part_start(0, n), reach, on_sem, n, near) for n in range(2)]
    to_near = [
        send(panel, first, size, side_sem, n, near)
        for n, (first, size) in enumerate(((reach, span), (3 * reach, reach), (0, reach)))
    ]
    contract = (((0,), (0,)), ((), ()))

    def product(left, right):
        return lax.dot_general(left, right, contract, preferred_element_type=jnp.float32)

    def rows_of(which, start, size):
        return block[which, pl.ds(start, size)].reshape(size * block.shape[2], wide)

    def add_own(start, size):
        @pl.loop(0, size // part)
        def _(index):
            own = rows_of(panel, start + index * part, part)
            near_acc[:wide, :] += product(own, own)

    def add_near(start, size):
        @pl.loop(0, size // part)
        def _(index):
            own = rows_of(panel, start + index * part, part)
            beside = rows_of(near, start + index * part, part)

            @pl.when(core == 0)
            def _():
                near_acc[wide:, :] += product(beside[:, :short], own)

            @pl.when(core == 1)
            def _():
                near_acc[wide:, :] += product(own[:, short:], beside)

    def add_across(number):
        @pl.loop(0, 2)
        def _(index):
            start = part_start(side, number) + index * part
            own, there = rows_of(panel, start, part), rows_of(over, start, part)

            @pl.when(side == 0)
            def _():
                cross[core] += product(there, own)

            @pl.when(side == 1)
            def _():
                cross[core] += product(own, there)
                cross[1 - core] += product(rows_of(near, start, part), there)

    def add_beyond(number):
        @pl.when(side == 0)
        def _():
            @pl.loop(0, 2)
            def _(index):
                start = part_start(0, number) + index * part
                cross[1 - core] += product(rows_of(beyond, start, part), rows_of(panel, start, part))

    @pl.when(below)
    def _():
        to_lower(0, 0).start()

    @pl.when(above)
    def _():
        to_upper(0, 0).start()

    near_acc[...] = jnp.zeros_like(near_acc)
    cross[...] = jnp.zeros_like(cross)
    for fetch in fetches:
        fetch.wait()

    for step in range(DEGREE):
        last = step == DEGREE - 1
        compute(step, reach, reach, windows[step])
        compute(step, span, reach, windows[step])
        if last:
            to_over[0].start()
            to_near[0].start()

        @pl.when(below)
        def _():
            to_lower(step, 0).wait_send()
            to_lower(step, 1).start()

        @pl.when(above)
        def _():
            to_upper(step, 0).wait_send()
            to_upper(step, 1).start()

        if last:
            add_own(reach, span)

        @pl.when(above)
        def _():
            to_lower(step, 0).wait_recv()
            join_bottom(step).start()

        compute(step, 3 * reach, part, bottoms[step % 2][0])

        @pl.when(below)
        def _():
            to_upper(step, 0).wait_recv()
            join_top(step).start()

        compute(step, part, part, tops[step % 2][0])
        if last:
            to_near[0].wait()
            add_near(reach, span)
            to_over[0].wait()
            passed[0].start()

            @pl.when(side == 0)
            def _():
                rest[0].start()

            add_across(0)
            passed[0].wait()
            add_beyond(0)

        @pl.when(above)
        def _():
            join_bottom(step).wait()
            to_lower(step, 1).wait_recv()

        compute(step, 3 * reach + part, part, bottoms[step % 2][1])
        if last:
            to_near[1].start()

            @pl.when(side == 0)
            def _():
                to_over[1].start()
        else:

            @pl.when(above)
            def _():
                to_upper(step + 1, 0).start()

        @pl.when(below)
        def _():
            join_top(step).wait()
            to_upper(step, 1).wait_recv()

        compute(step, 0, part, tops[step % 2][1])
        if last:
            to_near[2].start()

            @pl.when(side == 1)
            def _():
                to_over[1].start()
        else:

            @pl.when(below)
            def _():
                to_lower(step + 1, 0).start()

        @pl.when(below)
        def _():
            to_lower(step, 1).wait_send()

        @pl.when(above)
        def _():
            to_upper(step, 1).wait_send()

    keep_own = pltpu.make_async_copy(block.at[panel], block_ref.at[panel], keep_sem.at[0])
    keep_own.start()
    add_own(3 * reach, reach)
    add_own(0, reach)
    to_near[1].wait()
    add_near(3 * reach, reach)
    to_near[2].wait()
    add_near(0, reach)
    keep_near = pltpu.make_async_copy(block.at[near], block_ref.at[near], keep_sem.at[1])
    keep_near.start()

    quarter = short // 2
    near_total[:short, :short] = near_acc[:short, :short]
    near_total[:short, short:] = near_acc[short:wide, short:]
    near_total[short : short + quarter, :short] = near_acc[short : short + quarter, :short]
    near_total[short : short + quarter, short:] = near_acc[short + quarter : wide, :short]
    near_total[short + quarter :, :] = near_acc[wide:, :]
    shape = (me, panel)
    near_sum = Reduction(near_stages, *shape, near_total, near_landing, full, 0, near_stage_sem, near_all_sem)
    cross_sum = Reduction(
        cross_stages, *shape, cross_total, cross_landing, full, near_total.shape[0], cross_stage_sem, cross_all_sem
    )
    stages = len(near_stages)
    ahead = min(stages, 3)
    near_sum.reduce_start(0)
    for number in range(stages):
        near_sum.reduce_finish(number)
        near_sum.reduce_start(number + 1)
    near_sum.publish()
    near_sum.gather_start(0)
    to_over[1].wait()
    passed[1].start()
    add_across(1)
    passed[1].wait()
    add_beyond(1)
    swap = pltpu.make_async_remote_copy(
        src_ref=cross.at[1 - side], dst_ref=cross_in,
        send_sem=swap_sem.at[0], recv_sem=swap_sem.at[1], device_id={"vecs": over},
    )
    swap.start()
    near_sum.gather_finish(0)
    near_sum.gather_start(1)
    swap.wait()
    cross_total[...] = cross[side] + cross_in[...]
    cross_sum.reduce_start(0)
    for number in range(1, stages):
        near_sum.gather_finish(number)
        near_sum.gather_start(number + 1)
        if number == 1:
            cross_sum.reduce_finish(0)
            cross_sum.reduce_start(1)
    near_sum.settle()
    near_sum.close()

    @pl.when(side == 0)
    def _():
        rest[0].wait_send()
        rest[1].start()

    def gather_next(number):
        cross_sum.gather_finish(number)
        cross_sum.gather_start(number + 1)

    def reduced():
        cross_sum.reduce_finish(2)
        for number in range(3, stages):
            cross_sum.reduce_start(number)
            cross_sum.reduce_finish(number)
        cross_sum.publish()
        cross_sum.gather_start(0)

    def reduce_second():
        cross_sum.reduce_finish(1)
        cross_sum.reduce_start(2)

    def pass_rest():
        @pl.when(side == 1)
        def _():
            for copy, pass_on in zip(rest, onward):
                copy.wait_recv()
                pass_on.start()

    later = [functools.partial(gather_next, n) for n in range(1, len(cross_sum.gathers))]
    actions = [
        [reduce_second], [reduced], [functools.partial(gather_next, 0)], later[:1], later[1:], [],
        [pass_rest], [cross_sum.settle],
    ]
    fill_lower(full, 0, work)
    square_factor(work, lead, block.shape[2], actions)
    lead_copy = pltpu.make_async_copy(lead, lead_ref, copy_sem.at[0])
    lead_copy.start()
    keep_own.wait()
    keep_near.wait()
    keep_over = pltpu.make_async_copy(block.at[over], block_ref.at[over], keep_sem.at[0])
    keep_beyond = pltpu.make_async_copy(block.at[beyond], block_ref.at[beyond], keep_sem.at[1])

    @pl.when(side == 0)
    def _():
        rest[1].wait_send()

    @pl.when(side == 1)
    def _():
        keep_over.start()

    cross_sum.close()
    low_sums = pltpu.make_async_copy(full.at[:2], sums_ref.at[:2], keep_sem.at[2])
    high_sums = pltpu.make_async_copy(full.at[2:], sums_ref.at[2:], keep_sem.at[3])
    low_sums.start()

    @pl.when(side == 1)
    def _():
        high_sums.start()
        onward[0].wait()
        onward[1].wait()
        keep_beyond.start()
        keep_over.wait()
        keep_beyond.wait()
        high_sums.wait()

    low_sums.wait()
    lead_copy.wait()


def filtered_sums(vectors, blocks, columns):
    rows, width = vectors.shape
    block_rows, nnz, size_b = blocks.shape[:3]
    panels, devices = lax.axis_size("vecs"), lax.axis_size("rows")
    reach = block_rows // 4
    part = reach // 2
    near_rows, cross_rows = width + width // 4, width
    near_stages, cross_stages = gram_stages(near_rows, devices), gram_stages(cross_rows, devices)
    steps = len(near_stages)
    row = lax.broadcasted_iota(jnp.int32, columns.shape, 0)
    shift = jnp.zeros_like(columns)
    for start, amount in (
        (0, reach), (part, part), (reach, 0), (3 * reach, -2 * reach), (3 * reach + part, -2 * reach - part),
    ):
        shift = jnp.where(row >= start, amount, shift)
    place = columns - lax.axis_index("rows") * block_rows + shift
    window = pltpu.VMEM((block_rows, size_b, width), jnp.bfloat16)
    side = pltpu.VMEM((2 * reach + part, size_b, width), jnp.bfloat16)
    state = pltpu.VMEM((block_rows, size_b, width), jnp.float32)
    anywhere = pl.BlockSpec(memory_space=pl.ANY)
    dma = pltpu.SemaphoreType.DMA

    def single(tall):
        return pltpu.VMEM((tall, width), jnp.float32)

    def kernel(*refs):
        inputs, wins, refs = refs[:6], refs[6:9], refs[9:]
        tops = ((refs[0], refs[1]), (refs[2], refs[3]))
        bottoms = ((refs[4], refs[5]), (refs[6], refs[7]))
        filter_kernel(near_stages, cross_stages, *inputs, *wins, tops, bottoms, *refs[8:])

    sums, block, lead = pl.pallas_call(
        kernel,
        out_shape=[
            jax.ShapeDtypeStruct((panels, near_rows + cross_rows, width), jnp.float32),
            jax.ShapeDtypeStruct((panels, block_rows, size_b, width), jnp.bfloat16),
            jax.ShapeDtypeStruct((2 * width, 2 * width), jnp.float32),
        ],
        in_specs=[pl.BlockSpec(memory_space=pltpu.SMEM), anywhere, anywhere],
        out_specs=[anywhere] * 3,
        scratch_shapes=[window] * 3 + [side] * 8 + [state] * 2 + [
            pltpu.VMEM(blocks.shape, jnp.bfloat16),
            pltpu.VMEM((panels, block_rows, size_b, width), jnp.bfloat16),
            pltpu.VMEM((2, width, width), jnp.float32),
            single(width + width // 2), single(near_rows), single(cross_rows),
            pltpu.VMEM((panels, near_rows + cross_rows, width), jnp.float32),
            single(2 * near_rows), single(2 * cross_rows), single(width),
            pltpu.VMEM((2 * width, 2 * width), jnp.float32),
            pltpu.VMEM((2 * width, 2 * width), jnp.float32),
            dma((6,)), dma((2, 2, 2)), dma((2, 2, 2)), dma((2,)), dma((4,)), dma((2,)),
            dma((2, 3)), dma((2, 2)), dma((2, 2)), dma((2, 2)), dma((2, 2)),
            dma((4, steps)), dma((2, 3, steps + 1)), dma((4, steps)), dma((2, 3, steps + 1)),
        ],
        compiler_params=pltpu.CompilerParams(
            vmem_limit_bytes=VMEM_LIMIT, collective_id=0, has_side_effects=True
        ),
    )(place, vectors.reshape(block_rows, size_b, width), blocks)
    return sums, block.reshape(panels, rows, width), lead


def scales(diagonal):
    wide = diagonal.shape[0]
    down = lax.broadcasted_iota(jnp.int32, (wide, wide), 0)
    across = lax.broadcasted_iota(jnp.int32, (wide, wide), 1)
    kept = jnp.where(down == across, diagonal, 0.0)
    sums = jnp.sum(kept, axis=0, keepdims=True)
    return lax.rsqrt(jnp.sum(kept, axis=1, keepdims=True)), lax.rsqrt(sums), sums


def fill_lower(full, first, work):
    wide = full.shape[2]
    short, quarter = wide // 2, wide // 4
    parts = []
    for n in range(2):
        ends = [scales(full[first + n, :short, m * short : (m + 1) * short]) for m in range(2)]
        parts.append([jnp.concatenate([end[axis] for end in ends], axis=min(axis, 1)) for axis in range(3)])
        start = n * wide
        for m in range(2):
            own = slice(start + m * short, start + (m + 1) * short)
            work[own, own] = full[first + n, :short, m * short : (m + 1) * short] * ends[m][0] * ends[m][1]
            rows = slice(start + short + m * quarter, start + short + (m + 1) * quarter)
            part = full[first + n, short : short + quarter, m * short : (m + 1) * short]
            down = ends[1][0][m * quarter : (m + 1) * quarter, :]
            work[rows, start : start + short] = part * down * ends[0][1]
    for n in range(2):
        rows = slice(n * short, (n + 1) * short)
        below = wide + n * short
        work[below : below + short, :wide] = (
            full[first + n, short + quarter : wide + quarter, :] * parts[1][0][rows, :] * parts[0][1]
        )
    return parts


def square_factor(work, inverse, size, actions=()):
    full = work.shape[0]
    count = full // size
    waiting = list(actions)

    def act():
        for action in waiting.pop(0) if waiting else []:
            action()

    def span(c):
        return slice(c * size, (c + 1) * size)

    done = factor_block(work[span(0), span(0)], act)
    act()
    for c in range(count):
        own = span(c)
        lower = halves(done)
        inverse[own, own] = done
        if c + 1 < count:
            inverse[own, (c + 1) * size :] = jnp.zeros((size, full - (c + 1) * size), jnp.float32)
            below = slice((c + 1) * size, full)
            column = triple(halves(work[below, own]), lower, TURNED)
            pieces = halves(column)
            top = (pieces[0][:size], pieces[1][:size])
            following = work[span(c + 1), span(c + 1)] - triple(top, top, TURNED)
        if c > 0:
            known = triple(lower, halves(work[own, : c * size]), PLAIN)
            inverse[own, : c * size] = known
        if c + 1 < count:
            done = factor_block(following, act)
            act()
            work[below, own] = -triple(pieces, lower, PLAIN)
            if c > 0:
                work[below, : c * size] -= triple(pieces, halves(known), PLAIN)
            for j in range(c + 1, count):
                first = max(j, c + 2)
                if first == count:
                    continue
                rows = slice((first - c - 1) * size, (count - c - 1) * size)
                cols = slice((j - c - 1) * size, (j - c) * size)
                work[first * size :, span(j)] -= triple(
                    (pieces[0][rows], pieces[1][rows]), (pieces[0][cols], pieces[1][cols]), TURNED
                )


def finish_kernel(
    size, total_rows, sums_ref, lead_ref, block_ref, out_ref,
    work, inverse, cross, mixed, factor, block, result, in_sem, out_sem,
):
    panels, _, wide = sums_ref.shape
    short = wide // 2
    mine = lax.axis_index("vecs")
    side = mine // 2

    def fetch(panel):
        return pltpu.make_async_copy(block_ref.at[panel], block.at[panel], in_sem.at[panel])

    for panel in range(panels):

        @pl.when(panel <= mine)
        def _():
            fetch(panel).start()

    def scaled(sums):
        return lax.rsqrt(sums * (1.0 / total_rows))

    parts = []
    for panel in range(2):
        for m in range(2):
            parts.append(scales(sums_ref[panel, :short, m * short : (m + 1) * short]))
    left_scale = jnp.concatenate([scaled(part[2]) for part in parts], axis=1)
    along = [jnp.concatenate([part[1] for part in parts[2 * n : 2 * n + 2]], axis=1) for n in range(2)]

    def keep(rows, first):
        high, low = halves(rows)
        factor[0, :, first : first + 2 * wide] = high
        factor[1, :, first : first + 2 * wide] = low

    @pl.when(side == 0)
    def _():
        keep(lead_ref[pl.ds(pl.multiple_of(mine * wide, wide), wide), :] * left_scale, 0)

    @pl.when(side == 1)
    def _():
        later = fill_lower(sums_ref, 2, work)
        for panel in range(panels):
            core, row = panel % 2, panel // 2
            cross[row * wide : (row + 1) * wide, core * wide : (core + 1) * wide] = (
                sums_ref[panel, wide + short // 2 :, :] * later[row][0] * along[core]
            )
        lead = halves(lead_ref[...])
        ratio = halves(triple(halves(cross[...]), lead, TURNED))
        upper = (ratio[0][:wide], ratio[1][:wide])
        lower = (ratio[0][wide:], ratio[1][wide:])
        work[:wide, :wide] -= triple(upper, upper, TURNED)
        work[wide:, :] -= triple(lower, ratio, TURNED)
        mixed[...] = triple(ratio, lead, PLAIN)
        square_factor(work, inverse, size)
        own = inverse[pl.ds(pl.multiple_of((mine - 2) * wide, wide), wide), :]
        keep(-triple(halves(own), halves(mixed[...]), PLAIN) * left_scale, 0)
        keep(own * jnp.concatenate([scaled(part[2]) for part in later], axis=1), 2 * wide)

    tiles = out_sem.shape[0]
    tile = block.shape[1] // tiles

    def store(index):
        rows = pl.ds(pl.multiple_of(index * tile, tile), tile)
        return pltpu.make_async_copy(result.at[rows], out_ref.at[rows], out_sem.at[index])

    for number in range(1, panels + 1):

        @pl.when(mine == number - 1)
        def _():
            for panel in range(number):
                fetch(panel).wait()
            deep = number * wide
            right = jnp.concatenate([factor[0, :, :deep], factor[1, :, :deep]], axis=1)

            @pl.loop(0, tiles)
            def _(index):
                rows = pl.ds(pl.multiple_of(index * tile, tile), tile)
                left = jnp.concatenate([block[panel, rows, :] for panel in range(number)] * 2, axis=1)
                result[rows, :] = lax.dot_general(
                    left, right, TURNED, preferred_element_type=jnp.float32
                )
                store(index).start()

    for index in range(tiles):
        store(index).wait()


def finish(sums, block, lead, total_rows):
    panels, rows, wide = block.shape
    size = 128
    tiles = 4
    anywhere = pl.BlockSpec(memory_space=pl.ANY)
    near = pl.BlockSpec(memory_space=pltpu.VMEM)
    square = pltpu.VMEM((2 * wide, 2 * wide), jnp.float32)
    return pl.pallas_call(
        functools.partial(finish_kernel, size, total_rows),
        out_shape=jax.ShapeDtypeStruct((rows, wide), jnp.float32),
        in_specs=[near, near, anywhere],
        out_specs=anywhere,
        scratch_shapes=[square] * 4 + [
            pltpu.VMEM((2, wide, panels * wide), jnp.bfloat16),
            pltpu.VMEM((panels, rows, wide), jnp.bfloat16),
            pltpu.VMEM((rows, wide), jnp.float32),
            pltpu.SemaphoreType.DMA((panels,)),
            pltpu.SemaphoreType.DMA((tiles,)),
        ],
        compiler_params=pltpu.CompilerParams(vmem_limit_bytes=VMEM_LIMIT),
    )(sums, lead, block)


def shards(vectors, blocks, columns):
    total_rows = vectors.shape[0] * lax.axis_size("rows")
    sums, block, lead = filtered_sums(vectors, blocks, columns)
    return finish(sums, block, lead, total_rows)


def solution(mesh):
    in_specs = (P("rows", "vecs"), P("rows", None, None, None), P("rows", None))
    out_specs = P("rows", "vecs")
    return jax.shard_map(shards, mesh=mesh, in_specs=in_specs, out_specs=out_specs, check_vma=False)
```

```python
import functools

import jax
import jax.numpy as jnp
from jax import lax
from jax.experimental import pallas as pl
from jax.experimental.pallas import tpu as pltpu
from jax.sharding import PartitionSpec as P

DEGREE = 4

filter_center = 0.25
filter_radius = 1.25

VMEM_LIMIT = 56 * 1024 * 1024


def factor_block(block, middle=None):
    size = block.shape[0]
    tiles = [block[8 * t : 8 * (t + 1), :] for t in range(size // 8)]
    lane = lax.broadcasted_iota(jnp.int32, (8, size), 1)
    sub = lax.broadcasted_iota(jnp.int32, (8, size), 0)

    def spread(array):
        return jnp.broadcast_to(array, (8, size))

    for first in range(size // 8):
        if middle and first == size // 16:
            middle()
        j = 8 * first
        each = range(8)
        at_any = jnp.logical_and(lane >= j, lane < j + 8)
        head = tiles[first]
        cols = [spread(head[:, j + a : j + a + 1]) for a in each]
        p = [[spread(cols[a][b : b + 1, :]) for a in range(b + 1)] for b in each]
        rows = [jnp.where(at_any, 0.0, spread(head[a : a + 1, :])) for a in each]
        rows = [jnp.where(lane == j + a, 1.0, rows[a]) for a in each]
        pairs, ready = [], []
        for a in range(0, 8, 2):
            b = a + 1
            det = p[a][a] * p[b][b] - p[b][a] * p[b][a]
            inv = 1.0 / det
            e_aa, e_ab, e_bb = p[b][b] * inv, p[b][a] * inv, p[a][a] * inv
            over = 1.0 / p[a][a]
            ready.append(rows[a] * lax.rsqrt(p[a][a]))
            ready.append((rows[b] - (p[b][a] * over) * rows[a]) * lax.rsqrt(det * over))
            mult = {}
            for c in range(b + 1, 8):
                mult[c, 0] = p[c][a] * e_aa - p[c][b] * e_ab
                mult[c, 1] = p[c][b] * e_bb - p[c][a] * e_ab
            for c in range(b + 1, 8):
                for d in range(b + 1, c + 1):
                    p[c][d] = p[c][d] - (mult[c, 0] * p[d][a] + mult[c, 1] * p[d][b])
            pairs.append((e_aa, e_ab, e_bb, mult, rows[a], rows[b]))
            for c in range(b + 1, 8):
                rows[c] = rows[c] - (mult[c, 0] * rows[a] + mult[c, 1] * rows[b])
        use = [None] * 8
        for number in reversed(range(4)):
            a, b = 2 * number, 2 * number + 1
            e_aa, e_ab, e_bb, mult, row_a, row_b = pairs[number]
            use[a] = e_aa * row_a - e_ab * row_b
            use[b] = e_bb * row_b - e_ab * row_a
            for c in range(b + 1, 8):
                use[a] = use[a] - mult[c, 0] * use[c]
                use[b] = use[b] - mult[c, 1] * use[c]
        for t in range(first + 1, size // 8):
            tile = tiles[t]
            cols = [spread(tile[:, j + a : j + a + 1]) for a in each]
            terms = [cols[a] * use[a] for a in each]
            while len(terms) > 1:
                terms = [x + y for x, y in zip(terms[::2], terms[1::2])]
            tiles[t] = jnp.where(at_any, 0.0, tile) - terms[0]
        top = ready[0]
        for a in range(1, 8):
            top = jnp.where(sub == a, ready[a], top)
        tiles[first] = top
    done = jnp.concatenate(tiles, axis=0)
    down = lax.broadcasted_iota(jnp.int32, (size, size), 0)
    across = lax.broadcasted_iota(jnp.int32, (size, size), 1)
    return jnp.where(across <= down, done, 0.0)


def halves(array):
    high = array.astype(jnp.bfloat16)
    return high, (array - high.astype(jnp.float32)).astype(jnp.bfloat16)


PLAIN = (((1,), (0,)), ((), ()))
TURNED = (((1,), (1,)), ((), ()))


def triple(left, right, dims):
    def one(a, b):
        return lax.dot_general(a, b, dims, preferred_element_type=jnp.float32)

    return one(left[0], right[0]) + (one(left[0], right[1]) + one(left[1], right[0]))


def gram_stages(rows, devices):
    stages, bit, held = [], 1, rows
    while bit < devices:
        halve = held % 16 == 0
        stages.append((bit, halve))
        held, bit = held // 2 if halve else held, bit * 2
    return stages


def flipped(index, bit):
    return index + bit - 2 * bit * lax.rem(index // bit, 2)


class Reduction:
    def __init__(self, stages, me, panel, total, landing, full, base, stage_sem, all_sem):
        self.me, self.panel, self.total, self.landing, self.full = me, panel, total, landing, full
        self.base, self.stage_sem, self.all_sem = base, stage_sem, all_sem
        self.near, self.over, self.side = flipped(panel, 1), flipped(panel, 2), panel // 2
        self.steps, self.shared = [], []
        start, held, taken = 0, total.shape[0], 0
        for bit, halve in stages:
            size = held // 2 if halve else held
            upper = lax.rem(me // bit, 2)
            keep = pl.multiple_of(start + upper * size, 8) if halve else start
            give = pl.multiple_of(start + (1 - upper) * size, 8) if halve else start
            self.steps.append((bit, size, keep, give, taken))
            start, held, taken = keep, size, taken + size
        self.start, self.held = start, held
        self.gathers = [n for n in reversed(range(len(stages))) if stages[n][1]]

    def reduce_copy(self, number):
        bit, size, _, give, taken = self.steps[number]
        return pltpu.make_async_remote_copy(
            src_ref=self.total.at[pl.ds(give, size)], dst_ref=self.landing.at[taken : taken + size],
            send_sem=self.stage_sem.at[0, number], recv_sem=self.stage_sem.at[1, number],
            device_id={"rows": flipped(self.me, bit)},
        )

    def reduce_start(self, number):
        if number < len(self.steps):
            self.reduce_copy(number).start()

    def reduce_finish(self, number):
        if number < len(self.steps):
            _, size, keep, _, taken = self.steps[number]
            self.reduce_copy(number).wait()
            self.total[pl.ds(keep, size), :] += self.landing[taken : taken + size, :]

    def piece(self, which, first, size):
        return self.full.at[which, pl.ds(pl.multiple_of(self.base + first, 8), size)]

    def hand(self, which, kind, number, first, size, peer):
        piece = self.piece(which, first, size)
        return pltpu.make_async_remote_copy(
            src_ref=piece, dst_ref=piece, send_sem=self.all_sem.at[0, kind, number],
            recv_sem=self.all_sem.at[1, kind, number], device_id={"vecs": peer},
        )

    def hands(self, number, kind):
        first, size = self.shared[number]
        which = self.over if kind == 2 else self.panel
        peer = self.near if kind else self.over
        return self.hand(which, kind, number, first, size, peer)

    def share(self, first, size):
        self.shared.append((first, size))
        number = len(self.shared) - 1

        @pl.when(self.side == 0)
        def _():
            self.hands(number, 0).start()

        self.hands(number, 1).start()

    def publish(self):
        rows = pl.ds(pl.multiple_of(self.base + self.start, 8), self.held)
        self.full[self.panel, rows, :] = self.total[pl.ds(self.start, self.held), :]
        self.share(self.start, self.held)

    def gather_copy(self, index):
        number = self.gathers[index]
        bit, size, keep, _, _ = self.steps[number]
        piece = self.piece(self.panel, keep, size)
        return pltpu.make_async_remote_copy(
            src_ref=piece, dst_ref=piece, send_sem=self.stage_sem.at[2, number],
            recv_sem=self.stage_sem.at[3, number], device_id={"rows": flipped(self.me, bit)},
        )

    def gather_start(self, index):
        if index < len(self.gathers):
            self.gather_copy(index).start()

    def gather_finish(self, index):
        if index < len(self.gathers):
            self.gather_copy(index).wait()
            _, size, _, give, _ = self.steps[self.gathers[index]]
            self.share(give, size)

    def settle(self):
        for number in range(len(self.shared)):

            @pl.when(self.side == 1)
            def _():
                self.hands(number, 0).wait_recv()
                self.hands(number, 2).start()

            @pl.when(self.side == 0)
            def _():
                self.hands(number, 0).wait_send()

            self.hands(number, 1).wait()

    def close(self):
        @pl.when(self.side == 1)
        def _():
            for number in range(len(self.shared)):
                self.hands(number, 2).wait()


def filter_kernel(
    near_stages, cross_stages, place_ref, vectors_ref, blocks_ref, sums_ref, block_ref, lead_ref,
    first_win, even_win, odd_win, tops, bottoms, even, odd, held,
    block, cross, near_acc, near_total, cross_total, full, near_landing, cross_landing, cross_in, work, lead,
    in_sem, send_sem, recv_sem, copy_sem, keep_sem, swap_sem, side_sem, x_sem, pass_sem, rest_sem, on_sem,
    near_stage_sem, near_all_sem, cross_stage_sem, cross_all_sem,
):
    me, count = lax.axis_index("rows"), lax.axis_size("rows")
    panel = lax.axis_index("vecs")
    core, side = lax.rem(panel, 2), panel // 2
    near, over = flipped(panel, 1), flipped(panel, 2)
    beyond = flipped(over, 1)
    block_rows, nnz = blocks_ref.shape[:2]
    wide = block.shape[3]
    short = wide // 2
    reach = block_rows // 4
    span, part = 2 * reach, reach // 2
    windows = [first_win, odd_win, even_win, odd_win]
    states = [None, even, odd, even]
    above, below = me < count - 1, me > 0

    peers = [{"vecs": near}, {"vecs": over}] + [{"rows": flipped(me, bit)} for bit, _ in near_stages]
    inside = jnp.logical_and(above, below)
    for peer in peers:
        pl.semaphore_signal(pltpu.get_barrier_semaphore(), 1, device_id=peer)

    @pl.when(inside)
    def _():
        other = me - 1 + 2 * lax.rem(me, 2)
        pl.semaphore_signal(pltpu.get_barrier_semaphore(), 1, device_id={"rows": other})

    pieces = [
        (vectors_ref, first_win),
        (vectors_ref.at[:span], tops[0][0].at[part:]),
        (vectors_ref.at[: reach + part], tops[0][1].at[reach:]),
        (vectors_ref.at[span:], bottoms[0][0].at[:span]),
        (vectors_ref.at[span + part :], bottoms[0][1].at[: reach + part]),
        (blocks_ref, held),
    ]
    fetches = [pltpu.make_async_copy(*pair, in_sem.at[n]) for n, pair in enumerate(pieces)]
    for fetch in fetches:
        fetch.start()

    @pl.when(inside)
    def _():
        pl.semaphore_wait(pltpu.get_barrier_semaphore(), len(peers) + 1)

    @pl.when(jnp.logical_not(inside))
    def _():
        pl.semaphore_wait(pltpu.get_barrier_semaphore(), len(peers))

    def to_lower(step, far):
        source = vectors_ref if step == 0 else windows[step]
        return pltpu.make_async_remote_copy(
            src_ref=source.at[far * part : (far + 1) * part],
            dst_ref=bottoms[step % 2][far].at[span:],
            send_sem=send_sem.at[0, far, step % 2], recv_sem=recv_sem.at[0, far, step % 2],
            device_id={"rows": me - 1},
        )

    def to_upper(step, far):
        source = vectors_ref if step == 0 else windows[step]
        first = block_rows - (far + 1) * part
        return pltpu.make_async_remote_copy(
            src_ref=source.at[first : first + part], dst_ref=tops[step % 2][far].at[:part],
            send_sem=send_sem.at[1, far, step % 2], recv_sem=recv_sem.at[1, far, step % 2],
            device_id={"rows": me + 1},
        )

    def join_bottom(step):
        close, far = bottoms[step % 2]
        return pltpu.make_async_copy(close.at[span:], far.at[reach + part : span], copy_sem.at[0])

    def join_top(step):
        close, far = tops[step % 2]
        return pltpu.make_async_copy(close.at[:part], far.at[part:reach], copy_sem.at[1])

    def compute(step, start, rows, window):
        slot = (step + 1) % 2
        for row in range(start, start + rows):
            left = jnp.concatenate([held[row, j] for j in range(nnz)], axis=1)
            right = jnp.concatenate([window[place_ref[row, j]] for j in range(nnz)], axis=0)
            acc = jnp.dot(left, right, preferred_element_type=jnp.float32)
            cur = first_win[row].astype(jnp.float32) if step == 0 else states[step][row]
            new = (acc - filter_center * cur) * (1.0 / filter_radius)
            if step == 1:
                new = 2.0 * new - first_win[row].astype(jnp.float32)
            elif step > 1:
                new = 2.0 * new - states[step - 1][row]
            rounded = new.astype(jnp.bfloat16)
            if step == DEGREE - 1:
                block[panel, row] = rounded
                continue
            windows[step + 1][row] = rounded
            states[step + 1][row] = new
            if row < span:
                tops[slot][0][row + part] = rounded
            if row < reach + part:
                tops[slot][1][row + reach] = rounded
            if row >= span:
                bottoms[slot][0][row - span] = rounded
            if row >= span + part:
                bottoms[slot][1][row - span - part] = rounded

    def send(which, start, size, sems, number, peer):
        piece = block.at[which, pl.ds(start, size)]
        return pltpu.make_async_remote_copy(
            src_ref=piece, dst_ref=piece, send_sem=sems.at[0, number],
            recv_sem=sems.at[1, number], device_id={"vecs": peer},
        )

    def part_start(half, number):
        return half * 3 * reach if number else reach + half * reach

    to_over = [send(panel, part_start(1 - side, n), reach, x_sem, n, over) for n in range(2)]
    passed = [send(over, part_start(side, n), reach, pass_sem, n, near) for n in range(2)]
    rest = [send(panel, part_start(0, n), reach, rest_sem, n, over) for n in range(2)]
    onward = [send(over, part_start(0, n), reach, on_sem, n, near) for n in range(2)]
    to_near = [
        send(panel, first, size, side_sem, n, near)
        for n, (first, size) in enumerate(((reach, span), (3 * reach, reach), (0, reach)))
    ]
    contract = (((0,), (0,)), ((), ()))

    def product(left, right):
        return lax.dot_general(left, right, contract, preferred_element_type=jnp.float32)

    def rows_of(which, start, size):
        return block[which, pl.ds(start, size)].reshape(size * block.shape[2], wide)

    def add_own(start, size):
        @pl.loop(0, size // part)
        def _(index):
            own = rows_of(panel, start + index * part, part)
            near_acc[:wide, :] += product(own, own)

    def add_near(start, size):
        @pl.loop(0, size // part)
        def _(index):
            own = rows_of(panel, start + index * part, part)
            beside = rows_of(near, start + index * part, part)

            @pl.when(core == 0)
            def _():
                near_acc[wide:, :] += product(beside[:, :short], own)

            @pl.when(core == 1)
            def _():
                near_acc[wide:, :] += product(own[:, short:], beside)

    def add_across(number):
        @pl.loop(0, 2)
        def _(index):
            start = part_start(side, number) + index * part
            own, there = rows_of(panel, start, part), rows_of(over, start, part)

            @pl.when(side == 0)
            def _():
                cross[core] += product(there, own)

            @pl.when(side == 1)
            def _():
                cross[core] += product(own, there)
                cross[1 - core] += product(rows_of(near, start, part), there)

    def add_beyond(number):
        @pl.when(side == 0)
        def _():
            @pl.loop(0, 2)
            def _(index):
                start = part_start(0, number) + index * part
                cross[1 - core] += product(rows_of(beyond, start, part), rows_of(panel, start, part))

    @pl.when(below)
    def _():
        to_lower(0, 0).start()

    @pl.when(above)
    def _():
        to_upper(0, 0).start()

    near_acc[...] = jnp.zeros_like(near_acc)
    cross[...] = jnp.zeros_like(cross)
    for fetch in fetches:
        fetch.wait()

    for step in range(DEGREE):
        last = step == DEGREE - 1
        compute(step, reach, reach, windows[step])
        compute(step, span, reach, windows[step])
        if last:
            to_over[0].start()
            to_near[0].start()

        @pl.when(below)
        def _():
            to_lower(step, 0).wait_send()
            to_lower(step, 1).start()

        @pl.when(above)
        def _():
            to_upper(step, 0).wait_send()
            to_upper(step, 1).start()

        if last:
            add_own(reach, span)

        @pl.when(above)
        def _():
            to_lower(step, 0).wait_recv()
            join_bottom(step).start()

        compute(step, 3 * reach, part, bottoms[step % 2][0])

        @pl.when(below)
        def _():
            to_upper(step, 0).wait_recv()
            join_top(step).start()

        compute(step, part, part, tops[step % 2][0])
        @pl.when(above)
        def _():
            join_bottom(step).wait()
            to_lower(step, 1).wait_recv()

        compute(step, 3 * reach + part, part, bottoms[step % 2][1])
        if last:
            to_near[1].start()

            @pl.when(side == 0)
            def _():
                to_over[1].start()
        else:

            @pl.when(above)
            def _():
                to_upper(step + 1, 0).start()

        @pl.when(below)
        def _():
            join_top(step).wait()
            to_upper(step, 1).wait_recv()

        compute(step, 0, part, tops[step % 2][1])
        if last:
            to_near[2].start()

            @pl.when(side == 1)
            def _():
                to_over[1].start()
        else:

            @pl.when(below)
            def _():
                to_lower(step + 1, 0).start()

        @pl.when(below)
        def _():
            to_lower(step, 1).wait_send()

        @pl.when(above)
        def _():
            to_upper(step, 1).wait_send()

    keep_own = pltpu.make_async_copy(block.at[panel], block_ref.at[panel], keep_sem.at[0])
    keep_own.start()
    add_own(3 * reach, reach)
    add_own(0, reach)
    to_near[0].wait()
    add_near(reach, span)
    to_near[1].wait()
    add_near(3 * reach, reach)
    to_near[2].wait()
    add_near(0, reach)
    keep_near = pltpu.make_async_copy(block.at[near], block_ref.at[near], keep_sem.at[1])
    keep_near.start()

    quarter = short // 2
    near_total[:short, :short] = near_acc[:short, :short]
    near_total[:short, short:] = near_acc[short:wide, short:]
    near_total[short : short + quarter, :short] = near_acc[short : short + quarter, :short]
    near_total[short : short + quarter, short:] = near_acc[short + quarter : wide, :short]
    near_total[short + quarter :, :] = near_acc[wide:, :]
    shape = (me, panel)
    near_sum = Reduction(near_stages, *shape, near_total, near_landing, full, 0, near_stage_sem, near_all_sem)
    cross_sum = Reduction(
        cross_stages, *shape, cross_total, cross_landing, full, near_total.shape[0], cross_stage_sem, cross_all_sem
    )
    stages = len(near_stages)
    ahead = min(stages, 3)
    near_sum.reduce_start(0)
    to_over[0].wait()
    passed[0].start()

    @pl.when(side == 0)
    def _():
        rest[0].start()

    add_across(0)
    for number in range(stages):
        near_sum.reduce_finish(number)
        near_sum.reduce_start(number + 1)
        if number == 0:
            passed[0].wait()
            add_beyond(0)
    near_sum.publish()
    near_sum.gather_start(0)
    to_over[1].wait()
    passed[1].start()
    add_across(1)
    passed[1].wait()
    add_beyond(1)
    swap = pltpu.make_async_remote_copy(
        src_ref=cross.at[1 - side], dst_ref=cross_in,
        send_sem=swap_sem.at[0], recv_sem=swap_sem.at[1], device_id={"vecs": over},
    )
    swap.start()
    near_sum.gather_finish(0)
    near_sum.gather_start(1)
    swap.wait()
    cross_total[...] = cross[side] + cross_in[...]
    cross_sum.reduce_start(0)
    for number in range(1, stages):
        near_sum.gather_finish(number)
        near_sum.gather_start(number + 1)
        if number == 1:
            cross_sum.reduce_finish(0)
            cross_sum.reduce_start(1)
    near_sum.settle()
    near_sum.close()

    @pl.when(side == 0)
    def _():
        rest[0].wait_send()
        rest[1].start()

    def gather_next(number):
        cross_sum.gather_finish(number)
        cross_sum.gather_start(number + 1)

    def reduced():
        cross_sum.reduce_finish(2)
        for number in range(3, stages):
            cross_sum.reduce_start(number)
            cross_sum.reduce_finish(number)
        cross_sum.publish()
        cross_sum.gather_start(0)

    def reduce_second():
        cross_sum.reduce_finish(1)
        cross_sum.reduce_start(2)

    def pass_rest():
        @pl.when(side == 1)
        def _():
            for copy, pass_on in zip(rest, onward):
                copy.wait_recv()
                pass_on.start()

    later = [functools.partial(gather_next, n) for n in range(1, len(cross_sum.gathers))]
    actions = [
        [reduce_second], [reduced], [functools.partial(gather_next, 0)], later[:1], later[1:], [],
        [pass_rest], [cross_sum.settle],
    ]
    lead_factor(full, work, lead, actions)
    lead_copy = pltpu.make_async_copy(lead, lead_ref, copy_sem.at[0])
    lead_copy.start()
    keep_own.wait()
    keep_near.wait()
    keep_over = pltpu.make_async_copy(block.at[over], block_ref.at[over], keep_sem.at[0])
    keep_beyond = pltpu.make_async_copy(block.at[beyond], block_ref.at[beyond], keep_sem.at[1])

    @pl.when(side == 0)
    def _():
        rest[1].wait_send()

    @pl.when(side == 1)
    def _():
        keep_over.start()

    cross_sum.close()
    low_sums = pltpu.make_async_copy(full.at[:2], sums_ref.at[:2], keep_sem.at[2])
    high_sums = pltpu.make_async_copy(full.at[2:], sums_ref.at[2:], keep_sem.at[3])
    low_sums.start()

    @pl.when(side == 1)
    def _():
        high_sums.start()
        onward[0].wait()
        onward[1].wait()
        keep_beyond.start()
        keep_over.wait()
        keep_beyond.wait()
        high_sums.wait()

    low_sums.wait()
    lead_copy.wait()


def filtered_sums(vectors, blocks, columns):
    rows, width = vectors.shape
    block_rows, nnz, size_b = blocks.shape[:3]
    panels, devices = lax.axis_size("vecs"), lax.axis_size("rows")
    reach = block_rows // 4
    part = reach // 2
    near_rows, cross_rows = width + width // 4, width
    near_stages, cross_stages = gram_stages(near_rows, devices), gram_stages(cross_rows, devices)
    steps = len(near_stages)
    row = lax.broadcasted_iota(jnp.int32, columns.shape, 0)
    shift = jnp.zeros_like(columns)
    for start, amount in (
        (0, reach), (part, part), (reach, 0), (3 * reach, -2 * reach), (3 * reach + part, -2 * reach - part),
    ):
        shift = jnp.where(row >= start, amount, shift)
    place = columns - lax.axis_index("rows") * block_rows + shift
    window = pltpu.VMEM((block_rows, size_b, width), jnp.bfloat16)
    side = pltpu.VMEM((2 * reach + part, size_b, width), jnp.bfloat16)
    state = pltpu.VMEM((block_rows, size_b, width), jnp.float32)
    anywhere = pl.BlockSpec(memory_space=pl.ANY)
    dma = pltpu.SemaphoreType.DMA

    def single(tall):
        return pltpu.VMEM((tall, width), jnp.float32)

    def kernel(*refs):
        inputs, wins, refs = refs[:6], refs[6:9], refs[9:]
        tops = ((refs[0], refs[1]), (refs[2], refs[3]))
        bottoms = ((refs[4], refs[5]), (refs[6], refs[7]))
        filter_kernel(near_stages, cross_stages, *inputs, *wins, tops, bottoms, *refs[8:])

    sums, block, lead = pl.pallas_call(
        kernel,
        out_shape=[
            jax.ShapeDtypeStruct((panels, near_rows + cross_rows, width), jnp.float32),
            jax.ShapeDtypeStruct((panels, block_rows, size_b, width), jnp.bfloat16),
            jax.ShapeDtypeStruct((2 * width, 2 * width), jnp.float32),
        ],
        in_specs=[pl.BlockSpec(memory_space=pltpu.SMEM), anywhere, anywhere],
        out_specs=[anywhere] * 3,
        scratch_shapes=[window] * 3 + [side] * 8 + [state] * 2 + [
            pltpu.VMEM(blocks.shape, jnp.bfloat16),
            pltpu.VMEM((panels, block_rows, size_b, width), jnp.bfloat16),
            pltpu.VMEM((2, width, width), jnp.float32),
            single(width + width // 2), single(near_rows), single(cross_rows),
            pltpu.VMEM((panels, near_rows + cross_rows, width), jnp.float32),
            single(2 * near_rows), single(2 * cross_rows), single(width),
            pltpu.VMEM((2 * width, 2 * width), jnp.float32),
            pltpu.VMEM((2 * width, 2 * width), jnp.float32),
            dma((6,)), dma((2, 2, 2)), dma((2, 2, 2)), dma((2,)), dma((4,)), dma((2,)),
            dma((2, 3)), dma((2, 2)), dma((2, 2)), dma((2, 2)), dma((2, 2)),
            dma((4, steps)), dma((2, 3, steps + 1)), dma((4, steps)), dma((2, 3, steps + 1)),
        ],
        compiler_params=pltpu.CompilerParams(
            vmem_limit_bytes=VMEM_LIMIT, collective_id=0, has_side_effects=True
        ),
    )(place, vectors.reshape(block_rows, size_b, width), blocks)
    return sums, block.reshape(panels, rows, width), lead


def scales(diagonal):
    wide = diagonal.shape[0]
    down = lax.broadcasted_iota(jnp.int32, (wide, wide), 0)
    across = lax.broadcasted_iota(jnp.int32, (wide, wide), 1)
    kept = jnp.where(down == across, diagonal, 0.0)
    sums = jnp.sum(kept, axis=0, keepdims=True)
    return lax.rsqrt(jnp.sum(kept, axis=1, keepdims=True)), lax.rsqrt(sums), sums


def fill_lower(full, first, work):
    wide = full.shape[2]
    short, quarter = wide // 2, wide // 4
    parts = []
    for n in range(2):
        ends = [scales(full[first + n, :short, m * short : (m + 1) * short]) for m in range(2)]
        parts.append([jnp.concatenate([end[axis] for end in ends], axis=min(axis, 1)) for axis in range(3)])
        start = n * wide
        for m in range(2):
            own = slice(start + m * short, start + (m + 1) * short)
            work[own, own] = full[first + n, :short, m * short : (m + 1) * short] * ends[m][0] * ends[m][1]
            rows = slice(start + short + m * quarter, start + short + (m + 1) * quarter)
            part = full[first + n, short : short + quarter, m * short : (m + 1) * short]
            down = ends[1][0][m * quarter : (m + 1) * quarter, :]
            work[rows, start : start + short] = part * down * ends[0][1]
    for n in range(2):
        rows = slice(n * short, (n + 1) * short)
        below = wide + n * short
        work[below : below + short, :wide] = (
            full[first + n, short + quarter : wide + quarter, :] * parts[1][0][rows, :] * parts[0][1]
        )
    return parts


def lead_factor(full, work, lead, actions):
    whole = work.shape[0]
    wide, size = whole // 2, whole // 4
    work[:wide, wide:] = jnp.zeros((wide, wide), jnp.float32)
    fill_lower(full, 0, work)

    @pl.loop(0, 4)
    def _(k):
        start = pl.multiple_of(k * size, size)
        at = pl.ds(start, size)

        def act(second):
            for n in range(4):

                @pl.when(k == n)
                def _():
                    for action in actions[2 * n + second]:
                        action()

        done = factor_block(work[at, at], functools.partial(act, 0))
        act(1)
        lower = halves(done)
        rows = lax.broadcasted_iota(jnp.int32, (whole, size), 0)
        cols = lax.broadcasted_iota(jnp.int32, (size, whole), 1)
        below = rows >= start + size
        own = work[:, at]
        column = jnp.where(below, triple(halves(own), lower, TURNED), 0.0)
        known = jnp.where(cols < start, work[at, :], 0.0)
        lead[at, :] = triple(lower, halves(known), PLAIN)
        lead[at, at] = done
        work[:, at] = jnp.where(below, 0.0, own)
        pieces = halves(column)
        work[...] -= triple(pieces, halves(lead[at, :]), PLAIN) + triple(pieces, pieces, TURNED)


def square_factor(work, inverse, size, actions=()):
    full = work.shape[0]
    count = full // size
    waiting = list(actions)

    def act():
        for action in waiting.pop(0) if waiting else []:
            action()

    def span(c):
        return slice(c * size, (c + 1) * size)

    done = factor_block(work[span(0), span(0)], act)
    act()
    for c in range(count):
        own = span(c)
        lower = halves(done)
        inverse[own, own] = done
        if c + 1 < count:
            inverse[own, (c + 1) * size :] = jnp.zeros((size, full - (c + 1) * size), jnp.float32)
            below = slice((c + 1) * size, full)
            column = triple(halves(work[below, own]), lower, TURNED)
            pieces = halves(column)
            top = (pieces[0][:size], pieces[1][:size])
            following = work[span(c + 1), span(c + 1)] - triple(top, top, TURNED)
        if c > 0:
            known = triple(lower, halves(work[own, : c * size]), PLAIN)
            inverse[own, : c * size] = known
        if c + 1 < count:
            done = factor_block(following, act)
            act()
            work[below, own] = -triple(pieces, lower, PLAIN)
            if c > 0:
                work[below, : c * size] -= triple(pieces, halves(known), PLAIN)
            for j in range(c + 1, count):
                first = max(j, c + 2)
                if first == count:
                    continue
                rows = slice((first - c - 1) * size, (count - c - 1) * size)
                cols = slice((j - c - 1) * size, (j - c) * size)
                work[first * size :, span(j)] -= triple(
                    (pieces[0][rows], pieces[1][rows]), (pieces[0][cols], pieces[1][cols]), TURNED
                )


def finish_kernel(
    size, total_rows, sums_ref, lead_ref, block_ref, out_ref,
    work, inverse, cross, mixed, factor, block, result, in_sem, out_sem,
):
    panels, _, wide = sums_ref.shape
    short = wide // 2
    mine = lax.axis_index("vecs")
    side = mine // 2

    def fetch(panel):
        return pltpu.make_async_copy(block_ref.at[panel], block.at[panel], in_sem.at[panel])

    for panel in range(panels):

        @pl.when(panel <= mine)
        def _():
            fetch(panel).start()

    def scaled(sums):
        return lax.rsqrt(sums * (1.0 / total_rows))

    parts = []
    for panel in range(2):
        for m in range(2):
            parts.append(scales(sums_ref[panel, :short, m * short : (m + 1) * short]))
    left_scale = jnp.concatenate([scaled(part[2]) for part in parts], axis=1)
    along = [jnp.concatenate([part[1] for part in parts[2 * n : 2 * n + 2]], axis=1) for n in range(2)]

    def keep(rows, first):
        high, low = halves(rows)
        factor[0, :, first : first + 2 * wide] = high
        factor[1, :, first : first + 2 * wide] = low

    @pl.when(side == 0)
    def _():
        keep(lead_ref[pl.ds(pl.multiple_of(mine * wide, wide), wide), :] * left_scale, 0)

    @pl.when(side == 1)
    def _():
        later = fill_lower(sums_ref, 2, work)
        for panel in range(panels):
            core, row = panel % 2, panel // 2
            cross[row * wide : (row + 1) * wide, core * wide : (core + 1) * wide] = (
                sums_ref[panel, wide + short // 2 :, :] * later[row][0] * along[core]
            )
        lead = halves(lead_ref[...])
        ratio = halves(triple(halves(cross[...]), lead, TURNED))
        upper = (ratio[0][:wide], ratio[1][:wide])
        lower = (ratio[0][wide:], ratio[1][wide:])
        work[:wide, :wide] -= triple(upper, upper, TURNED)
        work[wide:, :] -= triple(lower, ratio, TURNED)
        mixed[...] = triple(ratio, lead, PLAIN)
        square_factor(work, inverse, size)
        own = inverse[pl.ds(pl.multiple_of((mine - 2) * wide, wide), wide), :]
        keep(-triple(halves(own), halves(mixed[...]), PLAIN) * left_scale, 0)
        keep(own * jnp.concatenate([scaled(part[2]) for part in later], axis=1), 2 * wide)

    tiles = out_sem.shape[0]
    tile = block.shape[1] // tiles

    def store(index):
        rows = pl.ds(pl.multiple_of(index * tile, tile), tile)
        return pltpu.make_async_copy(result.at[rows], out_ref.at[rows], out_sem.at[index])

    for number in range(1, panels + 1):

        @pl.when(mine == number - 1)
        def _():
            for panel in range(number):
                fetch(panel).wait()
            deep = number * wide
            right = jnp.concatenate([factor[0, :, :deep], factor[1, :, :deep]], axis=1)

            @pl.loop(0, tiles)
            def _(index):
                rows = pl.ds(pl.multiple_of(index * tile, tile), tile)
                left = jnp.concatenate([block[panel, rows, :] for panel in range(number)] * 2, axis=1)
                result[rows, :] = lax.dot_general(
                    left, right, TURNED, preferred_element_type=jnp.float32
                )
                store(index).start()

    for index in range(tiles):
        store(index).wait()


def finish(sums, block, lead, total_rows):
    panels, rows, wide = block.shape
    size = 128
    tiles = 4
    anywhere = pl.BlockSpec(memory_space=pl.ANY)
    near = pl.BlockSpec(memory_space=pltpu.VMEM)
    square = pltpu.VMEM((2 * wide, 2 * wide), jnp.float32)
    return pl.pallas_call(
        functools.partial(finish_kernel, size, total_rows),
        out_shape=jax.ShapeDtypeStruct((rows, wide), jnp.float32),
        in_specs=[near, near, anywhere],
        out_specs=anywhere,
        scratch_shapes=[square] * 4 + [
            pltpu.VMEM((2, wide, panels * wide), jnp.bfloat16),
            pltpu.VMEM((panels, rows, wide), jnp.bfloat16),
            pltpu.VMEM((rows, wide), jnp.float32),
            pltpu.SemaphoreType.DMA((panels,)),
            pltpu.SemaphoreType.DMA((tiles,)),
        ],
        compiler_params=pltpu.CompilerParams(vmem_limit_bytes=VMEM_LIMIT),
    )(sums, lead, block)


def shards(vectors, blocks, columns):
    total_rows = vectors.shape[0] * lax.axis_size("rows")
    sums, block, lead = filtered_sums(vectors, blocks, columns)
    return finish(sums, block, lead, total_rows)


def solution(mesh):
    in_specs = (P("rows", "vecs"), P("rows", None, None, None), P("rows", None))
    out_specs = P("rows", "vecs")
    return jax.shard_map(shards, mesh=mesh, in_specs=in_specs, out_specs=out_specs, check_vma=False)
```

```python
import functools

import jax
import jax.numpy as jnp
from jax import lax
from jax.experimental import pallas as pl
from jax.experimental.pallas import tpu as pltpu
from jax.sharding import PartitionSpec as P

DEGREE = 4

filter_center = 0.25
filter_radius = 1.25

VMEM_LIMIT = 56 * 1024 * 1024


def factor_block(block, middle=None):
    size = block.shape[0]
    tiles = [block[8 * t : 8 * (t + 1), :] for t in range(size // 8)]
    lane = lax.broadcasted_iota(jnp.int32, (8, size), 1)
    sub = lax.broadcasted_iota(jnp.int32, (8, size), 0)

    def spread(array):
        return jnp.broadcast_to(array, (8, size))

    for first in range(size // 8):
        if middle and first == size // 16:
            middle()
        j = 8 * first
        each = range(8)
        at_any = jnp.logical_and(lane >= j, lane < j + 8)
        head = tiles[first]
        cols = [spread(head[:, j + a : j + a + 1]) for a in each]
        p = [[spread(cols[a][b : b + 1, :]) for a in range(b + 1)] for b in each]
        rows = [jnp.where(at_any, 0.0, spread(head[a : a + 1, :])) for a in each]
        rows = [jnp.where(lane == j + a, 1.0, rows[a]) for a in each]
        pairs, ready = [], []
        for a in range(0, 8, 2):
            b = a + 1
            det = p[a][a] * p[b][b] - p[b][a] * p[b][a]
            inv = 1.0 / det
            e_aa, e_ab, e_bb = p[b][b] * inv, p[b][a] * inv, p[a][a] * inv
            over = 1.0 / p[a][a]
            ready.append(rows[a] * lax.rsqrt(p[a][a]))
            ready.append((rows[b] - (p[b][a] * over) * rows[a]) * lax.rsqrt(det * over))
            mult = {}
            for c in range(b + 1, 8):
                mult[c, 0] = p[c][a] * e_aa - p[c][b] * e_ab
                mult[c, 1] = p[c][b] * e_bb - p[c][a] * e_ab
            for c in range(b + 1, 8):
                for d in range(b + 1, c + 1):
                    p[c][d] = p[c][d] - (mult[c, 0] * p[d][a] + mult[c, 1] * p[d][b])
            pairs.append((e_aa, e_ab, e_bb, mult, rows[a], rows[b]))
            for c in range(b + 1, 8):
                rows[c] = rows[c] - (mult[c, 0] * rows[a] + mult[c, 1] * rows[b])
        use = [None] * 8
        for number in reversed(range(4)):
            a, b = 2 * number, 2 * number + 1
            e_aa, e_ab, e_bb, mult, row_a, row_b = pairs[number]
            use[a] = e_aa * row_a - e_ab * row_b
            use[b] = e_bb * row_b - e_ab * row_a
            for c in range(b + 1, 8):
                use[a] = use[a] - mult[c, 0] * use[c]
                use[b] = use[b] - mult[c, 1] * use[c]
        for t in range(first + 1, size // 8):
            tile = tiles[t]
            cols = [spread(tile[:, j + a : j + a + 1]) for a in each]
            terms = [cols[a] * use[a] for a in each]
            while len(terms) > 1:
                terms = [x + y for x, y in zip(terms[::2], terms[1::2])]
            tiles[t] = jnp.where(at_any, 0.0, tile) - terms[0]
        top = ready[0]
        for a in range(1, 8):
            top = jnp.where(sub == a, ready[a], top)
        tiles[first] = top
    done = jnp.concatenate(tiles, axis=0)
    down = lax.broadcasted_iota(jnp.int32, (size, size), 0)
    across = lax.broadcasted_iota(jnp.int32, (size, size), 1)
    return jnp.where(across <= down, done, 0.0)


def halves(array):
    high = array.astype(jnp.bfloat16)
    return high, (array - high.astype(jnp.float32)).astype(jnp.bfloat16)


PLAIN = (((1,), (0,)), ((), ()))
TURNED = (((1,), (1,)), ((), ()))


def triple(left, right, dims):
    def one(a, b):
        return lax.dot_general(a, b, dims, preferred_element_type=jnp.float32)

    return one(left[0], right[0]) + (one(left[0], right[1]) + one(left[1], right[0]))


def gram_stages(rows, devices):
    stages, bit, held = [], 1, rows
    while bit < devices:
        halve = held % 16 == 0
        stages.append((bit, halve))
        held, bit = held // 2 if halve else held, bit * 2
    return stages


def flipped(index, bit):
    return index + bit - 2 * bit * lax.rem(index // bit, 2)


class Reduction:
    def __init__(self, stages, me, panel, total, landing, full, base, stage_sem, all_sem):
        self.me, self.panel, self.total, self.landing, self.full = me, panel, total, landing, full
        self.base, self.stage_sem, self.all_sem = base, stage_sem, all_sem
        self.near, self.over, self.side = flipped(panel, 1), flipped(panel, 2), panel // 2
        self.steps, self.shared = [], []
        start, held, taken = 0, total.shape[0], 0
        for bit, halve in stages:
            size = held // 2 if halve else held
            upper = lax.rem(me // bit, 2)
            keep = pl.multiple_of(start + upper * size, 8) if halve else start
            give = pl.multiple_of(start + (1 - upper) * size, 8) if halve else start
            self.steps.append((bit, size, keep, give, taken))
            start, held, taken = keep, size, taken + size
        self.start, self.held = start, held
        self.gathers = [n for n in reversed(range(len(stages))) if stages[n][1]]

    def reduce_copy(self, number):
        bit, size, _, give, taken = self.steps[number]
        return pltpu.make_async_remote_copy(
            src_ref=self.total.at[pl.ds(give, size)], dst_ref=self.landing.at[taken : taken + size],
            send_sem=self.stage_sem.at[0, number], recv_sem=self.stage_sem.at[1, number],
            device_id={"rows": flipped(self.me, bit)},
        )

    def reduce_start(self, number):
        if number < len(self.steps):
            self.reduce_copy(number).start()

    def reduce_finish(self, number):
        if number < len(self.steps):
            _, size, keep, _, taken = self.steps[number]
            self.reduce_copy(number).wait()
            self.total[pl.ds(keep, size), :] += self.landing[taken : taken + size, :]

    def piece(self, which, first, size):
        return self.full.at[which, pl.ds(pl.multiple_of(self.base + first, 8), size)]

    def hand(self, which, kind, number, first, size, peer):
        piece = self.piece(which, first, size)
        return pltpu.make_async_remote_copy(
            src_ref=piece, dst_ref=piece, send_sem=self.all_sem.at[0, kind, number],
            recv_sem=self.all_sem.at[1, kind, number], device_id={"vecs": peer},
        )

    def hands(self, number, kind):
        first, size = self.shared[number]
        which = self.over if kind == 2 else self.panel
        peer = self.near if kind else self.over
        return self.hand(which, kind, number, first, size, peer)

    def share(self, first, size):
        self.shared.append((first, size))
        number = len(self.shared) - 1

        @pl.when(self.side == 0)
        def _():
            self.hands(number, 0).start()

        self.hands(number, 1).start()

    def publish(self):
        rows = pl.ds(pl.multiple_of(self.base + self.start, 8), self.held)
        self.full[self.panel, rows, :] = self.total[pl.ds(self.start, self.held), :]
        self.share(self.start, self.held)

    def gather_copy(self, index):
        number = self.gathers[index]
        bit, size, keep, _, _ = self.steps[number]
        piece = self.piece(self.panel, keep, size)
        return pltpu.make_async_remote_copy(
            src_ref=piece, dst_ref=piece, send_sem=self.stage_sem.at[2, number],
            recv_sem=self.stage_sem.at[3, number], device_id={"rows": flipped(self.me, bit)},
        )

    def gather_start(self, index):
        if index < len(self.gathers):
            self.gather_copy(index).start()

    def gather_finish(self, index):
        if index < len(self.gathers):
            self.gather_copy(index).wait()
            _, size, _, give, _ = self.steps[self.gathers[index]]
            self.share(give, size)

    def settle(self):
        for number in range(len(self.shared)):

            @pl.when(self.side == 1)
            def _():
                self.hands(number, 0).wait_recv()
                self.hands(number, 2).start()

            @pl.when(self.side == 0)
            def _():
                self.hands(number, 0).wait_send()

            self.hands(number, 1).wait()

    def close(self):
        @pl.when(self.side == 1)
        def _():
            for number in range(len(self.shared)):
                self.hands(number, 2).wait()


def filter_kernel(
    near_stages, cross_stages, place_ref, vectors_ref, blocks_ref, sums_ref, block_ref, lead_ref,
    first_win, even_win, odd_win, tops, bottoms, even, odd, held,
    block, cross, near_acc, near_total, cross_total, full, near_landing, cross_landing, cross_in, work, lead,
    in_sem, send_sem, recv_sem, copy_sem, keep_sem, swap_sem, side_sem, x_sem, pass_sem, rest_sem, on_sem,
    near_stage_sem, near_all_sem, cross_stage_sem, cross_all_sem,
):
    me, count = lax.axis_index("rows"), lax.axis_size("rows")
    panel = lax.axis_index("vecs")
    core, side = lax.rem(panel, 2), panel // 2
    near, over = flipped(panel, 1), flipped(panel, 2)
    beyond = flipped(over, 1)
    block_rows, nnz = blocks_ref.shape[:2]
    wide = block.shape[3]
    short = wide // 2
    reach = block_rows // 4
    span, part = 2 * reach, reach // 2
    windows = [first_win, odd_win, even_win, odd_win]
    states = [None, even, odd, even]
    above, below = me < count - 1, me > 0

    peers = [{"vecs": near}, {"vecs": over}] + [{"rows": flipped(me, bit)} for bit, _ in near_stages]
    inside = jnp.logical_and(above, below)
    for peer in peers:
        pl.semaphore_signal(pltpu.get_barrier_semaphore(), 1, device_id=peer)

    @pl.when(inside)
    def _():
        other = me - 1 + 2 * lax.rem(me, 2)
        pl.semaphore_signal(pltpu.get_barrier_semaphore(), 1, device_id={"rows": other})

    pieces = [
        (vectors_ref, first_win),
        (vectors_ref.at[:span], tops[0][0].at[part:]),
        (vectors_ref.at[: reach + part], tops[0][1].at[reach:]),
        (vectors_ref.at[span:], bottoms[0][0].at[:span]),
        (vectors_ref.at[span + part :], bottoms[0][1].at[: reach + part]),
        (blocks_ref, held),
    ]
    fetches = [pltpu.make_async_copy(*pair, in_sem.at[n]) for n, pair in enumerate(pieces)]
    for fetch in fetches:
        fetch.start()

    @pl.when(inside)
    def _():
        pl.semaphore_wait(pltpu.get_barrier_semaphore(), len(peers) + 1)

    @pl.when(jnp.logical_not(inside))
    def _():
        pl.semaphore_wait(pltpu.get_barrier_semaphore(), len(peers))

    def to_lower(step, far):
        source = vectors_ref if step == 0 else windows[step]
        return pltpu.make_async_remote_copy(
            src_ref=source.at[far * part : (far + 1) * part],
            dst_ref=bottoms[step % 2][far].at[span:],
            send_sem=send_sem.at[0, far, step % 2], recv_sem=recv_sem.at[0, far, step % 2],
            device_id={"rows": me - 1},
        )

    def to_upper(step, far):
        source = vectors_ref if step == 0 else windows[step]
        first = block_rows - (far + 1) * part
        return pltpu.make_async_remote_copy(
            src_ref=source.at[first : first + part], dst_ref=tops[step % 2][far].at[:part],
            send_sem=send_sem.at[1, far, step % 2], recv_sem=recv_sem.at[1, far, step % 2],
            device_id={"rows": me + 1},
        )

    def join_bottom(step):
        close, far = bottoms[step % 2]
        return pltpu.make_async_copy(close.at[span:], far.at[reach + part : span], copy_sem.at[0])

    def join_top(step):
        close, far = tops[step % 2]
        return pltpu.make_async_copy(close.at[:part], far.at[part:reach], copy_sem.at[1])

    def compute(step, start, rows, window):
        slot = (step + 1) % 2
        for row in range(start, start + rows):
            left = jnp.concatenate([held[row, j] for j in range(nnz)], axis=1)
            right = jnp.concatenate([window[place_ref[row, j]] for j in range(nnz)], axis=0)
            acc = jnp.dot(left, right, preferred_element_type=jnp.float32)
            cur = first_win[row].astype(jnp.float32) if step == 0 else states[step][row]
            new = (acc - filter_center * cur) * (1.0 / filter_radius)
            if step == 1:
                new = 2.0 * new - first_win[row].astype(jnp.float32)
            elif step > 1:
                new = 2.0 * new - states[step - 1][row]
            rounded = new.astype(jnp.bfloat16)
            if step == DEGREE - 1:
                block[panel, row] = rounded
                continue
            windows[step + 1][row] = rounded
            states[step + 1][row] = new
            if row < span:
                tops[slot][0][row + part] = rounded
            if row < reach + part:
                tops[slot][1][row + reach] = rounded
            if row >= span:
                bottoms[slot][0][row - span] = rounded
            if row >= span + part:
                bottoms[slot][1][row - span - part] = rounded

    def send(which, start, size, sems, number, peer):
        piece = block.at[which, pl.ds(start, size)]
        return pltpu.make_async_remote_copy(
            src_ref=piece, dst_ref=piece, send_sem=sems.at[0, number],
            recv_sem=sems.at[1, number], device_id={"vecs": peer},
        )

    def part_start(half, number):
        return half * 3 * reach if number else reach + half * reach

    to_over = [send(panel, part_start(1 - side, n), reach, x_sem, n, over) for n in range(2)]
    passed = [send(over, part_start(side, n), reach, pass_sem, n, near) for n in range(2)]
    rest = [send(panel, part_start(0, n), reach, rest_sem, n, over) for n in range(2)]
    onward = [send(over, part_start(0, n), reach, on_sem, n, near) for n in range(2)]
    to_near = [
        send(panel, first, size, side_sem, n, near)
        for n, (first, size) in enumerate(((reach, span), (3 * reach, reach), (0, reach)))
    ]
    contract = (((0,), (0,)), ((), ()))

    def product(left, right):
        return lax.dot_general(left, right, contract, preferred_element_type=jnp.float32)

    def rows_of(which, start, size):
        return block[which, pl.ds(start, size)].reshape(size * block.shape[2], wide)

    def add_own(start, size):
        @pl.loop(0, size // part)
        def _(index):
            own = rows_of(panel, start + index * part, part)
            near_acc[:wide, :] += product(own, own)

    def add_near(start, size):
        @pl.loop(0, size // part)
        def _(index):
            own = rows_of(panel, start + index * part, part)
            beside = rows_of(near, start + index * part, part)

            @pl.when(core == 0)
            def _():
                near_acc[wide:, :] += product(beside[:, :short], own)

            @pl.when(core == 1)
            def _():
                near_acc[wide:, :] += product(own[:, short:], beside)

    def add_across(number):
        @pl.loop(0, 2)
        def _(index):
            start = part_start(side, number) + index * part
            own, there = rows_of(panel, start, part), rows_of(over, start, part)

            @pl.when(side == 0)
            def _():
                cross[core] += product(there, own)

            @pl.when(side == 1)
            def _():
                cross[core] += product(own, there)
                cross[1 - core] += product(rows_of(near, start, part), there)

    def add_beyond(number):
        @pl.when(side == 0)
        def _():
            @pl.loop(0, 2)
            def _(index):
                start = part_start(0, number) + index * part
                cross[1 - core] += product(rows_of(beyond, start, part), rows_of(panel, start, part))

    @pl.when(below)
    def _():
        to_lower(0, 0).start()

    @pl.when(above)
    def _():
        to_upper(0, 0).start()

    near_acc[...] = jnp.zeros_like(near_acc)
    cross[...] = jnp.zeros_like(cross)
    for fetch in fetches:
        fetch.wait()

    for step in range(DEGREE):
        last = step == DEGREE - 1
        compute(step, reach, reach, windows[step])
        compute(step, span, reach, windows[step])
        if last:
            to_over[0].start()
            to_near[0].start()

        @pl.when(below)
        def _():
            to_lower(step, 0).wait_send()
            to_lower(step, 1).start()

        @pl.when(above)
        def _():
            to_upper(step, 0).wait_send()
            to_upper(step, 1).start()

        if last:
            add_own(reach, span)

        @pl.when(above)
        def _():
            to_lower(step, 0).wait_recv()
            join_bottom(step).start()

        compute(step, 3 * reach, part, bottoms[step % 2][0])

        @pl.when(below)
        def _():
            to_upper(step, 0).wait_recv()
            join_top(step).start()

        compute(step, part, part, tops[step % 2][0])
        @pl.when(above)
        def _():
            join_bottom(step).wait()
            to_lower(step, 1).wait_recv()

        compute(step, 3 * reach + part, part, bottoms[step % 2][1])
        if last:
            to_near[1].start()

            @pl.when(side == 0)
            def _():
                to_over[1].start()
        else:

            @pl.when(above)
            def _():
                to_upper(step + 1, 0).start()

        @pl.when(below)
        def _():
            join_top(step).wait()
            to_upper(step, 1).wait_recv()

        compute(step, 0, part, tops[step % 2][1])
        if last:
            to_near[2].start()

            @pl.when(side == 1)
            def _():
                to_over[1].start()
        else:

            @pl.when(below)
            def _():
                to_lower(step + 1, 0).start()

        @pl.when(below)
        def _():
            to_lower(step, 1).wait_send()

        @pl.when(above)
        def _():
            to_upper(step, 1).wait_send()

    keep_own = pltpu.make_async_copy(block.at[panel], block_ref.at[panel], keep_sem.at[0])
    keep_own.start()
    add_own(3 * reach, reach)
    add_own(0, reach)
    to_near[0].wait()
    add_near(reach, span)
    to_near[1].wait()
    add_near(3 * reach, reach)
    to_near[2].wait()
    add_near(0, reach)
    keep_near = pltpu.make_async_copy(block.at[near], block_ref.at[near], keep_sem.at[1])
    keep_near.start()

    quarter = short // 2
    near_total[:short, :short] = near_acc[:short, :short]
    near_total[:short, short:] = near_acc[short:wide, short:]
    near_total[short : short + quarter, :short] = near_acc[short : short + quarter, :short]
    near_total[short : short + quarter, short:] = near_acc[short + quarter : wide, :short]
    near_total[short + quarter :, :] = near_acc[wide:, :]
    shape = (me, panel)
    near_sum = Reduction(near_stages, *shape, near_total, near_landing, full, 0, near_stage_sem, near_all_sem)
    cross_sum = Reduction(
        cross_stages, *shape, cross_total, cross_landing, full, near_total.shape[0], cross_stage_sem, cross_all_sem
    )
    stages = len(near_stages)
    ahead = min(stages, 3)
    near_sum.reduce_start(0)
    to_over[0].wait()
    passed[0].start()

    @pl.when(side == 0)
    def _():
        rest[0].start()

    add_across(0)
    for number in range(stages):
        near_sum.reduce_finish(number)
        near_sum.reduce_start(number + 1)
        if number == 0:
            passed[0].wait()
            add_beyond(0)
    near_sum.publish()
    near_sum.gather_start(0)
    to_over[1].wait()
    passed[1].start()
    add_across(1)
    passed[1].wait()
    add_beyond(1)
    swap = pltpu.make_async_remote_copy(
        src_ref=cross.at[1 - side], dst_ref=cross_in,
        send_sem=swap_sem.at[0], recv_sem=swap_sem.at[1], device_id={"vecs": over},
    )
    swap.start()
    near_sum.gather_finish(0)
    near_sum.gather_start(1)
    swap.wait()
    cross_total[...] = cross[side] + cross_in[...]
    cross_sum.reduce_start(0)
    for number in range(1, stages):
        near_sum.gather_finish(number)
        near_sum.gather_start(number + 1)
        if number == 1:
            cross_sum.reduce_finish(0)
            cross_sum.reduce_start(1)
    near_sum.settle()
    near_sum.close()

    @pl.when(side == 0)
    def _():
        rest[0].wait_send()
        rest[1].start()

    def gather_next(number):
        cross_sum.gather_finish(number)
        cross_sum.gather_start(number + 1)

    def reduced():
        cross_sum.reduce_finish(2)
        for number in range(3, stages):
            cross_sum.reduce_start(number)
            cross_sum.reduce_finish(number)
        cross_sum.publish()
        cross_sum.gather_start(0)

    def reduce_second():
        cross_sum.reduce_finish(1)
        cross_sum.reduce_start(2)

    def pass_rest():
        @pl.when(side == 1)
        def _():
            for copy, pass_on in zip(rest, onward):
                copy.wait_recv()
                pass_on.start()

    later = [functools.partial(gather_next, n) for n in range(1, len(cross_sum.gathers))]
    actions = [
        [reduce_second], [reduced], [functools.partial(gather_next, 0)], later[:1], later[1:], [],
        [pass_rest], [cross_sum.settle],
    ]
    lead_factor(full, work, lead, actions)
    lead_copy = pltpu.make_async_copy(lead, lead_ref, copy_sem.at[0])
    lead_copy.start()
    keep_own.wait()
    keep_near.wait()
    keep_over = pltpu.make_async_copy(block.at[over], block_ref.at[over], keep_sem.at[0])
    keep_beyond = pltpu.make_async_copy(block.at[beyond], block_ref.at[beyond], keep_sem.at[1])

    @pl.when(side == 0)
    def _():
        rest[1].wait_send()

    @pl.when(side == 1)
    def _():
        keep_over.start()

    cross_sum.close()
    low_sums = pltpu.make_async_copy(full.at[:2], sums_ref.at[:2], keep_sem.at[2])
    high_sums = pltpu.make_async_copy(full.at[2:], sums_ref.at[2:], keep_sem.at[3])
    low_sums.start()

    @pl.when(side == 1)
    def _():
        high_sums.start()
        onward[0].wait()
        onward[1].wait()
        keep_beyond.start()
        keep_over.wait()
        keep_beyond.wait()
        high_sums.wait()

    low_sums.wait()
    lead_copy.wait()


def filtered_sums(vectors, blocks, columns):
    rows, width = vectors.shape
    block_rows, nnz, size_b = blocks.shape[:3]
    panels, devices = lax.axis_size("vecs"), lax.axis_size("rows")
    reach = block_rows // 4
    part = reach // 2
    near_rows, cross_rows = width + width // 4, width
    near_stages, cross_stages = gram_stages(near_rows, devices), gram_stages(cross_rows, devices)
    steps = len(near_stages)
    row = lax.broadcasted_iota(jnp.int32, columns.shape, 0)
    shift = jnp.zeros_like(columns)
    for start, amount in (
        (0, reach), (part, part), (reach, 0), (3 * reach, -2 * reach), (3 * reach + part, -2 * reach - part),
    ):
        shift = jnp.where(row >= start, amount, shift)
    place = columns - lax.axis_index("rows") * block_rows + shift
    window = pltpu.VMEM((block_rows, size_b, width), jnp.bfloat16)
    side = pltpu.VMEM((2 * reach + part, size_b, width), jnp.bfloat16)
    state = pltpu.VMEM((block_rows, size_b, width), jnp.float32)
    anywhere = pl.BlockSpec(memory_space=pl.ANY)
    dma = pltpu.SemaphoreType.DMA

    def single(tall):
        return pltpu.VMEM((tall, width), jnp.float32)

    def kernel(*refs):
        inputs, wins, refs = refs[:6], refs[6:9], refs[9:]
        tops = ((refs[0], refs[1]), (refs[2], refs[3]))
        bottoms = ((refs[4], refs[5]), (refs[6], refs[7]))
        filter_kernel(near_stages, cross_stages, *inputs, *wins, tops, bottoms, *refs[8:])

    sums, block, lead = pl.pallas_call(
        kernel,
        out_shape=[
            jax.ShapeDtypeStruct((panels, near_rows + cross_rows, width), jnp.float32),
            jax.ShapeDtypeStruct((panels, block_rows, size_b, width), jnp.bfloat16),
            jax.ShapeDtypeStruct((2 * width, 2 * width), jnp.float32),
        ],
        in_specs=[pl.BlockSpec(memory_space=pltpu.SMEM), anywhere, anywhere],
        out_specs=[anywhere] * 3,
        scratch_shapes=[window] * 3 + [side] * 8 + [state] * 2 + [
            pltpu.VMEM(blocks.shape, jnp.bfloat16),
            pltpu.VMEM((panels, block_rows, size_b, width), jnp.bfloat16),
            pltpu.VMEM((2, width, width), jnp.float32),
            single(width + width // 2), single(near_rows), single(cross_rows),
            pltpu.VMEM((panels, near_rows + cross_rows, width), jnp.float32),
            single(2 * near_rows), single(2 * cross_rows), single(width),
            pltpu.VMEM((2 * width, 2 * width), jnp.float32),
            pltpu.VMEM((2 * width, 2 * width), jnp.float32),
            dma((6,)), dma((2, 2, 2)), dma((2, 2, 2)), dma((2,)), dma((4,)), dma((2,)),
            dma((2, 3)), dma((2, 2)), dma((2, 2)), dma((2, 2)), dma((2, 2)),
            dma((4, steps)), dma((2, 3, steps + 1)), dma((4, steps)), dma((2, 3, steps + 1)),
        ],
        compiler_params=pltpu.CompilerParams(
            vmem_limit_bytes=VMEM_LIMIT, collective_id=0, has_side_effects=True
        ),
    )(place, vectors.reshape(block_rows, size_b, width), blocks)
    return sums, block.reshape(panels, rows, width), lead


def scales(diagonal):
    wide = diagonal.shape[0]
    down = lax.broadcasted_iota(jnp.int32, (wide, wide), 0)
    across = lax.broadcasted_iota(jnp.int32, (wide, wide), 1)
    kept = jnp.where(down == across, diagonal, 0.0)
    sums = jnp.sum(kept, axis=0, keepdims=True)
    return lax.rsqrt(jnp.sum(kept, axis=1, keepdims=True)), lax.rsqrt(sums), sums


def fill_lower(full, first, work):
    wide = full.shape[2]
    short, quarter = wide // 2, wide // 4
    parts = []
    for n in range(2):
        ends = [scales(full[first + n, :short, m * short : (m + 1) * short]) for m in range(2)]
        parts.append([jnp.concatenate([end[axis] for end in ends], axis=min(axis, 1)) for axis in range(3)])
        start = n * wide
        for m in range(2):
            own = slice(start + m * short, start + (m + 1) * short)
            work[own, own] = full[first + n, :short, m * short : (m + 1) * short] * ends[m][0] * ends[m][1]
            rows = slice(start + short + m * quarter, start + short + (m + 1) * quarter)
            part = full[first + n, short : short + quarter, m * short : (m + 1) * short]
            down = ends[1][0][m * quarter : (m + 1) * quarter, :]
            work[rows, start : start + short] = part * down * ends[0][1]
    for n in range(2):
        rows = slice(n * short, (n + 1) * short)
        below = wide + n * short
        work[below : below + short, :wide] = (
            full[first + n, short + quarter : wide + quarter, :] * parts[1][0][rows, :] * parts[0][1]
        )
    return parts


def lead_factor(full, work, lead, actions):
    whole = work.shape[0]
    wide, size = whole // 2, whole // 4
    work[:wide, wide:] = jnp.zeros((wide, wide), jnp.float32)
    fill_lower(full, 0, work)

    @pl.loop(0, 4)
    def _(k):
        start = pl.multiple_of(k * size, size)
        at = pl.ds(start, size)

        def act(second):
            for n in range(4):

                @pl.when(k == n)
                def _():
                    for action in actions[2 * n + second]:
                        action()

        done = factor_block(work[at, at], functools.partial(act, 0))
        act(1)
        lower = halves(done)
        rows = lax.broadcasted_iota(jnp.int32, (whole, size), 0)
        cols = lax.broadcasted_iota(jnp.int32, (size, whole), 1)
        below = rows >= start + size
        own = work[:, at]
        column = jnp.where(below, triple(halves(own), lower, TURNED), 0.0)
        known = jnp.where(cols < start, work[at, :], 0.0)
        lead[at, :] = triple(lower, halves(known), PLAIN)
        lead[at, at] = done
        work[:, at] = jnp.where(below, 0.0, own)
        pieces = halves(column)
        work[...] -= triple(pieces, halves(lead[at, :]), PLAIN) + triple(pieces, pieces, TURNED)


def square_factor(work, inverse, size, actions=()):
    full = work.shape[0]
    count = full // size
    waiting = list(actions)

    def act():
        for action in waiting.pop(0) if waiting else []:
            action()

    def span(c):
        return slice(c * size, (c + 1) * size)

    done = factor_block(work[span(0), span(0)], act)
    act()
    for c in range(count):
        own = span(c)
        lower = halves(done)
        inverse[own, own] = done
        if c + 1 < count:
            inverse[own, (c + 1) * size :] = jnp.zeros((size, full - (c + 1) * size), jnp.float32)
            below = slice((c + 1) * size, full)
            column = triple(halves(work[below, own]), lower, TURNED)
            pieces = halves(column)
            top = (pieces[0][:size], pieces[1][:size])
            following = work[span(c + 1), span(c + 1)] - triple(top, top, TURNED)
        if c > 0:
            known = triple(lower, halves(work[own, : c * size]), PLAIN)
            inverse[own, : c * size] = known
        if c + 1 < count:
            done = factor_block(following, act)
            act()
            work[below, own] = -triple(pieces, lower, PLAIN)
            if c > 0:
                work[below, : c * size] -= triple(pieces, halves(known), PLAIN)
            for j in range(c + 1, count):
                first = max(j, c + 2)
                if first == count:
                    continue
                rows = slice((first - c - 1) * size, (count - c - 1) * size)
                cols = slice((j - c - 1) * size, (j - c) * size)
                work[first * size :, span(j)] -= triple(
                    (pieces[0][rows], pieces[1][rows]), (pieces[0][cols], pieces[1][cols]), TURNED
                )


def finish_kernel(
    size, total_rows, sums_ref, lead_ref, block_ref, out_ref,
    work, inverse, cross, mixed, factor, block, result, in_sem, out_sem,
):
    panels, _, wide = sums_ref.shape
    short = wide // 2
    mine = lax.axis_index("vecs")
    side = mine // 2

    def fetch(panel):
        return pltpu.make_async_copy(block_ref.at[panel], block.at[panel], in_sem.at[panel])

    for panel in range(panels):

        @pl.when(panel <= mine)
        def _():
            fetch(panel).start()

    def scaled(sums):
        return lax.rsqrt(sums * (1.0 / total_rows))

    parts = []
    for panel in range(2):
        for m in range(2):
            parts.append(scales(sums_ref[panel, :short, m * short : (m + 1) * short]))
    left_scale = jnp.concatenate([scaled(part[2]) for part in parts], axis=1)
    along = [jnp.concatenate([part[1] for part in parts[2 * n : 2 * n + 2]], axis=1) for n in range(2)]

    def keep(rows, first):
        high, low = halves(rows)
        factor[0, :, first : first + 2 * wide] = high
        factor[1, :, first : first + 2 * wide] = low

    @pl.when(side == 0)
    def _():
        keep(lead_ref[pl.ds(pl.multiple_of(mine * wide, wide), wide), :] * left_scale, 0)

    @pl.when(side == 1)
    def _():
        later = fill_lower(sums_ref, 2, work)
        for panel in range(panels):
            core, row = panel % 2, panel // 2
            cross[row * wide : (row + 1) * wide, core * wide : (core + 1) * wide] = (
                sums_ref[panel, wide + short // 2 :, :] * later[row][0] * along[core]
            )
        lead = halves(lead_ref[...])
        ratio = halves(triple(halves(cross[...]), lead, TURNED))
        upper = (ratio[0][:wide], ratio[1][:wide])
        lower = (ratio[0][wide:], ratio[1][wide:])
        work[:wide, :wide] -= triple(upper, upper, TURNED)
        work[wide:, :] -= triple(lower, ratio, TURNED)
        mixed[...] = triple(ratio, lead, PLAIN)
        square_factor(work, inverse, size)
        own = inverse[pl.ds(pl.multiple_of((mine - 2) * wide, wide), wide), :]
        keep(-triple(halves(own), halves(mixed[...]), PLAIN) * left_scale, 0)
        keep(own * jnp.concatenate([scaled(part[2]) for part in later], axis=1), 2 * wide)

    tiles = out_sem.shape[0]
    tile = block.shape[1] // tiles

    def store(index):
        rows = pl.ds(pl.multiple_of(index * tile, tile), tile)
        return pltpu.make_async_copy(result.at[rows], out_ref.at[rows], out_sem.at[index])

    for number in range(1, panels + 1):

        @pl.when(mine == number - 1)
        def _():
            for panel in range(number):
                fetch(panel).wait()
            deep = number * wide
            right = jnp.concatenate([factor[0, :, :deep], factor[1, :, :deep]], axis=1)

            @pl.loop(0, tiles)
            def _(index):
                rows = pl.ds(pl.multiple_of(index * tile, tile), tile)
                left = jnp.concatenate([block[panel, rows, :] for panel in range(number)] * 2, axis=1)
                result[rows, :] = lax.dot_general(
                    left, right, TURNED, preferred_element_type=jnp.float32
                )
                store(index).start()

    for index in range(tiles):
        store(index).wait()


def finish(sums, block, lead, total_rows):
    panels, rows, wide = block.shape
    size = 128
    tiles = 2
    anywhere = pl.BlockSpec(memory_space=pl.ANY)
    near = pl.BlockSpec(memory_space=pltpu.VMEM)
    square = pltpu.VMEM((2 * wide, 2 * wide), jnp.float32)
    return pl.pallas_call(
        functools.partial(finish_kernel, size, total_rows),
        out_shape=jax.ShapeDtypeStruct((rows, wide), jnp.float32),
        in_specs=[near, near, anywhere],
        out_specs=anywhere,
        scratch_shapes=[square] * 4 + [
            pltpu.VMEM((2, wide, panels * wide), jnp.bfloat16),
            pltpu.VMEM((panels, rows, wide), jnp.bfloat16),
            pltpu.VMEM((rows, wide), jnp.float32),
            pltpu.SemaphoreType.DMA((panels,)),
            pltpu.SemaphoreType.DMA((tiles,)),
        ],
        compiler_params=pltpu.CompilerParams(vmem_limit_bytes=VMEM_LIMIT),
    )(sums, lead, block)


def shards(vectors, blocks, columns):
    total_rows = vectors.shape[0] * lax.axis_size("rows")
    sums, block, lead = filtered_sums(vectors, blocks, columns)
    return finish(sums, block, lead, total_rows)


def solution(mesh):
    in_specs = (P("rows", "vecs"), P("rows", None, None, None), P("rows", None))
    out_specs = P("rows", "vecs")
    return jax.shard_map(shards, mesh=mesh, in_specs=in_specs, out_specs=out_specs, check_vma=False)
```
